32 devices in a mesh: dp: 8 (over z, x), tensor: 4 (over y, core).
Axes of the slice: x: 2, y: 2, z: 4, core: 2. Of those that a mesh axis runs over, the one named last changes fastest.
Arguments:
- tokens: bfloat16 [32768, 768], P(('dp', 'tensor')), may hold values from -6 to 6
- query_weight: bfloat16 [768, 768], P('dp', 'tensor'), may hold values from -0.21875 to 0.21875
- key_weight: bfloat16 [768, 768], P('dp', 'tensor'), may hold values from -0.21875 to 0.21875
- value_weight: bfloat16 [768, 768], P('dp', 'tensor'), may hold values from -0.21875 to 0.21875
- output_weight: bfloat16 [768, 768], P('tensor', 'dp'), may hold values from -3.5 to 3.5
- query_bias: bfloat16 [12, 64], P('tensor', 'dp'), may hold values from -3 to 3
- value_bias: bfloat16 [12, 64], P('tensor', 'dp'), may hold values from -0.109375 to 0.109375
- output_bias: float32 [768], P(('dp', 'tensor')), may hold values from -1.75 to 1.75
- first_gain: float32 [768], P(('dp', 'tensor')), may hold values from 0.5 to 1.5
- first_shift: float32 [768], P(('dp', 'tensor')), may hold values from -1.75 to 1.75
- up_weight: bfloat16 [768, 3072], P('dp', 'tensor'), may hold values from -0.21875 to 0.21875
- up_bias: bfloat16 [48, 64], P('tensor', 'dp'), may hold values from -3 to 3
- down_weight: bfloat16 [3072, 768], P('tensor', 'dp'), may hold values from -0.109375 to 0.109375
- down_bias: float32 [768], P(('dp', 'tensor')), may hold values from -1.75 to 1.75
- second_gain: float32 [768], P(('dp', 'tensor')), may hold values from 0.5 to 1.5
- second_shift: float32 [768], P(('dp', 'tensor')), may hold values from -1.75 to 1.75
- cotangent: bfloat16 [32768, 768], P(('dp', 'tensor')), may hold values from -6 to 6
Outputs:
- layer_output: bfloat16 [32768, 768], P(('dp', 'tensor'))
- grad_tokens: float32 [32768, 768], P(('dp', 'tensor'))
- grad_query_weight: float32 [768, 768], P('dp', 'tensor')
- grad_key_weight: float32 [768, 768], P('dp', 'tensor')
- grad_value_weight: float32 [768, 768], P('dp', 'tensor')
- grad_output_weight: float32 [768, 768], P('tensor', 'dp')
- grad_query_bias: float32 [12, 64], P('tensor', 'dp')
- grad_value_bias: float32 [12, 64], P('tensor', 'dp')
- grad_output_bias: float32 [768], P(('dp', 'tensor'))
- grad_first_gain: float32 [768], P(('dp', 'tensor'))
- grad_first_shift: float32 [768], P(('dp', 'tensor'))
- grad_up_weight: float32 [768, 3072], P('dp', 'tensor')
- grad_up_bias: float32 [48, 64], P('tensor', 'dp')
- grad_down_weight: float32 [3072, 768], P('tensor', 'dp')
- grad_down_bias: float32 [768], P(('dp', 'tensor'))
- grad_second_gain: float32 [768], P(('dp', 'tensor'))
- grad_second_shift: float32 [768], P(('dp', 'tensor'))
The draws below stay inside these ranges and needn't reach their ends.
All inputs are finite; a program needn't handle non-finite values.
Results may differ from the reference program's by a relative error of at most 0.014.
Values may be sent and summed in bfloat16 or wider, within the bound.
No kernel may reach another device: no remote copies, remote signals or barrier semaphores. Data moves between devices by JAX's collectives and lax.ppermute only.
A program may use at most 192 MiB of HBM per device.

```python
import jax
import jax.numpy as jnp
from jax import lax

D = 768
HEADS = 12
HD = 64
FF = 3072
L = 1024
SEQS = 4
FF_ROWS = 48
TOKENS = 32768


def strengthened(array, own_key, source, target, shards_of, factor):
    def block_of(position):
        return (jnp.arange(array.shape[position]) // (array.shape[position] // shards_of)).reshape((-1,) + (1,) * (array.ndim - 1 - position))

    one_side = jax.random.permutation(own_key, shards_of)[block_of(target)]
    second = (block_of(target) + shards_of // 2) % shards_of
    return jnp.where((block_of(source) == one_side) | (block_of(source) == second), factor * array, array)


def levels(own_key, dims, cuts, low, largest):
    loudness, own = 1.0, jax.random.fold_in(own_key, 6)
    for axis_at, parts in cuts:
        steps = jnp.exp(jax.random.uniform(jax.random.fold_in(own, axis_at), (parts,), jnp.float32, low / len(cuts), largest / len(cuts)))
        loudness = loudness * jnp.repeat(steps, dims[axis_at] // parts).reshape([-1 if axis == axis_at else 1 for axis in range(len(dims))])
    return loudness


def noise(own_key, extent, spread, reach, shards=(), dtype=jnp.bfloat16):
    gain = levels(own_key, extent, shards, -0.22, 0.18) if shards else 1.0
    entries = jax.random.normal(own_key, extent, jnp.float32) * spread * gain
    return jnp.minimum(jnp.maximum(entries, -reach), reach).astype(dtype)


def gaussian_with(own_key, shape, deviation, reach, pieces, heavy, held_as=jnp.bfloat16):
    entries = deviation * jax.random.normal(own_key, shape, jnp.float32)
    if pieces:
        entries = entries * levels(own_key, shape, pieces, -0.22, 0.18)
    return jnp.clip(strengthened(entries, jax.random.fold_in(own_key, 3), *heavy), -reach, reach).astype(held_as)


def setup_inputs(seed: int = 0) -> dict:
    keys = jax.random.split(jax.random.key(seed), 18)
    return {
        "tokens": noise(keys[0], (TOKENS, D), 1.0, 6.0, ((0, 32),)),
        "query_weight": noise(keys[1], (D, D), D ** -0.5, 0.21875, ((0, 8), (1, 4))),
        "key_weight": noise(keys[2], (D, D), D ** -0.5, 0.21875, ((0, 8), (1, 4))),
        "value_weight": noise(keys[3], (D, D), D ** -0.5, 0.21875, ((0, 8), (1, 4))),
        "output_weight": noise(keys[4], (D, D), (max(1, 4 * D // L)) ** -0.5, 3.5, ((0, 4), (1, 8))),
        "query_bias": noise(keys[5], (HEADS, HD), 0.5, 3.0, ((0, 4), (1, 8))),
        "value_bias": noise(keys[6], (HEADS, HD), (0.6 / L ** 0.5), 0.109375, ((0, 4), (1, 8))),
        "output_bias": noise(keys[7], (D,), 0.3, 1.75, ((0, 32),), jnp.float32),
        "first_gain": jnp.clip(1.0 + 0.1 * jax.random.normal(keys[8], (D,), jnp.float32), 0.5, 1.5),
        "first_shift": noise(keys[9], (D,), 0.3, 1.75, ((0, 32),), jnp.float32),
        "up_weight": noise(keys[10], (D, FF), D ** -0.5, 0.21875, ((0, 8), (1, 4))),
        "up_bias": noise(keys[11], (FF_ROWS, HD), 0.5, 3.0, ((0, 4), (1, 8))),
        "down_weight": noise(keys[12], (FF, D), FF ** -0.5, 0.109375, ((0, 4), (1, 8))),
        "down_bias": noise(keys[13], (D,), 0.3, 1.75, ((0, 32),), jnp.float32),
        "second_gain": jnp.clip(1.0 + 0.1 * jax.random.normal(keys[14], (D,), jnp.float32), 0.5, 1.5),
        "second_shift": noise(keys[15], (D,), 0.3, 1.75, ((0, 32),), jnp.float32),
        "cotangent": gaussian_with(keys[16], (TOKENS, D), 1.0, 6.0, ((0, 32),), (0, 1, 32, 2.75)),
    }


EPSILON = 1e-12

@jax.custom_vjp
def low(v):
    return lax.optimization_barrier(v.astype(jnp.bfloat16)).astype(jnp.float32)

@jax.custom_vjp
def low_back(v):
    return v

def low_keep(v):
    return (low(v), None)

def low_pass(kept, grad):
    return (grad,)

def back_keep(v):
    return (v, None)

def back_low(kept, grad):
    return (low(grad),)
low.defvjp(low_keep, low_pass)
low_back.defvjp(back_keep, back_low)

def matmul(left, right):
    return jnp.dot(left, right, precision=lax.Precision.HIGHEST)

def layer_norm(residual, norm_gain, norm_shift):
    average = lax.optimization_barrier(jnp.mean(residual, axis=-1, keepdims=True))
    centered = residual - average
    variance = lax.optimization_barrier(jnp.mean(centered * centered, axis=-1, keepdims=True))
    return centered * lax.rsqrt(variance + EPSILON) * norm_gain + norm_shift

def attend_packed(packed):
    query_seq, key_seq, value_seq = packed
    scores = jnp.einsum('qhd,khd->hqk', query_seq, key_seq, precision=lax.Precision.HIGHEST) * (1.0 / HD ** 0.5)
    softmax_in = low_back(scores)
    weights_low = low(jax.nn.softmax(softmax_in, axis=-1))
    return jnp.einsum('hqk,khd->qhd', weights_low, value_seq, precision=lax.Precision.HIGHEST)

def by_heads(matrix):
    return matrix.reshape(-1, L, HEADS, HD)

def group_forward(tokens_in, params):
    query_weight, key_weight, value_weight, output_weight, query_bias, value_bias, output_bias, first_gain, first_shift, up_weight, up_bias, down_weight, down_bias, second_gain, second_shift = params
    inputs_low = low(tokens_in)
    queries = low(low_back(matmul(inputs_low, query_weight)) + query_bias)
    keys_low = low(low_back(matmul(inputs_low, key_weight)))
    values_low = low(low_back(matmul(inputs_low, value_weight)) + value_bias)
    context = lax.map(jax.checkpoint(attend_packed), (by_heads(queries), by_heads(keys_low), by_heads(values_low)))
    context = low(low_back(context.reshape(-1, D)))
    attended = low_back(matmul(context, output_weight)) + output_bias
    first_out = layer_norm(tokens_in + attended, first_gain, first_shift)
    hidden = low(first_out)
    pre_activation = low_back(matmul(hidden, up_weight)) + up_bias
    activated = low(jax.nn.gelu(pre_activation, approximate=False))
    branch = low_back(matmul(activated, down_weight)) + down_bias
    return layer_norm(first_out + branch, second_gain, second_shift)

def reference(tokens, query_weight, key_weight, value_weight, output_weight, query_bias, value_bias, output_bias, first_gain, first_shift, up_weight, up_bias, down_weight, down_bias, second_gain, second_shift, cotangent):
    params = (query_weight.astype(jnp.float32), key_weight.astype(jnp.float32), value_weight.astype(jnp.float32), output_weight.astype(jnp.float32), query_bias.astype(jnp.float32).reshape(D), value_bias.astype(jnp.float32).reshape(D), output_bias.astype(jnp.float32), first_gain.astype(jnp.float32), first_shift.astype(jnp.float32), up_weight.astype(jnp.float32), up_bias.astype(jnp.float32).reshape(FF), down_weight.astype(jnp.float32), down_bias.astype(jnp.float32), second_gain.astype(jnp.float32), second_shift.astype(jnp.float32))
    group_tokens = tokens.astype(jnp.float32).reshape(-1, SEQS * L, D)
    group_cot = cotangent.astype(jnp.float32).reshape(-1, SEQS * L, D)
    zeros_init = jax.tree.map(jnp.zeros_like, params)

    def group_step(totals, pair_in):
        group_in, group_ct = pair_in
        result, pullback = jax.vjp(group_forward, group_in, params)
        grad_in, grad_params = pullback(group_ct)
        totals = jax.tree.map(jnp.add, totals, grad_params)
        return (totals, (result.astype(jnp.bfloat16), grad_in))
    totals, (outputs, grad_tokens) = lax.scan(group_step, zeros_init, (group_tokens, group_cot))
    g_query, g_key, g_value, g_output, g_qbias, g_vbias, g_obias, g_fgain, g_fshift, g_up, g_upbias, g_down, g_dbias, g_sgain, g_sshift = totals
    return (outputs.reshape(-1, D), grad_tokens.reshape(-1, D), g_query, g_key, g_value, g_output, g_qbias.reshape(HEADS, HD), g_vbias.reshape(HEADS, HD), g_obias, g_fgain, g_fshift, g_up, g_upbias.reshape(FF_ROWS, HD), g_down, g_dbias, g_sgain, g_sshift)
```

```python
import math

import jax
import jax.numpy as jnp
from jax import lax
from jax.sharding import PartitionSpec as P

HD = 64
L = 1024
EPSILON = 1e-12
AXES = ("dp", "tensor")
EXTRA = 16
BF = jnp.bfloat16
F32 = jnp.float32


def partner(device, stage, bits):
    if stage == "core":
        return device ^ 1
    if stage == "a":
        return device ^ (2 if device & 1 else 4)
    if stage == "b":
        return device ^ (4 if device & 1 else 2)
    return device ^ (1 << stage)


def exchange(array, stage, count):
    bits = count.bit_length() - 1
    return lax.ppermute(array, AXES, [(d, partner(d, stage, bits)) for d in range(count)])


def stages_of(count):
    bits = count.bit_length() - 1
    return [*range(bits - 1, 2, -1), "a", "b", "core"]


def gather_blocks(block, count):
    held = block[None]
    for stage in stages_of(count):
        held = jnp.concatenate([held, exchange(held, stage, count)], axis=0)
    return held


def scatter_blocks(blocks, count):
    for stage in reversed(stages_of(count)):
        half = blocks.shape[0] // 2
        arrived = exchange(blocks[half:], stage, count)
        total = blocks[:half].astype(F32) + arrived.astype(F32)
        blocks = total if half == 1 else total.astype(BF)
    return blocks[0]


def position_table(me, count):
    bits = count.bit_length() - 1
    device = jnp.arange(count, dtype=jnp.int32)
    differs = device ^ me
    one, two = (differs >> 1) & 1, (differs >> 2) & 1
    odd = (device & 1) == 1
    place = ((differs & 1) << (bits - 1)) | (jnp.where(odd, two, one) << (bits - 2))
    place = place | (jnp.where(odd, one, two) << (bits - 3))
    for k in range(3, bits):
        place = place | (((differs >> k) & 1) << (bits - 1 - k))
    return place


def three_parts(vector):
    high = lax.reduce_precision(vector, 8, 7)
    middle = lax.reduce_precision(vector - high, 8, 7)
    lowest = lax.reduce_precision(vector - high - middle, 8, 7)
    return jnp.stack([high, middle, lowest]).astype(BF)


def matmul(left, right):
    return jnp.dot(left, right, preferred_element_type=F32)


def contract_rows(left, right):
    return lax.dot_general(left, right, (((0,), (0,)), ((), ())), preferred_element_type=F32)


def contract_cols(left, right):
    return lax.dot_general(left, right, (((1,), (1,)), ((), ())), preferred_element_type=F32)


def layer_norm(residual, gain, shift):
    average = jnp.mean(residual, axis=-1, keepdims=True)
    centered = residual - average
    variance = jnp.mean(centered * centered, axis=-1, keepdims=True)
    inverse = lax.rsqrt(variance + EPSILON)
    normed = centered * inverse
    return normed * gain + shift, normed, inverse


def norm_backward(upstream, gain, normed, inverse):
    scaled = upstream * gain
    first_mean = jnp.mean(scaled, axis=-1, keepdims=True)
    second_mean = jnp.mean(scaled * normed, axis=-1, keepdims=True)
    return inverse * (scaled - first_mean - normed * second_mean)


def local(
    tokens, query_weight, key_weight, value_weight, output_weight, query_bias, value_bias,
    output_bias, first_gain, first_shift, up_weight, up_bias, down_weight, down_bias,
    second_gain, second_shift, cotangent,
):
    dp, tensor = lax.axis_size("dp"), lax.axis_size("tensor")
    count = dp * tensor
    rows = query_weight.shape[0]
    width = rows * dp
    groups = query_weight.shape[1] // HD
    heads = groups * tensor
    hidden_block = up_weight.shape[1]
    slot = output_bias.shape[0]
    place = position_table(lax.axis_index(AXES), count)
    vectors = jnp.stack([output_bias, first_gain, first_shift, down_bias, second_gain, second_shift])
    small = jnp.concatenate([
        three_parts(vectors).reshape(-1), query_bias.reshape(-1), value_bias.reshape(-1), up_bias.reshape(-1),
    ])
    extra = jnp.pad(small, (0, EXTRA * 4 * HD - small.shape[0])).reshape(EXTRA, 4 * HD)
    output_turned = output_weight.T
    by_group = [
        jnp.concatenate([w[:, c * HD : (c + 1) * HD] for w in (query_weight, key_weight, value_weight, output_turned)], axis=1)
        for c in range(groups)
    ]
    first_set = gather_blocks(jnp.concatenate([by_group[0], extra], axis=0), count)
    second_set = gather_blocks(jnp.concatenate(by_group[1:], axis=1), count)
    up_set = gather_blocks(up_weight, count)
    down_set = gather_blocks(down_weight.T, count)

    def whole(blocks):
        ordered = jnp.take(blocks, place, axis=0)
        return ordered.reshape(dp, tensor, rows, -1).transpose(1, 0, 2, 3).reshape(tensor, width, -1)

    packs = [whole(first_set[:, :rows])]
    rest = whole(second_set)
    packs += [rest[:, :, 4 * HD * c : 4 * HD * (c + 1)] for c in range(groups - 1)]
    up_all = whole(up_set)
    down_all = whole(down_set)
    small_all = jnp.take(first_set[:, rows:].reshape(count, -1), place, axis=0).astype(F32)
    triples = small_all[:, : 18 * slot].reshape(count, 3, 6, slot)
    vectors_all = (triples[:, 0] + triples[:, 1] + triples[:, 2]).transpose(1, 0, 2).reshape(6, width)
    bias_output, gain_first, shift_first, bias_down, gain_second, shift_second = vectors_all

    def biases(start, size):
        block = small_all[:, start : start + size].reshape(dp, tensor, -1, HD // dp)
        return block.transpose(1, 2, 0, 3).reshape(-1, HD)

    at = 18 * slot
    query_bias_all = biases(at, query_bias.size)
    value_bias_all = biases(at + query_bias.size, value_bias.size)
    up_bias_all = biases(at + 2 * query_bias.size, up_bias.size).reshape(tensor, hidden_block)

    sequences = tokens.shape[0] // L
    scale = 1.0 / math.sqrt(HD)
    pre = jnp.concatenate([matmul(tokens, packs[c][t][:, : 3 * HD])[None] for t in range(tensor) for c in range(groups)])
    pre = pre.reshape(heads, sequences, L, 3 * HD)
    queries = (pre[..., :HD] + query_bias_all[:, None, None]).astype(BF)
    keys = pre[..., HD : 2 * HD].astype(BF)
    values = (pre[..., 2 * HD :] + value_bias_all[:, None, None]).astype(BF)
    scores = jnp.einsum("hsqd,hskd->hsqk", queries, keys, preferred_element_type=F32) * scale
    probs = jax.nn.softmax(scores, axis=-1).astype(BF)
    context = jnp.einsum("hsqk,hskd->hsqd", probs, values, preferred_element_type=F32).astype(BF)
    context_flat = context.transpose(1, 2, 0, 3).reshape(-1, width)
    output_all = jnp.concatenate([packs[c][t][:, 3 * HD :] for t in range(tensor) for c in range(groups)], axis=1)
    attended = contract_cols(context_flat, output_all)
    first_out, normed_first, inverse_first = layer_norm(tokens.astype(F32) + (attended + bias_output), gain_first, shift_first)
    hidden = first_out.astype(BF)
    pre_act = jnp.stack([matmul(hidden, up_all[t]) + up_bias_all[t] for t in range(tensor)])
    act = jax.nn.gelu(pre_act, approximate=False).astype(BF)
    branch = sum(contract_cols(act[t], down_all[t]) for t in range(tensor))
    layer_out, normed_second, inverse_second = layer_norm(first_out + (branch + bias_down), gain_second, shift_second)

    upstream = cotangent.astype(F32)
    grad_second_gain = jnp.sum(upstream * normed_second, axis=0)
    grad_second_shift = jnp.sum(upstream, axis=0)
    err_two = norm_backward(upstream, gain_second, normed_second, inverse_second)
    grad_down_bias = jnp.sum(err_two, axis=0)
    err_two_low = err_two.astype(BF)

    def blocks_of(parts):
        stacked = jnp.stack(parts).reshape(tensor, dp, rows, -1).transpose(1, 0, 2, 3).reshape(count, rows, -1)
        return jnp.zeros_like(stacked).at[place].set(stacked)

    grad_down = scatter_blocks(blocks_of([contract_rows(err_two_low, act[t]).astype(BF) for t in range(tensor)]), count)
    grad_act = jnp.stack([matmul(err_two_low, down_all[t]) for t in range(tensor)])
    grad_pre = jax.vjp(lambda v: jax.nn.gelu(v, approximate=False), pre_act)[1](grad_act)[0]
    grad_up_bias = jnp.sum(grad_pre, axis=1)
    grad_pre_low = grad_pre.astype(BF)
    grad_up = scatter_blocks(blocks_of([contract_rows(hidden, grad_pre_low[t]).astype(BF) for t in range(tensor)]), count)
    err_in = err_two + sum(contract_cols(grad_pre_low[t], up_all[t]) for t in range(tensor))
    grad_first_gain = jnp.sum(err_in * normed_first, axis=0)
    grad_first_shift = jnp.sum(err_in, axis=0)
    err_one = norm_backward(err_in, gain_first, normed_first, inverse_first)
    grad_output_bias = jnp.sum(err_one, axis=0)
    err_one_low = err_one.astype(BF)
    context_grad = matmul(err_one_low, output_all).astype(BF).reshape(sequences, L, heads, HD).transpose(2, 0, 1, 3)
    grad_values = jnp.einsum("hsqk,hsqd->hskd", probs, context_grad, preferred_element_type=F32)
    dprobs = jnp.einsum("hsqd,hskd->hsqk", context_grad, values, preferred_element_type=F32)
    row_terms = jnp.sum(context_grad.astype(F32) * context.astype(F32), axis=-1, keepdims=True)
    dscores = (probs.astype(F32) * (dprobs - row_terms)).astype(BF)
    grad_queries = jnp.einsum("hsqk,hskd->hsqd", dscores, keys, preferred_element_type=F32) * scale
    grad_keys = jnp.einsum("hsqk,hsqd->hskd", dscores, queries, preferred_element_type=F32) * scale
    grad_query_bias = jnp.sum(grad_queries, axis=(1, 2))
    grad_value_bias = jnp.sum(grad_values, axis=(1, 2))
    triple = jnp.concatenate([grad_queries, grad_keys, grad_values], axis=-1).astype(BF).reshape(heads, -1, 3 * HD)
    context_rows = context.reshape(heads, -1, HD)

    def head_grad(h):
        return jnp.concatenate([contract_rows(tokens, triple[h]), contract_rows(err_one_low, context_rows[h])], axis=1).astype(BF)

    second_grad = scatter_blocks(blocks_of([
        jnp.concatenate([head_grad(t * groups + c) for c in range(1, groups)], axis=1) for t in range(tensor)
    ]), count)
    grad_tokens = err_one + sum(
        contract_cols(triple[t * groups + c], packs[c][t][:, : 3 * HD]) for t in range(tensor) for c in range(groups)
    )
    vector_grads = jnp.stack([
        grad_output_bias, grad_first_gain, grad_first_shift, grad_down_bias, grad_second_gain, grad_second_shift,
    ]).reshape(6, count, slot).transpose(1, 0, 2).reshape(count, -1)

    def bias_blocks(bias):
        return bias.reshape(tensor, -1, dp, HD // dp).transpose(2, 0, 1, 3).reshape(count, -1)

    small_grads = jnp.concatenate([
        vector_grads, bias_blocks(grad_query_bias), bias_blocks(grad_value_bias), bias_blocks(grad_up_bias.reshape(-1, HD)),
    ], axis=1)
    high = lax.reduce_precision(small_grads, 8, 7)
    small_grads = high
    small_grads = jnp.pad(small_grads, ((0, 0), (0, EXTRA * 4 * HD - small_grads.shape[1]))).astype(BF)
    small_grads = jnp.zeros_like(small_grads).at[place].set(small_grads).reshape(count, EXTRA, 4 * HD)
    first_grad = scatter_blocks(
        jnp.concatenate([blocks_of([head_grad(t * groups) for t in range(tensor)]), small_grads], axis=1), count
    )
    packed = jnp.concatenate([first_grad[:rows], second_grad], axis=1).reshape(rows, groups, 4, HD)
    out_query, out_key, out_value, out_output = (packed[:, :, i].reshape(rows, groups * HD) for i in range(4))
    tail = first_grad[rows:].reshape(-1)
    vecs = tail[: 6 * slot].reshape(6, slot)
    bias_at = 6 * slot
    return (
        layer_out.astype(BF),
        grad_tokens,
        out_query,
        out_key,
        out_value,
        out_output.T,
        tail[bias_at : bias_at + slot].reshape(query_bias.shape),
        tail[bias_at + slot : bias_at + 2 * slot].reshape(value_bias.shape),
        vecs[0],
        vecs[1],
        vecs[2],
        grad_up,
        tail[bias_at + 2 * slot : bias_at + 2 * slot + up_bias.size].reshape(up_bias.shape),
        grad_down.T,
        vecs[3],
        vecs[4],
        vecs[5],
    )


def solution(mesh):
    both, cross, turned, vector = P(AXES, None), P("dp", "tensor"), P("tensor", "dp"), P(AXES)
    return jax.shard_map(
        local,
        mesh=mesh,
        in_specs=(
            both, cross, cross, cross, turned, turned, turned, vector, vector, vector,
            cross, turned, turned, vector, vector, vector, both,
        ),
        out_specs=(
            both, both, cross, cross, cross, turned, turned, turned, vector, vector, vector,
            cross, turned, turned, vector, vector, vector,
        ),
        check_vma=False,
    )
```

```python
import functools
import math

import jax
import jax.numpy as jnp
import numpy as np
from jax import lax
from jax.experimental import pallas as pl
from jax.experimental.pallas import tpu as pltpu
from jax.sharding import PartitionSpec as P

HD = 64
L = 1024
PACK = 4 * HD
EPSILON = 1e-12
AXES = ("dp", "tensor")
EXTRA = 16
LANES = 128
BF = jnp.bfloat16
F32 = jnp.float32
SDS = jax.ShapeDtypeStruct
ANY = pl.BlockSpec(memory_space=pl.ANY)


def nn(a, b):
    return lax.dot_general(a, b, (((1,), (0,)), ((), ())), preferred_element_type=F32)


def nt(a, b):
    return lax.dot_general(a, b, (((1,), (1,)), ((), ())), preferred_element_type=F32)


def full(shape):
    return pl.BlockSpec(shape, lambda *_: (0,) * len(shape))


def call(body, grid, tables, ins, outs, scratch, cost, name):
    flops, moved = cost
    return pl.pallas_call(
        body,
        grid_spec=pltpu.PrefetchScalarGridSpec(
            num_scalar_prefetch=len(tables),
            grid=grid,
            in_specs=[s for _, s in ins],
            out_specs=[s for _, _, s in outs],
            scratch_shapes=scratch,
        ),
        out_shape=[SDS(s, d) for s, d, _ in outs],
        compiler_params=pltpu.CompilerParams(
            dimension_semantics=("arbitrary",) * len(grid), vmem_limit_bytes=56 * 2**20
        ),
        cost_estimate=pl.CostEstimate(flops=int(flops), bytes_accessed=int(moved), transcendentals=0),
        name=name,
    )(*tables, *[a for a, _ in ins])


def partner(device, stage):
    if stage == "core":
        return device ^ 1
    if stage == "a":
        return device ^ (2 if device & 1 else 4)
    if stage == "b":
        return device ^ (4 if device & 1 else 2)
    return device ^ (1 << stage)


def exchange(array, stage, count):
    return lax.ppermute(array, AXES, [(d, partner(d, stage)) for d in range(count)])


def stages_of(count):
    bits = count.bit_length() - 1
    return [*range(bits - 1, 2, -1), "a", "b", "core"]


def gather_blocks(block, count):
    held = block[None]
    for stage in stages_of(count)[:-2]:
        held = jnp.concatenate([held, exchange(held, stage, count)], axis=0)
    pieces = [held, exchange(held, "b", count)]
    return pieces + [exchange(piece, "core", count) for piece in pieces]


def scatter_blocks(keep, send, count):
    terms = [keep]
    for stage in reversed(stages_of(count)):
        terms.append(exchange(send, stage, count))
        half = terms[-1].shape[0] // 2
        if half:
            send = sum(t[half : 2 * half].astype(F32) for t in terms).astype(BF)
            terms = [t[:half] for t in terms]
    return sum(t[0].astype(F32) for t in terms)


def position_table(me, count):
    bits = count.bit_length() - 1
    device = jnp.arange(count, dtype=jnp.int32)
    differs = device ^ me
    one, two = (differs >> 1) & 1, (differs >> 2) & 1
    odd = (device & 1) == 1
    place = ((differs & 1) << (bits - 1)) | (jnp.where(odd, two, one) << (bits - 2))
    place = place | (jnp.where(odd, one, two) << (bits - 3))
    for k in range(3, bits):
        place = place | (((differs >> k) & 1) << (bits - 1 - k))
    return place


def device_table(me, count):
    bits = count.bit_length() - 1
    place = jnp.arange(count, dtype=jnp.int32)
    core = (place >> (bits - 1)) & 1
    upper, lower = (place >> (bits - 2)) & 1, (place >> (bits - 3)) & 1
    odd = ((me ^ core) & 1) == 1
    one, two = jnp.where(odd, lower, upper), jnp.where(odd, upper, lower)
    differs = core | (one << 1) | (two << 2)
    for k in range(3, bits):
        differs = differs | (((place >> (bits - 1 - k)) & 1) << k)
    return differs ^ me


class Blocks:
    def __init__(self, n, rows, tensor):
        self.n, self.rows, self.tensor = n, rows, tensor

    def at(self, d):
        return lax.rem(d, self.tensor), pl.multiple_of(lax.div(d, self.tensor) * self.rows, self.rows)

    def loads(self, devs, pieces, target, sems, lane=0):
        out, p = [], 0
        width = target.shape[-1]
        for piece in pieces:
            for j in range(piece.shape[0]):
                t, row = self.at(devs[p])
                out.append(pltpu.make_async_copy(
                    piece.at[j, pl.ds(0, self.rows), pl.ds(lane, width)], target.at[t, pl.ds(row, self.rows), :], sems.at[p]
                ))
                p += 1
        return out

    def stores(self, place, t, stage, keep, send, sems, action):
        half = self.n // 2
        for i in range(self.n // self.tensor):
            p = place[i * self.tensor + t]
            source = stage.at[pl.ds(i * self.rows, self.rows), :]
            kept = pltpu.make_async_copy(source, keep.at[lax.rem(p, half), pl.ds(0, self.rows), :], sems.at[i])
            sent = pltpu.make_async_copy(source, send.at[lax.rem(p, half), pl.ds(0, self.rows), :], sems.at[i])
            if action == "wait":
                kept.wait()
            else:
                pl.when(p < half)(kept.start)
                pl.when(p >= half)(sent.start)


def spread_constants(slot, cols, width):
    lane = np.arange(width)
    a, c = np.zeros((LANES, width), np.float32), np.zeros((LANES, width), np.float32)
    for j in range(slot):
        a[j] = lane % slot == j
    for j in range(cols):
        a[32 + j] = lane % cols == j
        c[64 + j] = lane % cols == j
    return jnp.asarray(a, BF), jnp.asarray(c, BF)


def small_masks(device, slot, cols, width, tensor):
    n = device.shape[0]
    shift = tensor.bit_length() - 1
    row = lax.broadcasted_iota(jnp.int32, (n, EXTRA, width), 1)
    lane = lax.broadcasted_iota(jnp.int32, (n, EXTRA, width), 2)
    i, t = device >> shift, device & (tensor - 1)
    in_head = (lane & (HD - 1)) >> (cols.bit_length() - 1)
    groups = width // HD // tensor
    vector = (row < 9) & (lane >= device * slot) & (lane < (device + 1) * slot)
    bias = (row >= 9) & (row < 9 + groups) & ((lane >> 6) == t * groups + row - 9) & (in_head == i)
    hidden = (row < width // HD) & ((lane >> 6) == row) & (in_head == i)
    return vector | bias, hidden, t


def unpack_small(extras, device, slot, cols, width, tensor):
    n = extras.shape[0]
    spread_a, spread_c = spread_constants(slot, cols, width)

    def body(x_ref, d_ref, a_ref, c_ref, vec_ref, bias_ref, up_ref):
        x = x_ref[...].reshape(n * EXTRA, 2 * LANES)
        d = d_ref[...].reshape(n, 1, 1)
        main, hidden, t = small_masks(d, slot, cols, width, tensor)
        for half in range(2):
            y = nn(x[:, half * LANES : (half + 1) * LANES], a_ref[...]).reshape(n, EXTRA, width)
            total = jnp.sum(jnp.where(main, y, 0.0), axis=0)
            for v in range(half, 6, 2):
                r = v // 2
                vec_ref[v : v + 1, :] = total[r : r + 1] + total[3 + r : 4 + r] + total[6 + r : 7 + r]
            bias_ref[half : half + 1, :] = jnp.sum(total[9:EXTRA], axis=0, keepdims=True)
        y = nn(x[:, :LANES], c_ref[...]).reshape(n, EXTRA, width)
        y = jnp.where(hidden, y, 0.0)
        for k in range(tensor):
            picked = jnp.sum(jnp.where(t == k, y, 0.0), axis=0)
            up_ref[k : k + 1, :] = jnp.sum(picked, axis=0, keepdims=True)

    row8 = (8, width)
    return call(
        body, (1,), [],
        [(extras, full(extras.shape)), (device, full(device.shape)), (spread_a, full(spread_a.shape)), (spread_c, full(spread_c.shape))],
        [(row8, F32, full(row8))] * 3, [], (3 * 2 * n * EXTRA * LANES * width, extras.size * 2), "unpack_small",
    )


def pack_small_grads(vec, bias, up, device, slot, cols, tensor):
    n, width = device.shape[0], vec.shape[-1]
    spread_a, spread_c = spread_constants(slot, cols, width)

    def body(v_ref, b_ref, u_ref, d_ref, a_ref, c_ref, out_ref):
        d = d_ref[...].reshape(n, 1, 1)
        main, hidden, t = small_masks(d, slot, cols, width, tensor)
        row = lax.broadcasted_iota(jnp.int32, (EXTRA, width), 0)
        halves = []
        for half in range(2):
            z = jnp.zeros((EXTRA, width), F32)
            for v in range(half, 6, 2):
                z = jnp.where(row == v // 2, v_ref[v : v + 1, :], z)
            z = jnp.where((row >= 9), b_ref[half : half + 1, :], z)
            spread = jnp.where(main, z[None], 0.0).astype(BF).reshape(n * EXTRA, width)
            halves.append(nt(spread, a_ref[...]))
        z = jnp.zeros((n, EXTRA, width), F32)
        for k in range(tensor):
            z = jnp.where(t == k, u_ref[k : k + 1, :].reshape(1, 1, width), z)
        spread = jnp.where(hidden, z, 0.0).astype(BF).reshape(n * EXTRA, width)
        halves[0] = halves[0] + nt(spread, c_ref[...])
        out_ref[...] = jnp.concatenate(halves, axis=1).astype(BF).reshape(n, EXTRA, 2 * LANES)

    shape = (n, EXTRA, PACK)
    return call(
        body, (1,), [],
        [(a, full(a.shape)) for a in (vec, bias, up, device, spread_a, spread_c)],
        [(shape, BF, full(shape))], [], (3 * 2 * n * EXTRA * LANES * width, 2 * n * EXTRA * PACK), "pack_small",
    )[0]


def three_parts(vector):
    high = lax.reduce_precision(vector, 8, 7)
    middle = lax.reduce_precision(vector - high, 8, 7)
    lowest = lax.reduce_precision(vector - high - middle, 8, 7)
    return jnp.stack([high, middle, lowest]).astype(BF)


def small_block(vectors, query_bias, value_bias, up_bias):
    slot = vectors.shape[1]
    parts = three_parts(vectors).reshape(9, 2, slot)

    def placed(array, row, lane):
        return jnp.pad(array, ((row, EXTRA - row - array.shape[0]), (lane, PACK - lane - array.shape[1])))

    return (
        placed(parts[:, 0], 0, 0) + placed(parts[:, 1], 0, LANES) + placed(query_bias, 9, 32)
        + placed(value_bias, 9, LANES + 32) + placed(up_bias, 0, 64)
    )


def attention_forward(tokens, pieces, lane, bias, devs, blocks):
    length, width = tokens.shape
    heads = blocks.tensor
    inner = heads * HD

    def body(devs_ref, x_ref, b_ref, *refs):
        piece_refs, (qkv_ref, e_ref, ctx_ref, ctxt_ref, inv_ref, ot_ref, w, ot_s, sems) = refs[: len(pieces)], refs[len(pieces) :]
        t = pl.program_id(0)

        @pl.when(t == 0)
        def _():
            copies = blocks.loads(devs_ref, piece_refs, w, sems, lane)
            for c in copies:
                c.start()
            for c in copies:
                c.wait()

        wt = w[t]
        pre = nn(x_ref[...], wt)
        b = b_ref[pl.ds(t, 1), :]
        col = lax.broadcasted_iota(jnp.int32, (1, PACK), 1)
        full_rows = (pre + b) * jnp.where(col < HD, 1.0 / math.sqrt(HD), 1.0)
        low = full_rows.astype(BF)
        qkv_ref[0] = low
        q, k = low[:, :HD], low[:, HD : 2 * HD]
        vt = low[:, 2 * HD :].T[:HD]
        scores = nt(k, q)
        e = jnp.exp(scores - jnp.max(scores, axis=0, keepdims=True)).astype(BF)
        e_ref[0] = e
        mixed = nn(jnp.concatenate([vt, jnp.ones((16, length), BF)], axis=0), e)
        inv = 1.0 / mixed[HD : HD + 1]
        inv_ref[0] = jnp.broadcast_to(inv, (8, length))
        ctxt_ref[pl.ds(t * HD, HD), :] = mixed[:HD] * inv
        ot_s[pl.ds(t * HD, HD), :] = wt[:, 2 * HD :].T[HD:].astype(F32)

        @pl.when(t == heads - 1)
        def _():
            ctx_ref[...] = ctxt_ref[...].T.astype(BF)
            ot_ref[...] = ot_s[...].astype(BF)

    by_head = lambda *s: pl.BlockSpec((1, *s), lambda t, *_: (t, 0, 0))
    return call(
        body, (heads,), [devs],
        [(tokens, full(tokens.shape)), (bias, full(bias.shape))] + [(p, ANY) for p in pieces],
        [
            ((heads, length, PACK), BF, by_head(length, PACK)),
            ((heads, length, length), BF, by_head(length, length)),
            ((length, inner), BF, full((length, inner))),
            ((inner, length), F32, full((inner, length))),
            ((heads, 8, length), F32, by_head(8, length)),
            ((inner, width), BF, full((inner, width))),
        ],
        [pltpu.VMEM((heads, width, PACK), BF), pltpu.VMEM((inner, width), F32), pltpu.SemaphoreType.DMA((blocks.n,))],
        (heads * (2 * length * width * PACK + 16 * length * length * HD), heads * length * length * 2), "attention_forward",
    )


def attention_backward(tokens_t, err_t, qkv, e, inv, ctx, ctxt, dctxt, place, blocks, extra):
    width, length = tokens_t.shape
    heads = blocks.tensor
    inner = heads * HD
    half = blocks.n // 2
    scale = 1.0 / math.sqrt(HD)

    def body(place_ref, xt_ref, et_ref, qkv_ref, e_ref, inv_ref, ctx_ref, ctxt_ref, dctxt_ref, keep_ref, send_ref, d_ref, b_ref, stage, go, sems):
        t = pl.program_id(0)

        @pl.when(t == 0)
        def _():
            go[...] = nn(et_ref[...], ctx_ref[...])

        q, k, v = qkv_ref[0, :, :HD], qkv_ref[0, :, HD : 2 * HD], qkv_ref[0, :, 2 * HD : 3 * HD]
        mine = pl.ds(t * HD, HD)
        dot = (dctxt_ref[mine, :].astype(F32) * inv_ref[0, :1, :]).astype(BF)
        delta = jnp.sum(dot.astype(F32) * ctxt_ref[mine, :], axis=0, keepdims=True)
        ee = e_ref[0]
        ds = (ee.astype(F32) * (nn(v, dot) - delta)).astype(BF)
        dv = nn(ee, dot.T)
        dk = nn(ds, q)
        dq = (nn(k.T, ds) * scale).T
        d = jnp.concatenate([dq, dk, dv, jnp.zeros_like(dv)], axis=1)
        b_ref[0] = jnp.broadcast_to(jnp.sum(d, axis=0, keepdims=True), (8, PACK))
        low = d.astype(BF)
        d_ref[0] = low
        slot = lax.rem(t, 2)

        @pl.when(t >= 2)
        def _():
            blocks.stores(place_ref, t - 2, stage.at[slot], keep_ref, send_ref, sems.at[slot], "wait")

        g = nn(xt_ref[...], low)
        for h in range(heads):
            @pl.when(t == h)
            def _():
                stage[slot] = jnp.concatenate([g[:, : 3 * HD], go[:, h * HD : (h + 1) * HD]], axis=1).astype(BF)

        blocks.stores(place_ref, t, stage.at[slot], keep_ref, send_ref, sems.at[slot], "start")

        @pl.when(t == heads - 1)
        def _():
            for last in range(max(heads - 2, 0), heads):
                blocks.stores(place_ref, last, stage.at[last % 2], keep_ref, send_ref, sems.at[last % 2], "wait")

    by_head = lambda *s: pl.BlockSpec((1, *s), lambda t, *_: (t, 0, 0))
    out = (half, blocks.rows + extra, PACK)
    return call(
        body, (heads,), [place],
        [
            (tokens_t, full(tokens_t.shape)), (err_t, full(err_t.shape)), (qkv, by_head(length, PACK)), (e, by_head(length, length)),
            (inv, by_head(8, length)), (ctx, full(ctx.shape)), (ctxt, full(ctxt.shape)), (dctxt, full(dctxt.shape)),
        ],
        [(out, BF, ANY), (out, BF, ANY), ((heads, length, PACK), BF, by_head(length, PACK)), ((heads, 8, PACK), F32, by_head(8, PACK))],
        [pltpu.VMEM((2, width, PACK), BF), pltpu.VMEM((width, inner), F32), pltpu.SemaphoreType.DMA((2, blocks.n // heads))],
        (heads * (2 * length * width * PACK + 32 * length * length * HD), heads * length * length * 2), "attention_backward",
    )


def tokens_backward(err_one, grads, weights, devs, blocks):
    length, width = err_one.shape
    heads = blocks.tensor
    groups = len(grads)
    flat = [p for pieces, _ in weights for p in pieces]

    def body(devs_ref, err_ref, *refs):
        d_refs, piece_refs, (out_ref, w, sems) = refs[:groups], refs[groups : groups + len(flat)], refs[groups + len(flat) :]
        c = pl.program_id(0)

        @pl.when(c == 0)
        def _():
            at, copies = 0, []
            for g, (pieces, lane) in enumerate(weights):
                copies += blocks.loads(devs_ref, piece_refs[at : at + len(pieces)], w.at[g], sems.at[g], lane)
                at += len(pieces)
            for copy in copies:
                copy.start()
            for copy in copies:
                copy.wait()

        total = err_ref[...]
        for g in range(groups):
            for t in range(heads):
                total = total + nt(d_refs[g][t][:, : 3 * HD], w[g, t][:, : 3 * HD])
        out_ref[...] = total

    chunk = min(256, length)
    rows = pl.BlockSpec((chunk, width), lambda c, *_: (c, 0))
    return call(
        body, (length // chunk,), [devs],
        [(err_one, rows)] + [(d, pl.BlockSpec((heads, chunk, PACK), lambda c, *_: (0, c, 0))) for d in grads] + [(p, ANY) for p in flat],
        [((length, width), F32, rows)],
        [pltpu.VMEM((groups, heads, width, PACK), BF), pltpu.SemaphoreType.DMA((groups, blocks.n))],
        (2 * groups * heads * length * width * PACK, groups * heads * width * PACK * 2 + length * width * 8), "tokens_backward",
    )[0]


def layer_norm(residual):
    centered = residual - jnp.mean(residual, axis=-1, keepdims=True)
    inverse = lax.rsqrt(jnp.mean(centered * centered, axis=-1, keepdims=True) + EPSILON)
    return centered * inverse, inverse


def norm_backward(scaled, normed, inverse):
    first = jnp.mean(scaled, axis=-1, keepdims=True)
    second = jnp.mean(scaled * normed, axis=-1, keepdims=True)
    return inverse * (scaled - first - normed * second)


def output_and_up(tokens, contexts, outputs, vec, up_bias, pieces, devs, blocks):
    length, width = tokens.shape
    tensor = blocks.tensor
    hidden_width = tensor * pieces[0].shape[-1]
    part = pieces[0].shape[-1]
    groups = len(contexts)
    chunk = min(256, length)

    def body(devs_ref, x_ref, vec_ref, ub_ref, *refs):
        c_refs, o_refs, piece_refs = refs[:groups], refs[groups : 2 * groups], refs[2 * groups : 2 * groups + len(pieces)]
        norm_ref, inv_ref, hid_ref, hidt_ref, act_ref, slope_ref, w, sems = refs[2 * groups + len(pieces) :]
        c = pl.program_id(0)

        @pl.when(c == 0)
        def _():
            for copy in blocks.loads(devs_ref, piece_refs, w, sems):
                copy.start()

        attended = sum(nn(a[...], b[...]) for a, b in zip(c_refs, o_refs)) + vec_ref[0:1, :]
        normed, inverse = layer_norm(x_ref[...].astype(F32) + attended)
        norm_ref[...] = normed
        inv_ref[...] = inverse
        first_out = normed * vec_ref[1:2, :] + vec_ref[2:3, :]
        hidden = first_out.astype(BF)
        hid_ref[...] = hidden
        hidt_ref[...] = first_out.T.astype(BF)

        @pl.when(c == 0)
        def _():
            for copy in blocks.loads(devs_ref, piece_refs, w, sems):
                copy.wait()

        for t in range(tensor):
            pre = nn(hidden, w[t]) + ub_ref[t : t + 1, :]
            phi = 0.5 * (1.0 + lax.erf(pre * (1.0 / math.sqrt(2.0))))
            act_ref[:, t * part : (t + 1) * part] = (pre * phi).astype(BF)
            density = jnp.exp(-0.5 * pre * pre) * (1.0 / math.sqrt(2.0 * math.pi))
            slope_ref[:, t * part : (t + 1) * part] = (phi + pre * density).astype(BF)

    rows = lambda n: pl.BlockSpec((chunk, n), lambda c, *_: (c, 0))
    cols = lambda n: pl.BlockSpec((n, chunk), lambda c, *_: (0, c))
    return call(
        body, (length // chunk,), [devs],
        [(tokens, rows(width)), (vec, full(vec.shape)), (up_bias, full(up_bias.shape))]
        + [(a, rows(a.shape[1])) for a in contexts] + [(b, full(b.shape)) for b in outputs] + [(p, ANY) for p in pieces],
        [
            ((length, width), F32, rows(width)), ((length, 1), F32, rows(1)), ((length, width), BF, rows(width)),
            ((width, length), BF, cols(width)), ((length, hidden_width), BF, rows(hidden_width)), ((length, hidden_width), BF, rows(hidden_width)),
        ],
        [pltpu.VMEM((tensor, width, part), BF), pltpu.SemaphoreType.DMA((blocks.n,))],
        (2 * length * width * (width + hidden_width), 16 * length * width + 4 * length * hidden_width), "output_and_up",
    )


def down_and_norm(act, normed_one, cotangent, vec, pieces, devs, blocks):
    length, width = normed_one.shape
    tensor = blocks.tensor
    part = pieces[0].shape[-1]
    chunk = min(256, length)

    def body(devs_ref, act_ref, n1_ref, cot_ref, vec_ref, *refs):
        piece_refs, (out_ref, err_ref, errlow_ref, errt_ref, sums_ref, w, sems) = refs[: len(pieces)], refs[len(pieces) :]
        c = pl.program_id(0)

        @pl.when(c == 0)
        def _():
            copies = blocks.loads(devs_ref, piece_refs, w, sems)
            for copy in copies:
                copy.start()
            for copy in copies:
                copy.wait()

        branch = sum(nt(act_ref[:, t * part : (t + 1) * part], w[t]) for t in range(tensor)) + vec_ref[3:4, :]
        first_out = n1_ref[...] * vec_ref[1:2, :] + vec_ref[2:3, :]
        normed, inverse = layer_norm(first_out + branch)
        out_ref[...] = (normed * vec_ref[4:5, :] + vec_ref[5:6, :]).astype(BF)
        upstream = cot_ref[...].astype(F32)
        err = norm_backward(upstream * vec_ref[4:5, :], normed, inverse)
        err_ref[...] = err
        errlow_ref[...] = err.astype(BF)
        errt_ref[...] = err.T.astype(BF)
        rows = [jnp.sum(a, axis=0, keepdims=True) for a in (err, upstream * normed, upstream)]
        sums = jnp.concatenate(rows + [jnp.zeros((5, width), F32)], axis=0)

        @pl.when(c == 0)
        def _():
            sums_ref[...] = sums

        @pl.when(c > 0)
        def _():
            sums_ref[...] += sums

    rows = lambda n: pl.BlockSpec((chunk, n), lambda c, *_: (c, 0))
    return call(
        body, (length // chunk,), [devs],
        [(act, rows(act.shape[1])), (normed_one, rows(width)), (cotangent, rows(width)), (vec, full(vec.shape))] + [(p, ANY) for p in pieces],
        [
            ((length, width), BF, rows(width)), ((length, width), F32, rows(width)), ((length, width), BF, rows(width)),
            ((width, length), BF, pl.BlockSpec((width, chunk), lambda c, *_: (0, c))), ((8, width), F32, full((8, width))),
        ],
        [pltpu.VMEM((tensor, width, part), BF), pltpu.SemaphoreType.DMA((blocks.n,))],
        (2 * length * width * act.shape[1], 2 * act.size + 16 * length * width), "down_and_norm",
    )


def weight_gradient(left_t, right, place, blocks):
    width, length = left_t.shape
    tensor = blocks.tensor
    part = right.shape[1] // tensor

    def body(place_ref, l_ref, r_ref, keep_ref, send_ref, stage, sems):
        t = pl.program_id(0)
        slot = lax.rem(t, 2)

        @pl.when(t >= 2)
        def _():
            blocks.stores(place_ref, t - 2, stage.at[slot], keep_ref, send_ref, sems.at[slot], "wait")

        stage[slot] = nn(l_ref[...], r_ref[...]).astype(BF)
        blocks.stores(place_ref, t, stage.at[slot], keep_ref, send_ref, sems.at[slot], "start")

        @pl.when(t == tensor - 1)
        def _():
            for last in range(max(tensor - 2, 0), tensor):
                blocks.stores(place_ref, last, stage.at[last % 2], keep_ref, send_ref, sems.at[last % 2], "wait")

    out = (blocks.n // 2, blocks.rows, part)
    return call(
        body, (tensor,), [place],
        [(left_t, full(left_t.shape)), (right, pl.BlockSpec((length, part), lambda t, *_: (0, t)))],
        [(out, BF, ANY), (out, BF, ANY)],
        [pltpu.VMEM((2, width, part), BF), pltpu.SemaphoreType.DMA((2, blocks.n // tensor))],
        (2 * length * width * right.shape[1], 2 * (left_t.size + right.size + width * right.shape[1])), "weight_gradient",
    )


def pre_gradient(err_low, slope, pieces, devs, blocks):
    length, width = err_low.shape
    tensor = blocks.tensor
    part = pieces[0].shape[-1]

    def body(devs_ref, e_ref, s_ref, *refs):
        piece_refs, (out_ref, sum_ref, w, sems) = refs[: len(pieces)], refs[len(pieces) :]
        t = pl.program_id(0)

        @pl.when(t == 0)
        def _():
            copies = blocks.loads(devs_ref, piece_refs, w, sems)
            for copy in copies:
                copy.start()
            for copy in copies:
                copy.wait()

        grad = nn(e_ref[...], w[t]) * s_ref[...].astype(F32)
        out_ref[...] = grad.astype(BF)
        sum_ref[pl.ds(t, 1), :] = jnp.sum(grad, axis=0, keepdims=True)

    part_cols = pl.BlockSpec((length, part), lambda t, *_: (0, t))
    return call(
        body, (tensor,), [devs],
        [(err_low, full(err_low.shape)), (slope, part_cols)] + [(p, ANY) for p in pieces],
        [(slope.shape, BF, part_cols), ((8, part), F32, full((8, part)))],
        [pltpu.VMEM((tensor, width, part), BF), pltpu.SemaphoreType.DMA((blocks.n,))],
        (2 * length * width * slope.shape[1], 4 * slope.size + 2 * width * slope.shape[1]), "pre_gradient",
    )


def hidden_gradient(grad_pre, err_two, normed_one, inverse_one, vec, outputs, pieces, devs, blocks):
    length, width = err_two.shape
    tensor = blocks.tensor
    part = pieces[0].shape[-1]
    groups = len(outputs)
    chunk = min(256, length)

    def body(devs_ref, g_ref, e2_ref, n1_ref, i1_ref, vec_ref, *refs):
        o_refs, piece_refs = refs[:groups], refs[groups : groups + len(pieces)]
        err_ref, errt_ref, sums_ref, *dctx_refs, w, sems = refs[groups + len(pieces) :]
        c = pl.program_id(0)

        @pl.when(c == 0)
        def _():
            copies = blocks.loads(devs_ref, piece_refs, w, sems)
            for copy in copies:
                copy.start()
            for copy in copies:
                copy.wait()

        back = sum(nt(g_ref[:, t * part : (t + 1) * part], w[t]) for t in range(tensor))
        err_in = e2_ref[...] + back
        normed = n1_ref[...]
        err = norm_backward(err_in * vec_ref[1:2, :], normed, i1_ref[...])
        err_ref[...] = err
        err_t = err.T.astype(BF)
        errt_ref[...] = err_t
        for o, d in zip(o_refs, dctx_refs):
            d[...] = nn(o[...], err_t).astype(BF)
        rows = [jnp.sum(a, axis=0, keepdims=True) for a in (err, err_in * normed, err_in)]
        sums = jnp.concatenate(rows + [jnp.zeros((5, width), F32)], axis=0)

        @pl.when(c == 0)
        def _():
            sums_ref[...] = sums

        @pl.when(c > 0)
        def _():
            sums_ref[...] += sums

    rows = lambda n: pl.BlockSpec((chunk, n), lambda c, *_: (c, 0))
    cols = lambda n: pl.BlockSpec((n, chunk), lambda c, *_: (0, c))
    return call(
        body, (length // chunk,), [devs],
        [(grad_pre, rows(grad_pre.shape[1])), (err_two, rows(width)), (normed_one, rows(width)), (inverse_one, rows(1)), (vec, full(vec.shape))]
        + [(o, full(o.shape)) for o in outputs] + [(p, ANY) for p in pieces],
        [((length, width), F32, rows(width)), ((width, length), BF, cols(width)), ((8, width), F32, full((8, width)))]
        + [((o.shape[0], length), BF, cols(o.shape[0])) for o in outputs],
        [pltpu.VMEM((tensor, width, part), BF), pltpu.SemaphoreType.DMA((blocks.n,))],
        (2 * length * width * (grad_pre.shape[1] + width), 2 * grad_pre.size + 18 * length * width), "hidden_gradient",
    )


def local(
    tokens, query_weight, key_weight, value_weight, output_weight, query_bias, value_bias,
    output_bias, first_gain, first_shift, up_weight, up_bias, down_weight, down_bias,
    second_gain, second_shift, cotangent,
):
    dp, tensor = lax.axis_size("dp"), lax.axis_size("tensor")
    count = dp * tensor
    rows = query_weight.shape[0]
    width = rows * dp
    groups = query_weight.shape[1] // HD
    heads = groups * tensor
    slot = output_bias.shape[0]
    cols = query_bias.shape[1]
    me = lax.axis_index(AXES)
    place, devs = position_table(me, count), device_table(me, count)
    direct = rows % 16 == 0

    vectors = jnp.stack([output_bias, first_gain, first_shift, down_bias, second_gain, second_shift])
    extra = small_block(vectors, query_bias, value_bias, up_bias)
    output_turned = output_weight.T
    by_group = [
        jnp.concatenate([w[:, c * HD : (c + 1) * HD] for w in (query_weight, key_weight, value_weight, output_turned)], axis=1)
        for c in range(groups)
    ]
    first_set = gather_blocks(jnp.concatenate([by_group[0], extra], axis=0), count)
    second_set = gather_blocks(jnp.concatenate(by_group[1:], axis=1), count)
    up_set = gather_blocks(up_weight, count)
    down_set = gather_blocks(down_weight.T, count)

    extras = jnp.concatenate([p[:, rows:] for p in first_set], axis=0)
    if direct:
        blocks = Blocks(count, rows, tensor)
        block_place, block_devs = place, devs
    else:
        blocks = Blocks(tensor, width, tensor)
        block_place = block_devs = jnp.arange(tensor, dtype=jnp.int32)

        def whole(pieces):
            ordered = jnp.take(jnp.concatenate(pieces, axis=0)[:, :rows], place, axis=0)
            return [ordered.reshape(dp, tensor, rows, -1).transpose(1, 0, 2, 3).reshape(tensor, width, -1)]

        first_set, second_set, up_set, down_set = (whole(s) for s in (first_set, second_set, up_set, down_set))

    def scattered(keep, send, more=None):
        if not direct:
            stacked = jnp.concatenate([keep, send], axis=0).reshape(tensor, dp, rows, -1)
            stacked = jnp.take(stacked.transpose(1, 0, 2, 3).reshape(count, rows, -1), devs, axis=0)
            if more is not None:
                stacked = jnp.concatenate([stacked, more], axis=1)
            keep, send = stacked[: count // 2], stacked[count // 2 :]
        elif more is not None:
            keep = lax.dynamic_update_slice(keep, more[: count // 2], (0, rows, 0))
            send = lax.dynamic_update_slice(send, more[count // 2 :], (0, rows, 0))
        return scatter_blocks(keep, send, count)

    weights = [(first_set, 0)] + [(second_set, c * PACK) for c in range(groups - 1)]
    vec, bias_rows, up_rows = unpack_small(extras, devs.reshape(count, 1), slot, cols, width, tensor)
    bias_heads = bias_rows[:2].reshape(2, tensor, groups, HD).transpose(2, 1, 0, 3)
    bias_pack = jnp.concatenate(
        [bias_heads[:, :, 0], jnp.zeros_like(bias_heads[:, :, 0]), bias_heads[:, :, 1], jnp.zeros_like(bias_heads[:, :, 0])], axis=-1
    )
    forward = [attention_forward(tokens, p, lane, bias_pack[c], block_devs, blocks) for c, (p, lane) in enumerate(weights)]
    outputs = [f[5] for f in forward]
    normed_one, inverse_one, hidden, hidden_t, act, slope = output_and_up(
        tokens, [f[2] for f in forward], outputs, vec, up_rows, up_set, block_devs, blocks
    )
    layer_out, err_two, err_two_low, err_two_t, sums_two = down_and_norm(act, normed_one, cotangent, vec, down_set, block_devs, blocks)
    grad_down = scattered(*weight_gradient(err_two_t, act, block_place, blocks))
    grad_pre, up_sums = pre_gradient(err_two_low, slope, down_set, block_devs, blocks)
    grad_up = scattered(*weight_gradient(hidden_t, grad_pre, block_place, blocks))
    err_one, err_one_t, sums_one, *context_grads = hidden_gradient(
        grad_pre, err_two, normed_one, inverse_one, vec, outputs, up_set, block_devs, blocks
    )
    tokens_t = tokens.T
    backward = [None] * groups
    for c in reversed(range(groups)):
        qkv, e, ctx, ctxt, inv, _ = forward[c]
        backward[c] = attention_backward(
            tokens_t, err_one_t, qkv, e, inv, ctx, ctxt, context_grads[c], block_place, blocks, EXTRA if direct and c == 0 else 0
        )
    packed = [None] * groups
    for c in reversed(range(1, groups)):
        packed[c] = scattered(*backward[c][:2])
    sums = jnp.stack([b[3][:, 0] for b in backward]).reshape(groups, tensor, 4, HD).transpose(2, 1, 0, 3).reshape(4, width)
    bias_grads = jnp.concatenate([sums[0:1], sums[2:3], jnp.zeros((6, width), F32)], axis=0)
    vec_grads = jnp.concatenate([sums_one[:3], sums_two[:3], jnp.zeros((2, width), F32)], axis=0)
    small = pack_small_grads(vec_grads, bias_grads, up_sums, devs.reshape(count, 1), slot, cols, tensor)
    first = scattered(*backward[0][:2], small)
    grad_tokens = tokens_backward(err_one, [b[2] for b in backward], weights, block_devs, blocks)

    packed[0] = first[:rows]
    tail = first[rows:]
    out = jnp.stack(packed, axis=1).reshape(rows, groups, 4, HD)
    out_query, out_key, out_value, out_output = (out[:, :, i].reshape(rows, groups * HD) for i in range(4))
    vecs = [tail[v // 2, (v % 2) * LANES : (v % 2) * LANES + slot] for v in range(6)]
    return (
        layer_out,
        grad_tokens,
        out_query,
        out_key,
        out_value,
        out_output.T,
        tail[9 : 9 + groups, 32 : 32 + cols],
        tail[9 : 9 + groups, LANES + 32 : LANES + 32 + cols],
        vecs[0],
        vecs[1],
        vecs[2],
        grad_up,
        tail[: up_bias.shape[0], 64 : 64 + cols],
        grad_down.T,
        vecs[3],
        vecs[4],
        vecs[5],
    )


def solution(mesh):
    both, cross, turned, vector = P(AXES, None), P("dp", "tensor"), P("tensor", "dp"), P(AXES)
    return jax.shard_map(
        local,
        mesh=mesh,
        in_specs=(
            both, cross, cross, cross, turned, turned, turned, vector, vector, vector,
            cross, turned, turned, vector, vector, vector, both,
        ),
        out_specs=(
            both, both, cross, cross, cross, turned, turned, turned, vector, vector, vector,
            cross, turned, turned, vector, vector, vector,
        ),
        check_vma=False,
    )
```

```python
import functools
import math

import jax
import jax.numpy as jnp
import numpy as np
from jax import lax
from jax.experimental import pallas as pl
from jax.experimental.pallas import tpu as pltpu
from jax.sharding import PartitionSpec as P

HD = 64
L = 1024
PACK = 4 * HD
EPSILON = 1e-12
AXES = ("dp", "tensor")
EXTRA = 16
LANES = 128
BF = jnp.bfloat16
F32 = jnp.float32
SDS = jax.ShapeDtypeStruct
ANY = pl.BlockSpec(memory_space=pl.ANY)


def nn(a, b):
    return lax.dot_general(a, b, (((1,), (0,)), ((), ())), preferred_element_type=F32)


def nt(a, b):
    return lax.dot_general(a, b, (((1,), (1,)), ((), ())), preferred_element_type=F32)


def full(shape):
    return pl.BlockSpec(shape, lambda *_: (0,) * len(shape))


def once(shape):
    return pl.BlockSpec(shape, lambda *_: (0,) * len(shape), pipeline_mode=pl.Buffered(1))


def at_index(array, i):
    shape = (1, *array.shape[1:])
    return array, pl.BlockSpec(shape, lambda *_: (i,) + (0,) * (len(shape) - 1), pipeline_mode=pl.Buffered(1))


def call(body, grid, tables, ins, outs, scratch, cost, name):
    flops, moved = cost
    return pl.pallas_call(
        body,
        grid_spec=pltpu.PrefetchScalarGridSpec(
            num_scalar_prefetch=len(tables),
            grid=grid,
            in_specs=[s for _, s in ins],
            out_specs=[s for _, _, s in outs],
            scratch_shapes=scratch,
        ),
        out_shape=[SDS(s, d) for s, d, _ in outs],
        compiler_params=pltpu.CompilerParams(
            dimension_semantics=("arbitrary",) * len(grid), vmem_limit_bytes=60 * 2**20
        ),
        cost_estimate=pl.CostEstimate(flops=int(flops * 0.2), bytes_accessed=int(moved * 0.2), transcendentals=0),
        name=name,
    )(*tables, *[a for a, _ in ins])


def exchange(array, differs, count):
    return lax.ppermute(array, AXES, [(d, d ^ differs) for d in range(count)])


def phases_of(count):
    bits = count.bit_length() - 1
    return [*((k, 1) for k in range(bits - 1, 4, -1)), (3, 2), (1, 2), (0, 1)]


class Gathering:
    def __init__(self, block, count):
        self.pieces, self.count, self.phases = [block[None]], count, phases_of(count)
        while self.phases[0][1] == 1:
            self.move(self.outgoing())

    def outgoing(self):
        if self.phases[0] != (0, 1) and len(self.pieces) > 1:
            self.pieces = [jnp.concatenate(self.pieces, axis=0)]
        return self.pieces

    def move(self, pieces):
        low, bits = self.phases.pop(0)
        self.pieces = self.pieces + [exchange(p, k << low, self.count) for k in range(1, 1 << bits) for p in pieces]


class Scattering:
    def __init__(self, keep, send, count):
        self.terms, self.sends, self.count, self.phases = [keep], [send], count, phases_of(count)[::-1]

    def move(self, sends):
        low, _ = self.phases.pop(0)
        self.terms += [exchange(p, k << low, self.count) for k, p in enumerate(sends, 1)]
        self.sends = None

    def looked_at(self, *since):
        if since:
            self.terms = lax.optimization_barrier((self.terms, since))[0]

    def outgoing(self):
        if self.sends is None:
            parts = 1 << self.phases[0][1]
            size = self.terms[0].shape[0] // parts
            self.sends = [sum(t[k * size : (k + 1) * size].astype(F32) for t in self.terms).astype(BF) for k in range(1, parts)]
            self.terms = [t[:size] for t in self.terms]
        return self.sends

    def result(self):
        return sum(t[0].astype(F32) for t in self.terms)


def wave(moves, *beside, since=()):
    moves = [m for m in moves if m.phases]
    for m in moves:
        if since and isinstance(m, Scattering):
            m.looked_at(*since)
    outgoing, beside = lax.optimization_barrier(([m.outgoing() for m in moves], beside))
    for m, array in zip(moves, outgoing):
        m.move(array)
    return beside[0] if len(beside) == 1 else beside


def fields_of(count):
    top, fields = count.bit_length() - 1, []
    for low, bits in phases_of(count)[::-1]:
        top -= bits
        fields.append((low, bits, top))
    return fields


def position_table(me, count):
    differs = jnp.arange(count, dtype=jnp.int32) ^ me
    return sum(((differs >> low) & ((1 << bits) - 1)) << at for low, bits, at in fields_of(count))


def device_table(me, count):
    place = jnp.arange(count, dtype=jnp.int32)
    return sum(((place >> at) & ((1 << bits) - 1)) << low for low, bits, at in fields_of(count)) ^ me


class Blocks:
    def __init__(self, n, rows, tensor):
        self.n, self.rows, self.tensor = n, rows, tensor

    def at(self, d):
        return lax.rem(d, self.tensor), pl.multiple_of(lax.div(d, self.tensor) * self.rows, self.rows)

    def loads(self, devs, pieces, target, sems, lane=0, top=0):
        out, p = [], 0
        width = target.shape[-1]
        for piece in pieces:
            for j in range(piece.shape[0]):
                t, row = self.at(devs[p])
                out.append(pltpu.make_async_copy(
                    piece.at[j, pl.ds(top, self.rows), pl.ds(lane, width)], target.at[t, pl.ds(row, self.rows), :], sems.at[p]
                ))
                p += 1
        return out

    def ordered_stores(self, t, stage, out, sems):
        return [pltpu.make_async_copy(stage.at[i], out.at[i * self.tensor + t], sems.at[i]) for i in range(self.n // self.tensor)]

    def stores(self, place, t, stage, keep, send, sems, action):
        half = self.n // 2
        for i in range(self.n // self.tensor):
            p = place[i * self.tensor + t]
            kept = pltpu.make_async_copy(stage.at[i], keep.at[lax.rem(p, half)], sems.at[i])
            if action == "wait":
                kept.wait()
            else:
                sent = pltpu.make_async_copy(stage.at[i], send.at[lax.rem(p, half)], sems.at[i])
                pl.when(p < half)(kept.start)
                pl.when(p >= half)(sent.start)


def spread_constants(slot, cols, width):
    lane = np.arange(width)
    a, c = np.zeros((LANES, width), np.float32), np.zeros((LANES, width), np.float32)
    for j in range(slot):
        a[j] = lane % slot == j
    for j in range(cols):
        a[32 + j] = lane % cols == j
        c[64 + j] = lane % cols == j
    return jnp.asarray(a, BF), jnp.asarray(c, BF)


def small_masks(device, slot, cols, width, tensor):
    n = device.shape[0]
    shift = tensor.bit_length() - 1
    row = lax.broadcasted_iota(jnp.int32, (n, EXTRA, width), 1)
    lane = lax.broadcasted_iota(jnp.int32, (n, EXTRA, width), 2)
    i, t = device >> shift, device & (tensor - 1)
    in_head = (lane & (HD - 1)) >> (cols.bit_length() - 1)
    groups = width // HD // tensor
    vector = (row < 9) & (lane >= device * slot) & (lane < (device + 1) * slot)
    bias = (row >= 9) & (row < 9 + groups) & ((lane >> 6) == t * groups + row - 9) & (in_head == i)
    hidden = (row < width // HD) & ((lane >> 6) == row) & (in_head == i)
    return vector | bias, hidden, t


def unpack_small(extras, device, slot, cols, width, tensor):
    n = extras.shape[0]
    spread_a, spread_c = spread_constants(slot, cols, width)

    def body(x_ref, d_ref, a_ref, c_ref, vec_ref, bias_ref, up_ref):
        x = x_ref[...].reshape(n * EXTRA, 2 * LANES)
        d = d_ref[...].reshape(n, 1, 1)
        main, hidden, t = small_masks(d, slot, cols, width, tensor)
        for half in range(2):
            y = nn(x[:, half * LANES : (half + 1) * LANES], a_ref[...]).reshape(n, EXTRA, width)
            total = jnp.sum(jnp.where(main, y, 0.0), axis=0)
            for v in range(half, 6, 2):
                r = v // 2
                vec_ref[v : v + 1, :] = total[r : r + 1] + total[3 + r : 4 + r] + total[6 + r : 7 + r]
            bias_ref[half : half + 1, :] = jnp.sum(total[9:EXTRA], axis=0, keepdims=True)
        y = nn(x[:, :LANES], c_ref[...]).reshape(n, EXTRA, width)
        y = jnp.where(hidden, y, 0.0)
        for k in range(tensor):
            picked = jnp.sum(jnp.where(t == k, y, 0.0), axis=0)
            up_ref[k : k + 1, :] = jnp.sum(picked, axis=0, keepdims=True)

    row8 = (8, width)
    return call(
        body, (1,), [],
        [(extras, full(extras.shape)), (device, full(device.shape)), (spread_a, full(spread_a.shape)), (spread_c, full(spread_c.shape))],
        [(row8, F32, full(row8))] * 3, [], (3 * 2 * n * EXTRA * LANES * width, extras.size * 2), "unpack_small",
    )


def pack_small_grads(vec, up, device, slot, cols, tensor):
    n, width = device.shape[0], vec.shape[-1]
    spread_a, spread_c = spread_constants(slot, cols, width)

    def body(v_ref, u_ref, d_ref, a_ref, c_ref, out_ref):
        d = d_ref[...].reshape(n, 1, 1)
        main, hidden, t = small_masks(d, slot, cols, width, tensor)
        row = lax.broadcasted_iota(jnp.int32, (EXTRA, width), 0)
        halves = []
        for half in range(2):
            z = jnp.zeros((EXTRA, width), F32)
            for v in range(half, 6, 2):
                z = jnp.where(row == v // 2, v_ref[v : v + 1, :], z)
            spread = jnp.where(main, z[None], 0.0).astype(BF).reshape(n * EXTRA, width)
            halves.append(nt(spread, a_ref[...]))
        z = jnp.zeros((n, EXTRA, width), F32)
        for k in range(tensor):
            z = jnp.where(t == k, u_ref[k : k + 1, :].reshape(1, 1, width), z)
        spread = jnp.where(hidden, z, 0.0).astype(BF).reshape(n * EXTRA, width)
        halves[0] = halves[0] + nt(spread, c_ref[...])
        out_ref[...] = jnp.concatenate(halves, axis=1).astype(BF).reshape(n, EXTRA, 2 * LANES)

    shape = (n, EXTRA, PACK)
    return call(
        body, (1,), [],
        [(a, full(a.shape)) for a in (vec, up, device, spread_a, spread_c)],
        [(shape, BF, full(shape))], [], (3 * 2 * n * EXTRA * LANES * width, 2 * n * EXTRA * PACK), "pack_small",
    )[0]


def three_parts(vector):
    high = lax.reduce_precision(vector, 8, 7)
    middle = lax.reduce_precision(vector - high, 8, 7)
    lowest = lax.reduce_precision(vector - high - middle, 8, 7)
    return jnp.stack([high, middle, lowest]).astype(BF)


def small_block(vectors, query_bias, value_bias, up_bias):
    slot = vectors.shape[1]
    parts = three_parts(vectors).reshape(9, 2, slot)

    def placed(array, row, lane):
        return jnp.pad(array, ((row, EXTRA - row - array.shape[0]), (lane, PACK - lane - array.shape[1])))

    return (
        placed(parts[:, 0], 0, 0) + placed(parts[:, 1], 0, LANES) + placed(query_bias, 9, 32)
        + placed(value_bias, 9, LANES + 32) + placed(up_bias, 0, 64)
    )


def attention_forward(tokens, pieces, bias, devs, blocks):
    length, width = tokens.shape
    heads = blocks.tensor
    inner = heads * HD
    groups = pieces[0].shape[-1] // PACK

    def body(devs_ref, x_ref, b_ref, *refs):
        piece_refs, (qkv_ref, e_ref, ctx_ref, ctxt_ref, inv_ref, ot_ref, w, ot_s, vt_s, sems) = refs[: len(pieces)], refs[len(pieces) :]
        c, t = pl.program_id(0), pl.program_id(1)

        loads = [blocks.loads(devs_ref, piece_refs, w.at[g], sems.at[g], g * PACK) for g in range(groups)]

        @pl.when((c == 0) & (t == 0))
        def _():
            for copies in loads:
                for copy in copies:
                    copy.start()
            vt_s[HD:, :] = jnp.ones((HD, length), BF)

        for g in range(groups):
            @pl.when((c == g) & (t == 0))
            def _():
                for copy in loads[g]:
                    copy.wait()

        wt = w[c, t]
        col = lax.broadcasted_iota(jnp.int32, (1, PACK), 1)
        pre = nn(x_ref[...], wt) + b_ref[c, pl.ds(t, 1), :]
        low = (pre * jnp.where(col < HD, 1.0 / math.sqrt(HD), 1.0)).astype(BF)
        qkv_ref[0] = low
        q, k = low[:, :HD], low[:, HD : 2 * HD]
        vt_s[:HD, :] = low[:, 2 * HD :].T[:HD]
        square = pre[:, : 2 * HD] * pre[:, : 2 * HD]
        pick = lax.broadcasted_iota(jnp.int32, (2 * HD, LANES), 0) // HD == lax.broadcasted_iota(jnp.int32, (2 * HD, LANES), 1)
        norms = jnp.max(nn(square.astype(BF), pick.astype(BF)), axis=0, keepdims=True)
        bound = jnp.sqrt(norms[0, 0] * norms[0, 1]) * (1.1 / math.sqrt(HD))

        @pl.when(bound <= 40.0)
        def _():
            e_ref[0] = jnp.exp(nt(k, q)).astype(BF)

        @pl.when(jnp.logical_not(bound <= 40.0))
        def _():
            def some(j, _):
                at = pl.ds(pl.multiple_of(j * LANES, LANES), LANES)
                scores = nt(k, qkv_ref[0, at, :][:, :HD])
                e_ref[0, :, at] = jnp.exp(scores - jnp.max(scores, axis=0, keepdims=True)).astype(BF)
                return 0

            lax.fori_loop(0, length // LANES, some, 0)

        mixed = nn(vt_s[...], e_ref[0])
        inv = 1.0 / mixed[HD : HD + 1]
        inv_ref[0] = jnp.broadcast_to(inv, (8, length))
        ctxt_ref[0, pl.ds(t * HD, HD), :] = mixed[:HD] * inv
        ot_s[pl.ds(t * HD, HD), :] = wt[:, 2 * HD :].T[HD:].astype(F32)

        @pl.when(t == heads - 1)
        def _():
            ctx_ref[0] = ctxt_ref[0].T.astype(BF)
            ot_ref[0] = ot_s[...].astype(BF)

    by_head = lambda *s: pl.BlockSpec((1, *s), lambda c, t, *_: (c * heads + t, 0, 0))
    by_group = lambda *s: pl.BlockSpec((1, *s), lambda c, t, *_: (c, 0, 0))
    return call(
        body, (groups, heads), [devs],
        [(tokens, full(tokens.shape)), (bias, full(bias.shape))] + [(p, ANY) for p in pieces],
        [
            ((groups * heads, length, PACK), BF, by_head(length, PACK)),
            ((groups * heads, length, length), BF, by_head(length, length)),
            ((groups, length, inner), BF, by_group(length, inner)),
            ((groups, inner, length), F32, by_group(inner, length)),
            ((groups * heads, 8, length), F32, by_head(8, length)),
            ((groups, inner, width), BF, by_group(inner, width)),
        ],
        [pltpu.VMEM((groups, heads, width, PACK), BF), pltpu.VMEM((inner, width), F32), pltpu.VMEM((2 * HD, length), BF), pltpu.SemaphoreType.DMA((groups, blocks.n))],
        (groups * heads * (2 * length * width * PACK + 16 * length * length * HD), groups * heads * length * length * 2), "attention_forward",
    )


def attention_backward(tokens_t, err_t, forward, index, dctxt, place, blocks, more=None):
    width, length = tokens_t.shape
    qkv, e, ctx, ctxt, inv, _ = forward
    heads = blocks.tensor
    inner = heads * HD
    half = blocks.n // 2
    scale = 1.0 / math.sqrt(HD)
    rows, extra = blocks.rows, 0 if more is None else 1

    def body(place_ref, qkv_ref, e_ref, inv_ref, ctxt_ref, dctxt_ref, xt_hbm, et_hbm, ctx_hbm, *refs):
        more_ref, (keep_ref, send_ref, d_ref, stage, bias, xt, et, ctx, sems, in_sems) = refs[:extra], refs[extra:]
        t = pl.program_id(0)
        late = [pltpu.make_async_copy(a, b, in_sems.at[n]) for n, (a, b) in enumerate([(xt_hbm, xt), (et_hbm, et), (ctx_hbm.at[index], ctx)])]

        @pl.when(t == 0)
        def _():
            for copy in late:
                copy.start()

        q, k, v = qkv_ref[0, :, :HD], qkv_ref[0, :, HD : 2 * HD], qkv_ref[0, :, 2 * HD : 3 * HD]
        mine = pl.ds(t * HD, HD)
        dot = (dctxt_ref[mine, :].astype(F32) * inv_ref[0, :1, :]).astype(BF)
        delta = jnp.sum(dot.astype(F32) * ctxt_ref[0, mine, :], axis=0, keepdims=True)
        ee = e_ref[0]
        ds = (ee.astype(F32) * (nn(v, dot) - delta)).astype(BF)
        dv = nn(ee, dot.T)
        dk = nn(ds, q)
        dq = (nn(k.T, ds) * scale).T
        d = jnp.concatenate([dq, dk, dv, jnp.zeros_like(dv)], axis=1)
        bias[t] = jnp.broadcast_to(jnp.sum(d, axis=0, keepdims=True), (8, PACK))
        d_ref[:, pl.ds(pl.multiple_of(t * PACK, PACK), PACK)] = d.astype(BF)

        @pl.when(t == heads - 1)
        def _():
            for copy in late:
                copy.wait()
            go = nn(et[...], ctx[...])
            for h in range(heads):
                if h % 2 == 0:
                    both = nn(xt[...], d_ref[:, h * PACK : (h + 2) * PACK])
                g = both[:, h % 2 * PACK : (h % 2 + 1) * PACK]
                low = jnp.concatenate([g[:, : 3 * HD], go[:, h * HD : (h + 1) * HD]], axis=1).astype(BF)
                row = jnp.concatenate([bias[h]] * (EXTRA // 8), axis=0).astype(BF)
                for i in range(width // rows):
                    stage[h, i, :rows, :] = low[i * rows : (i + 1) * rows]
                    stage[h, i, rows : rows + EXTRA, :] = row
                    if extra:
                        stage[h, i, rows + EXTRA :, :] = more_ref[0][place_ref[i * heads + h]]
                blocks.stores(place_ref, h, stage.at[h], keep_ref, send_ref, sems.at[h], "start")
            for h in range(heads):
                blocks.stores(place_ref, h, stage.at[h], keep_ref, send_ref, sems.at[h], "wait")

    by_head = lambda *s: pl.BlockSpec((1, *s), lambda t, *_: (index * heads + t, 0, 0))
    high = rows + EXTRA * (1 + extra)
    out = (half, high, PACK)
    return call(
        body, (heads,), [place],
        [
            (qkv, by_head(length, PACK)), (e, by_head(length, length)), (inv, by_head(8, length)),
            (ctxt, pl.BlockSpec((1, *ctxt.shape[1:]), lambda t, *_: (index, 0, 0))), (dctxt, full(dctxt.shape)), (tokens_t, ANY), (err_t, ANY), (ctx, ANY),
            *([] if more is None else [(more, full(more.shape))]),
        ],
        [(out, BF, ANY), (out, BF, ANY), ((length, heads * PACK), BF, full((length, heads * PACK)))],
        [
            pltpu.VMEM((heads, width // rows, high, PACK), BF), pltpu.VMEM((heads, 8, PACK), F32), pltpu.VMEM((width, length), BF), pltpu.VMEM((width, length), BF), pltpu.VMEM((length, inner), BF),
            pltpu.SemaphoreType.DMA((heads, blocks.n // heads)), pltpu.SemaphoreType.DMA((3,)),
        ],
        (heads * (2 * length * width * PACK + 32 * length * length * HD), heads * length * length * 2), "attention_backward",
    )


def tokens_backward(err_one, grads, weights, devs, blocks):
    length, width = err_one.shape
    heads = blocks.tensor
    groups = len(grads)
    flat = [p for pieces, _ in weights for p in pieces]

    def body(devs_ref, err_ref, *refs):
        d_refs, piece_refs, (out_ref, w, sems) = refs[:groups], refs[groups : groups + len(flat)], refs[groups + len(flat) :]
        c = pl.program_id(0)

        @pl.when(c == 0)
        def _():
            at, copies = 0, []
            for g, (pieces, lane) in enumerate(weights):
                copies += blocks.loads(devs_ref, piece_refs[at : at + len(pieces)], w.at[g], sems.at[g], lane)
                at += len(pieces)
            for copy in copies:
                copy.start()
            for copy in copies:
                copy.wait()

        total = err_ref[...]
        for g in range(groups):
            for t in range(heads):
                total = total + nt(d_refs[g][:, t * PACK : t * PACK + 3 * HD], w[g, t][:, : 3 * HD])
        out_ref[...] = total

    chunk = min(256, length)
    rows = pl.BlockSpec((chunk, width), lambda c, *_: (c, 0))
    return call(
        body, (length // chunk,), [devs],
        [(err_one, rows)] + [(d, pl.BlockSpec((chunk, heads * PACK), lambda c, *_: (c, 0))) for d in grads] + [(p, ANY) for p in flat],
        [((length, width), F32, rows)],
        [pltpu.VMEM((groups, heads, width, PACK), BF), pltpu.SemaphoreType.DMA((groups, blocks.n))],
        (2 * groups * heads * length * width * PACK, groups * heads * width * PACK * 2 + length * width * 8), "tokens_backward",
    )[0]


def layer_norm(residual):
    centered = residual - jnp.mean(residual, axis=-1, keepdims=True)
    inverse = lax.rsqrt(jnp.mean(centered * centered, axis=-1, keepdims=True) + EPSILON)
    return centered * inverse, inverse


def norm_backward(scaled, normed, inverse):
    first = jnp.mean(scaled, axis=-1, keepdims=True)
    second = jnp.mean(scaled * normed, axis=-1, keepdims=True)
    return inverse * (scaled - first - normed * second)


def feed_loads(feed, target, sems, blocks, t, tops):
    copies = []
    for kind, top in enumerate(tops):
        for i in range(blocks.n // blocks.tensor):
            d = i * blocks.tensor + t
            copies.append(pltpu.make_async_copy(
                feed.at[d, pl.ds(top, blocks.rows), :], target.at[t, kind, pl.ds(i * blocks.rows, blocks.rows), :], sems.at[kind, d]
            ))
    return copies


def feed_forward(tokens, cotangent, contexts, outputs, vec, up_bias, feed, blocks):
    length, width = tokens.shape
    tensor = blocks.tensor
    feed, tops = feed
    part = feed.shape[-1]
    groups = len(contexts)
    chunk = min(256, length)

    def body(x_ref, vec_ref, ub_ref, *refs):
        c_refs, o_refs, refs = refs[:groups], refs[groups : 2 * groups], refs[2 * groups :]
        cot_hbm, feed_hbm, norm_hbm, inv_ref, hidt_hbm, slope_ref, out_hbm, err_hbm, low_hbm, blocks_hbm, sums_ref, *refs = refs
        w, act, hidden, norm, hidt, acc, out, err, low, errt, cot, stage, feed_sems, sems, store_sems = refs
        s = pl.program_id(0)
        cot_copy = pltpu.make_async_copy(cot_hbm, cot, sems.at[0])
        early = [pltpu.make_async_copy(a, b, sems.at[1 + n]) for n, (a, b) in enumerate([(norm, norm_hbm), (hidt, hidt_hbm)])]
        late = [pltpu.make_async_copy(a, b, sems.at[3 + n]) for n, (a, b) in enumerate([(out, out_hbm), (err, err_hbm), (low, low_hbm)])]

        @pl.when(s == 0)
        def _():
            for t in range(tensor):
                for copy in feed_loads(feed_hbm, w, feed_sems, blocks, t, tops):
                    copy.start()
            cot_copy.start()
            for c in range(0, length, chunk):
                rows = slice(c, c + chunk)
                attended = sum(nn(a[0, rows, :], b[0]) for a, b in zip(c_refs, o_refs)) + vec_ref[0:1, :]
                normed, inverse = layer_norm(x_ref[rows, :].astype(F32) + attended)
                norm[rows, :] = normed
                inv_ref[rows, :] = inverse
                first_out = normed * vec_ref[1:2, :] + vec_ref[2:3, :]
                hidden[rows, :] = first_out.astype(BF)
                hidt[:, rows] = first_out.T.astype(BF)
            for copy in early:
                copy.start()

        @pl.when(s < tensor)
        def _():
            for copy in feed_loads(feed_hbm, w, feed_sems, blocks, s, tops):
                copy.wait()
            pre = nn(hidden[...], w[s, 0]) + ub_ref[pl.ds(s, 1), :]
            phi = 0.5 * (1.0 + lax.erf(pre * (1.0 / math.sqrt(2.0))))
            act[s] = (pre * phi).astype(BF)
            density = jnp.exp(-0.5 * pre * pre) * (1.0 / math.sqrt(2.0 * math.pi))
            slope_ref[0] = (phi + pre * density).astype(BF)
            branch = nt(act[s], w[s, 1])

            @pl.when(s == 0)
            def _():
                acc[...] = branch

            @pl.when(s > 0)
            def _():
                acc[...] += branch

        @pl.when(s == tensor - 1)
        def _():
            cot_copy.wait()
            totals = jnp.zeros((8, width), F32)
            for c in range(0, length, chunk):
                rows = slice(c, c + chunk)
                first_out = norm[rows, :] * vec_ref[1:2, :] + vec_ref[2:3, :]
                normed, inverse = layer_norm(first_out + (acc[rows, :] + vec_ref[3:4, :]))
                out[rows, :] = (normed * vec_ref[4:5, :] + vec_ref[5:6, :]).astype(BF)
                upstream = cot[rows, :].astype(F32)
                error = norm_backward(upstream * vec_ref[4:5, :], normed, inverse)
                err[rows, :] = error
                low[rows, :] = error.astype(BF)
                errt[:, rows] = error.T.astype(BF)
                sums = [jnp.sum(a, axis=0, keepdims=True) for a in (error, upstream * normed, upstream)]
                totals += jnp.concatenate(sums + [jnp.zeros((5, width), F32)], axis=0)
            sums_ref[...] = totals
            for copy in late:
                copy.start()

        @pl.when(s >= tensor)
        def _():
            t = s - tensor
            slot = lax.rem(t, 2)

            @pl.when(t >= 2)
            def _():
                for copy in blocks.ordered_stores(t - 2, stage.at[slot], blocks_hbm, store_sems.at[slot]):
                    copy.wait()

            stage[slot] = nn(errt[...], act[t]).astype(BF).reshape(-1, blocks.rows, part)
            for copy in blocks.ordered_stores(t, stage.at[slot], blocks_hbm, store_sems.at[slot]):
                    copy.start()

        @pl.when(s == 2 * tensor - 1)
        def _():
            for last in range(max(tensor - 2, 0), tensor):
                for copy in blocks.ordered_stores(last, stage.at[last % 2], blocks_hbm, store_sems.at[last % 2]):
                    copy.wait()
            for copy in early + late:
                copy.wait()

    block_out = (blocks.n, blocks.rows, part)
    wide = (length, width)
    return call(
        body, (2 * tensor,), [],
        [(a, once(a.shape)) for a in (tokens, vec, up_bias)] + [at_index(a, i) for a, i in (*contexts, *outputs)] + [(cotangent, ANY), (feed, ANY)],
        [
            (wide, F32, ANY), ((length, 1), F32, once((length, 1))), ((width, length), BF, ANY),
            ((tensor, length, part), BF, pl.BlockSpec((1, length, part), lambda s, *_: (jnp.minimum(s, tensor - 1), 0, 0))),
            (wide, BF, ANY), (wide, F32, ANY), (wide, BF, ANY), (block_out, BF, ANY), ((8, width), F32, once((8, width))),
        ],
        [
            pltpu.VMEM((tensor, 2, width, part), BF), pltpu.VMEM((tensor, length, part), BF), pltpu.VMEM(wide, BF), pltpu.VMEM(wide, F32),
            pltpu.VMEM((width, length), BF), pltpu.VMEM(wide, F32), pltpu.VMEM(wide, BF), pltpu.VMEM(wide, F32), pltpu.VMEM(wide, BF),
            pltpu.VMEM((width, length), BF), pltpu.VMEM(wide, BF), pltpu.VMEM((2, width // blocks.rows, blocks.rows, part), BF),
            pltpu.SemaphoreType.DMA((2, blocks.n)), pltpu.SemaphoreType.DMA((6,)), pltpu.SemaphoreType.DMA((2, blocks.n // tensor)),
        ],
        (2 * length * width * (width + 3 * tensor * part), 30 * length * width + 4 * length * tensor * part), "feed_forward",
    )


def feed_backward(err_low, slope, hidden_t, err_two, normed_one, inverse_one, vec, outputs, feed, place, blocks):
    length, width = err_low.shape
    tensor = blocks.tensor
    feed, tops = feed
    part = feed.shape[-1]
    groups = len(outputs)
    chunk = min(256, length)
    inner = outputs[0][0].shape[1]

    def body(place_ref, e_ref, s_ref, h_ref, i1_ref, vec_ref, *refs):
        o_refs, refs = refs[:groups], refs[groups:]
        e2_hbm, n1_hbm, feed_hbm, keep, send, up_sums, err_hbm, errt_hbm, sums_ref, *refs = refs
        dctx_hbm, refs = refs[:groups], refs[groups:]
        w, acc, e2, n1, err, errt, dctx, stage, feed_sems, sems, out_sems, store_sems = refs
        t = pl.program_id(0)
        slot = lax.rem(t, 2)
        inputs = [pltpu.make_async_copy(a, b, sems.at[n]) for n, (a, b) in enumerate([(e2_hbm, e2), (n1_hbm, n1)])]

        @pl.when(t == 0)
        def _():
            for k in range(tensor):
                for copy in feed_loads(feed_hbm, w, feed_sems, blocks, k, tops[::-1]):
                    copy.start()
            for copy in inputs:
                copy.start()

        for copy in feed_loads(feed_hbm, w, feed_sems, blocks, t, tops[::-1]):
            copy.wait()
        grad = nn(e_ref[...], w[t, 0]) * s_ref[0].astype(F32)
        up_sums[pl.ds(t, 1), :] = jnp.sum(grad, axis=0, keepdims=True)
        low = grad.astype(BF)

        @pl.when(t >= 2)
        def _():
            blocks.stores(place_ref, t - 2, stage.at[slot], keep, send, store_sems.at[slot], "wait")

        stage[slot] = nn(h_ref[...], low).astype(BF).reshape(-1, blocks.rows, part)
        blocks.stores(place_ref, t, stage.at[slot], keep, send, store_sems.at[slot], "start")
        back = nt(low, w[t, 1])

        @pl.when(t == 0)
        def _():
            acc[...] = back

        @pl.when(t > 0)
        def _():
            acc[...] += back

        @pl.when(t == tensor - 1)
        def _():
            for copy in inputs:
                copy.wait()
            totals = jnp.zeros((8, width), F32)
            copies = []
            for n, c in enumerate(range(0, length, chunk)):
                rows = slice(c, c + chunk)
                err_in = e2[rows, :] + acc[rows, :]
                normed = n1[rows, :]
                error = norm_backward(err_in * vec_ref[1:2, :], normed, i1_ref[rows, :])
                err[rows, :] = error
                turned = error.T.astype(BF)
                errt[:, rows] = turned
                some = pl.ds(c, chunk)
                copies += [
                    pltpu.make_async_copy(err.at[some, :], err_hbm.at[some, :], out_sems.at[n, 0]),
                    pltpu.make_async_copy(errt.at[:, some], errt_hbm.at[:, some], out_sems.at[n, 1]),
                ]
                for g in range(groups):
                    dctx[g, :, rows] = nn(o_refs[g][0], turned).astype(BF)
                    copies.append(pltpu.make_async_copy(dctx.at[g, :, some], dctx_hbm[g].at[:, some], out_sems.at[n, 2 + g]))
                for copy in copies[-2 - groups :]:
                    copy.start()
                sums = [jnp.sum(a, axis=0, keepdims=True) for a in (error, err_in * normed, err_in)]
                totals += jnp.concatenate(sums + [jnp.zeros((5, width), F32)], axis=0)
            sums_ref[...] = totals
            for last in range(max(tensor - 2, 0), tensor):
                blocks.stores(place_ref, last, stage.at[last % 2], keep, send, store_sems.at[last % 2], "wait")
            for copy in copies:
                copy.wait()

    block_out = (blocks.n // 2, blocks.rows, part)
    wide = (length, width)
    return call(
        body, (tensor,), [place],
        [
            (err_low, once(wide)), (slope, pl.BlockSpec((1, length, part), lambda t, *_: (t, 0, 0))), (hidden_t, once((width, length))),
            (inverse_one, once((length, 1))), (vec, once(vec.shape)), *[at_index(o, i) for o, i in outputs],
            (err_two, ANY), (normed_one, ANY), (feed, ANY),
        ],
        [
            (block_out, BF, ANY), (block_out, BF, ANY), ((8, part), F32, once((8, part))), (wide, F32, ANY), ((width, length), BF, ANY),
            ((8, width), F32, once((8, width))), *[((inner, length), BF, ANY) for _ in outputs],
        ],
        [
            pltpu.VMEM((tensor, 2, width, part), BF), pltpu.VMEM(wide, F32), pltpu.VMEM(wide, F32), pltpu.VMEM(wide, F32), pltpu.VMEM(wide, F32),
            pltpu.VMEM((width, length), BF), pltpu.VMEM((groups, inner, length), BF), pltpu.VMEM((2, width // blocks.rows, blocks.rows, part), BF),
            pltpu.SemaphoreType.DMA((2, blocks.n)), pltpu.SemaphoreType.DMA((2,)), pltpu.SemaphoreType.DMA((length // chunk, 2 + groups)),
            pltpu.SemaphoreType.DMA((2, blocks.n // tensor)),
        ],
        (2 * length * width * (width + 3 * tensor * part), 30 * length * width + 2 * length * tensor * part), "feed_backward",
    )


def local(
    tokens, query_weight, key_weight, value_weight, output_weight, query_bias, value_bias,
    output_bias, first_gain, first_shift, up_weight, up_bias, down_weight, down_bias,
    second_gain, second_shift, cotangent,
):
    dp, tensor = lax.axis_size("dp"), lax.axis_size("tensor")
    count = dp * tensor
    rows = query_weight.shape[0]
    width = rows * dp
    groups = query_weight.shape[1] // HD
    heads = groups * tensor
    slot = output_bias.shape[0]
    cols = query_bias.shape[1]
    me = lax.axis_index(AXES)
    place, devs = position_table(me, count), device_table(me, count)
    direct = rows % 16 == 0

    vectors = jnp.stack([output_bias, first_gain, first_shift, down_bias, second_gain, second_shift])
    extra = small_block(vectors, query_bias, value_bias, up_bias)
    output_turned = output_weight.T
    by_group = [
        jnp.concatenate([w[:, c * HD : (c + 1) * HD] for w in (query_weight, key_weight, value_weight, output_turned)], axis=1)
        for c in range(groups)
    ]
    first, second = (Gathering(jnp.concatenate(blocks, axis=axis), count) for blocks, axis in (([by_group[0], extra], 0), (by_group[1:], 1)))
    feed = lax.all_gather(jnp.concatenate([up_weight, down_weight.T], axis=0), AXES, axis=0, tiled=False)
    tokens_t, place, devs = wave([first], tokens.T, place, devs)
    wave([first, second])
    wave([first])
    direct = rows % 16 == 0
    extras = jnp.concatenate([p[:, rows:] for p in first.pieces], axis=0)
    if direct:
        blocks = Blocks(count, rows, tensor)
        block_place, block_devs = place, devs
    else:
        blocks = Blocks(tensor, width, tensor)
        block_place = block_devs = jnp.arange(tensor, dtype=jnp.int32)

    def by_matrix(ordered):
        return [ordered.reshape(dp, tensor, rows, -1).transpose(1, 0, 2, 3).reshape(tensor, width, -1)]

    def ready(gathering):
        if direct:
            return gathering.pieces
        return by_matrix(jnp.take(jnp.concatenate(gathering.pieces, axis=0)[:, :rows], place, axis=0))

    def scattering(keep, send, more=None):
        if not direct:
            stacked = jnp.concatenate([keep, send], axis=0)
            parts = [stacked[:, :width].reshape(tensor, dp, rows, -1).transpose(1, 0, 2, 3).reshape(count, rows, -1)]
            if stacked.shape[1] > width:
                parts.append(jnp.tile(stacked[:, width:], (dp, 1, 1)))
            stacked = jnp.take(jnp.concatenate(parts, axis=1), devs, axis=0)
            if more is not None:
                stacked = jnp.concatenate([stacked, more], axis=1)
            keep, send = stacked[: count // 2], stacked[count // 2 :]
        return Scattering(keep, send, count)

    def summed(stacked):
        if not direct:
            stacked = stacked.reshape(tensor, dp, rows, -1).transpose(1, 0, 2, 3).reshape(count, rows, -1)
        return lax.psum_scatter(stacked.reshape(count * rows, -1), AXES, scatter_dimension=0, tiled=True).astype(F32)

    tokens_now, extras = wave([second], tokens, extras)
    vec, bias_rows, up_rows = unpack_small(extras, devs.reshape(count, 1), slot, cols, width, tensor)
    bias_heads = bias_rows[:2].reshape(2, tensor, groups, HD).transpose(2, 1, 0, 3)
    bias_pack = jnp.concatenate(
        [bias_heads[:, :, 0], jnp.zeros_like(bias_heads[:, :, 0]), bias_heads[:, :, 1], jnp.zeros_like(bias_heads[:, :, 0])], axis=-1
    )
    first_set = ready(first)
    one = attention_forward(tokens_now, first_set, bias_pack[:1], block_devs, blocks)
    tokens_now = wave([second], tokens, one[4])[0]
    second_set = ready(second)
    others = attention_forward(tokens_now, second_set, bias_pack[1:], block_devs, blocks)
    weights = [(first_set, 0)] + [(second_set, c * PACK) for c in range(groups - 1)]
    forward = [(one, 0)] + [(others, c) for c in range(groups - 1)]
    if not direct:
        feed = jnp.concatenate([by_matrix(feed[:, :rows])[0], by_matrix(feed[:, rows:])[0]], axis=1)
    feed = (feed, (0, feed.shape[1] // 2))
    outputs = [(f[5], i) for f, i in forward]
    normed_one, inverse_one, hidden_t, slope, layer_out, err_two, err_two_low, down_blocks, sums_two = feed_forward(
        tokens, cotangent, [(f[2], i) for f, i in forward], outputs, vec, up_rows, feed, blocks
    )
    grad_down = summed(down_blocks)
    up_keep, up_send, up_sums, err_one, err_one_t, sums_one, *context_grads = feed_backward(
        err_two_low, slope, hidden_t, err_two, normed_one, inverse_one, vec, outputs, feed, block_place, blocks
    )
    grad_up = scattering(up_keep, up_send)
    vec_grads = jnp.concatenate([sums_one[:3], sums_two[:3], jnp.zeros((2, width), F32)], axis=0)
    small = pack_small_grads(vec_grads, up_sums, devs.reshape(count, 1), slot, cols, tensor)
    backward, scatters = [None] * groups, [None] * groups
    last = (err_one_t,)
    for c in reversed(range(groups)):
        carries = c == groups - 1
        moving = [m for m in scatters[c + 1 : c + 3] if m] + ([grad_up] if c else [])
        backward[c] = attention_backward(
            tokens_t, err_one_t, *forward[c], wave(moving, context_grads[c], since=last), block_place, blocks, small if direct and carries else None
        )
        last = (backward[c][2],)
        scatters[c] = scattering(*backward[c][:2], small if carries else None)
    wave(scatters[:1])
    wave([*scatters[1:], grad_up], since=last)
    err_now = wave(scatters[:1], err_one)
    grad_tokens = tokens_backward(err_now, [b[2] for b in backward], weights, block_devs, blocks)
    wave(scatters[:2])
    while any(m.phases for m in scatters):
        wave(scatters)
    grad_up = grad_up.result()
    results = [m.result() for m in scatters]
    packed = [r[:rows] for r in results]
    tail = results[-1][rows + EXTRA :]
    bias_rows = jnp.stack([r[rows] for r in results])
    column = lax.axis_index("dp") * cols
    bias_out = [lax.dynamic_slice(bias_rows, (0, start + column), (groups, cols)) for start in (0, 2 * HD)]
    out = jnp.stack(packed, axis=1).reshape(rows, groups, 4, HD)
    out_query, out_key, out_value, out_output = (out[:, :, i].reshape(rows, groups * HD) for i in range(4))
    vecs = [tail[v // 2, (v % 2) * LANES : (v % 2) * LANES + slot] for v in range(6)]
    return (
        layer_out,
        grad_tokens,
        out_query,
        out_key,
        out_value,
        out_output.T,
        bias_out[0],
        bias_out[1],
        vecs[0],
        vecs[1],
        vecs[2],
        grad_up,
        tail[: up_bias.shape[0], 64 : 64 + cols],
        grad_down.T,
        vecs[3],
        vecs[4],
        vecs[5],
    )


def solution(mesh):
    both, cross, turned, vector = P(AXES, None), P("dp", "tensor"), P("tensor", "dp"), P(AXES)
    return jax.shard_map(
        local,
        mesh=mesh,
        in_specs=(
            both, cross, cross, cross, turned, turned, turned, vector, vector, vector,
            cross, turned, turned, vector, vector, vector, both,
        ),
        out_specs=(
            both, both, cross, cross, cross, turned, turned, turned, vector, vector, vector,
            cross, turned, turned, vector, vector, vector,
        ),
        check_vma=False,
    )
```

```python
import functools
import math

import jax
import jax.numpy as jnp
import numpy as np
from jax import lax
from jax.experimental import pallas as pl
from jax.experimental.pallas import tpu as pltpu
from jax.sharding import PartitionSpec as P

HD = 64
L = 1024
PACK = 4 * HD
EPSILON = 1e-12
AXES = ("dp", "tensor")
EXTRA = 16
LANES = 128
BF = jnp.bfloat16
F32 = jnp.float32
SDS = jax.ShapeDtypeStruct
ANY = pl.BlockSpec(memory_space=pl.ANY)


def nn(a, b):
    return lax.dot_general(a, b, (((1,), (0,)), ((), ())), preferred_element_type=F32)


def nt(a, b):
    return lax.dot_general(a, b, (((1,), (1,)), ((), ())), preferred_element_type=F32)


def full(shape):
    return pl.BlockSpec(shape, lambda *_: (0,) * len(shape))


def once(shape):
    return pl.BlockSpec(shape, lambda *_: (0,) * len(shape), pipeline_mode=pl.Buffered(1))


def at_index(array, i):
    shape = (1, *array.shape[1:])
    return array, pl.BlockSpec(shape, lambda *_: (i,) + (0,) * (len(shape) - 1), pipeline_mode=pl.Buffered(1))


def call(body, grid, tables, ins, outs, scratch, cost, name, aliases={}):
    flops, moved = cost
    return pl.pallas_call(
        body,
        grid_spec=pltpu.PrefetchScalarGridSpec(
            num_scalar_prefetch=len(tables),
            grid=grid,
            in_specs=[s for _, s in ins],
            out_specs=[s for _, _, s in outs],
            scratch_shapes=scratch,
        ),
        out_shape=[SDS(s, d) for s, d, _ in outs],
        compiler_params=pltpu.CompilerParams(
            dimension_semantics=("arbitrary",) * len(grid), vmem_limit_bytes=60 * 2**20
        ),
        cost_estimate=pl.CostEstimate(flops=int(flops * 0.01), bytes_accessed=int(moved * 0.01), transcendentals=0),
        name=name,
        input_output_aliases=aliases,
    )(*tables, *[a for a, _ in ins])


def exchange(array, differs, count):
    even, odd = differs if isinstance(differs, tuple) else (differs, differs)
    return lax.ppermute(array, AXES, [(d, d ^ (odd if d & 1 else even)) for d in range(count)])


def phases_of(count):
    bits = count.bit_length() - 1
    return [*((k, 1) for k in range(bits - 1, 4, -1)), (3, 2), (1, 2), (0, 1)]


def scatter_phases_of(count):
    bits = count.bit_length() - 1
    return [[1], [(2, 4)], [(4, 2)], [8, 16, 24], *([1 << k] for k in range(5, bits))]


class Gathering:
    def __init__(self, block, count):
        self.pieces, self.count, self.phases = [block[None]], count, phases_of(count)
        while self.phases[0][1] == 1:
            self.move(self.outgoing())

    def outgoing(self):
        if self.phases[0] != (0, 1) and len(self.pieces) > 1:
            self.pieces = [jnp.concatenate(self.pieces, axis=0)]
        return self.pieces

    def move(self, pieces):
        low, bits = self.phases.pop(0)
        self.pieces = self.pieces + [exchange(p, k << low, self.count) for k in range(1, 1 << bits) for p in pieces]


class Scattering:
    def __init__(self, keep, send, count):
        self.terms, self.sends, self.count, self.phases = [keep], [send], count, scatter_phases_of(count)
        self.size = keep.shape[0]

    def looked_at(self, *since):
        self.terms = lax.optimization_barrier((self.terms, since))[0]

    def outgoing(self):
        if self.sends is None:
            parts = 1 + len(self.phases[0])
            size = self.size // parts
            self.sends = [sum(t[k * size : (k + 1) * size].astype(F32) for t in self.terms).astype(BF) for k in range(1, parts)]
            self.size = size
        return self.sends

    def move(self, sends):
        self.terms = self.terms + [exchange(p, k, self.count) for k, p in zip(self.phases.pop(0), sends)]
        self.sends = None

    def result(self):
        return sum(t[0].astype(F32) for t in self.terms)


def wave(moves, *beside, since=()):
    moves = [m for m in moves if m.phases]
    for m in moves:
        if since and isinstance(m, Scattering):
            m.looked_at(*since)
    outgoing, beside = lax.optimization_barrier(([m.outgoing() for m in moves], beside))
    for m, array in zip(moves, outgoing):
        m.move(array)
    return beside[0] if len(beside) == 1 else beside


def fields_of(count):
    top, fields = count.bit_length() - 1, []
    for low, bits in phases_of(count)[::-1]:
        top -= bits
        fields.append((low, bits, top))
    return fields


def position_table(me, count):
    bits = count.bit_length() - 1
    device = jnp.arange(count, dtype=jnp.int32)
    differs = device ^ me
    one, two = (differs >> 1) & 1, (differs >> 2) & 1
    odd = (device & 1) == 1
    place = ((differs & 1) << (bits - 1)) | (jnp.where(odd, two, one) << (bits - 2)) | (jnp.where(odd, one, two) << (bits - 3))
    place = place | (((differs >> 3) & 3) << (bits - 5))
    for k in range(5, bits):
        place = place | (((differs >> k) & 1) << (bits - 1 - k))
    return place


def owner_table(me, count):
    bits = count.bit_length() - 1
    place = jnp.arange(count, dtype=jnp.int32)
    core, upper, lower = ((place >> (bits - k)) & 1 for k in (1, 2, 3))
    odd = ((me ^ core) & 1) == 1
    differs = core | (jnp.where(odd, lower, upper) << 1) | (jnp.where(odd, upper, lower) << 2) | (((place >> (bits - 5)) & 3) << 3)
    for k in range(5, bits):
        differs = differs | (((place >> (bits - 1 - k)) & 1) << k)
    return differs ^ me


def gathered_place(me, count):
    differs = jnp.arange(count, dtype=jnp.int32) ^ me
    return sum(((differs >> low) & ((1 << bits) - 1)) << at for low, bits, at in fields_of(count))


def device_table(me, count):
    place = jnp.arange(count, dtype=jnp.int32)
    return sum(((place >> at) & ((1 << bits) - 1)) << low for low, bits, at in fields_of(count)) ^ me


class Blocks:
    def __init__(self, n, rows, tensor):
        self.n, self.rows, self.tensor = n, rows, tensor

    def at(self, d):
        return lax.rem(d, self.tensor), pl.multiple_of(lax.div(d, self.tensor) * self.rows, self.rows)

    def loads(self, devs, pieces, target, sems, lane=0, top=0):
        out, p = [], 0
        flat = len(target.shape) == 2
        width = target.shape[-1] // (self.tensor if flat else 1)
        for piece in pieces:
            for j in range(piece.shape[0]):
                t, row = self.at(devs[p])
                rows = pl.ds(row, self.rows)
                into = target.at[rows, pl.ds(pl.multiple_of(t * width, width), width)] if flat else target.at[t, rows, :]
                out.append(pltpu.make_async_copy(
                    piece.at[j, pl.ds(top, self.rows), pl.ds(lane, width)], into, sems.at[p]
                ))
                p += 1
        return out

    def stores(self, place, t, stage, keep, send, sems, action, lane=0):
        half = self.n // 2
        lanes = pl.ds(lane, stage.shape[-1])
        for i in range(self.n // self.tensor):
            p = place[i * self.tensor + t]
            kept = pltpu.make_async_copy(stage.at[i], keep.at[lax.rem(p, half), :, lanes], sems.at[i])
            if action == "wait":
                kept.wait()
            else:
                sent = pltpu.make_async_copy(stage.at[i], send.at[lax.rem(p, half), :, lanes], sems.at[i])
                pl.when(p < half)(kept.start)
                pl.when(p >= half)(sent.start)


def spread_constants(slot, cols, width):
    lane = np.arange(width)
    a, c = np.zeros((LANES, width), np.float32), np.zeros((LANES, width), np.float32)
    for j in range(slot):
        a[j] = lane % slot == j
    for j in range(cols):
        a[32 + j] = lane % cols == j
        c[64 + j] = lane % cols == j
    return jnp.asarray(a, BF), jnp.asarray(c, BF)


def small_masks(device, slot, cols, width, tensor):
    n = device.shape[0]
    shift = tensor.bit_length() - 1
    row = lax.broadcasted_iota(jnp.int32, (n, EXTRA, width), 1)
    lane = lax.broadcasted_iota(jnp.int32, (n, EXTRA, width), 2)
    i, t = device >> shift, device & (tensor - 1)
    in_head = (lane & (HD - 1)) >> (cols.bit_length() - 1)
    groups = width // HD // tensor
    vector = (row < 9) & (lane >= device * slot) & (lane < (device + 1) * slot)
    bias = (row >= 9) & (row < 9 + groups) & ((lane >> 6) == t * groups + row - 9) & (in_head == i)
    hidden = (row < width // HD) & ((lane >> 6) == row) & (in_head == i)
    return vector | bias, hidden, t


def unpack_small(pieces, top, device, slot, cols, width, tensor):
    n = device.shape[0]
    groups = width // HD // tensor
    spread_a, spread_c = spread_constants(slot, cols, width)

    def body(d_ref, a_ref, c_ref, *refs):
        piece_refs, (vec_ref, bias_ref, up_ref, x_s, sems) = refs[: len(pieces)], refs[len(pieces) :]
        copies, at = [], 0
        for j, piece in enumerate(piece_refs):
            size = piece.shape[0]
            copies.append(pltpu.make_async_copy(piece.at[:, pl.ds(top, EXTRA), :], x_s.at[pl.ds(at, size)], sems.at[j]))
            at += size
        for copy in copies:
            copy.start()
        d = d_ref[...].reshape(n, 1, 1)
        main, hidden, t = small_masks(d, slot, cols, width, tensor)
        for copy in copies:
            copy.wait()
        x = x_s[...].reshape(n * EXTRA, 2 * LANES)
        bias_ref[...] = jnp.zeros_like(bias_ref)
        for half in range(2):
            y = nn(x[:, half * LANES : (half + 1) * LANES], a_ref[...]).reshape(n, EXTRA, width)
            total = jnp.sum(jnp.where(main, y, 0.0), axis=0)
            for v in range(half, 6, 2):
                r = v // 2
                vec_ref[v : v + 1, :] = total[r : r + 1] + total[3 + r : 4 + r] + total[6 + r : 7 + r]
            row = jnp.sum(total[9:EXTRA], axis=0, keepdims=True)
            for head in range(groups * tensor):
                at = half * 2 * HD
                bias_ref[head % groups, head // groups : head // groups + 1, at : at + HD] = row[:, head * HD : (head + 1) * HD]
        y = nn(x[:, :LANES], c_ref[...]).reshape(n, EXTRA, width)
        y = jnp.where(hidden, y, 0.0)
        for k in range(tensor):
            picked = jnp.sum(jnp.where(t == k, y, 0.0), axis=0)
            up_ref[k : k + 1, :] = jnp.sum(picked, axis=0, keepdims=True)

    row8, bias = (8, width), (groups, tensor, PACK)
    return call(
        body, (1,), [],
        [(a, full(a.shape)) for a in (device, spread_a, spread_c)] + [(p, ANY) for p in pieces],
        [(row8, F32, full(row8)), (bias, F32, full(bias)), (row8, F32, full(row8))],
        [pltpu.VMEM((n, EXTRA, PACK), BF), pltpu.SemaphoreType.DMA((len(pieces),))],
        (3 * 2 * n * EXTRA * LANES * width, n * EXTRA * PACK * 2), "unpack_small",
    )


def pack_small_grads(one, two, up, device, slot, cols, tensor):
    n, width = device.shape[0], one.shape[-1]
    spread_a, spread_c = spread_constants(slot, cols, width)

    def body(one_ref, two_ref, u_ref, d_ref, a_ref, c_ref, out_ref):
        d = d_ref[...].reshape(n, 1, 1)
        main, hidden, t = small_masks(d, slot, cols, width, tensor)
        row = lax.broadcasted_iota(jnp.int32, (EXTRA, width), 0)
        halves = []
        for half in range(2):
            z = jnp.zeros((EXTRA, width), F32)
            for v in range(half, 6, 2):
                z = jnp.where(row == v // 2, (one_ref, two_ref)[v // 3][v % 3 : v % 3 + 1, :], z)
            spread = jnp.where(main, z[None], 0.0).astype(BF).reshape(n * EXTRA, width)
            halves.append(nt(spread, a_ref[...]))
        z = jnp.zeros((n, EXTRA, width), F32)
        for k in range(tensor):
            z = jnp.where(t == k, u_ref[k : k + 1, :].reshape(1, 1, width), z)
        spread = jnp.where(hidden, z, 0.0).astype(BF).reshape(n * EXTRA, width)
        halves[0] = halves[0] + nt(spread, c_ref[...])
        out_ref[...] = jnp.concatenate(halves, axis=1).astype(BF).reshape(n, EXTRA, 2 * LANES)

    shape = (n, EXTRA, PACK)
    return call(
        body, (1,), [],
        [(a, full(a.shape)) for a in (one, two, up, device, spread_a, spread_c)],
        [(shape, BF, full(shape))], [], (3 * 2 * n * EXTRA * LANES * width, 2 * n * EXTRA * PACK), "pack_small",
    )[0]


def three_parts(vector):
    high = lax.reduce_precision(vector, 8, 7)
    middle = lax.reduce_precision(vector - high, 8, 7)
    lowest = lax.reduce_precision(vector - high - middle, 8, 7)
    return jnp.stack([high, middle, lowest]).astype(BF)


def small_block(vectors, query_bias, value_bias, up_bias):
    slot = vectors.shape[1]
    parts = three_parts(vectors).reshape(9, 2, slot)

    def placed(array, row, lane):
        return jnp.pad(array, ((row, EXTRA - row - array.shape[0]), (lane, PACK - lane - array.shape[1])))

    return (
        placed(parts[:, 0], 0, 0) + placed(parts[:, 1], 0, LANES) + placed(query_bias, 9, 32)
        + placed(value_bias, 9, LANES + 32) + placed(up_bias, 0, 64)
    )


def attention_forward(tokens, pieces, bias, base, devs, blocks):
    length, width = tokens.shape
    heads = blocks.tensor
    inner = heads * HD
    groups = pieces[0].shape[-1] // PACK

    def body(devs_ref, x_ref, b_ref, *refs):
        piece_refs, (qkv_ref, e_ref, ctx_ref, ctxt_ref, inv_ref, ot_ref, w, ot_s, vt_s, sems) = refs[: len(pieces)], refs[len(pieces) :]
        c, t = pl.program_id(0), pl.program_id(1)

        loads = [blocks.loads(devs_ref, piece_refs, w.at[g], sems.at[g], g * PACK) for g in range(groups)]

        @pl.when((c == 0) & (t == 0))
        def _():
            for copies in loads:
                for copy in copies:
                    copy.start()
            vt_s[HD:, :] = jnp.ones((HD, length), BF)

        for g in range(groups):
            @pl.when((c == g) & (t == 0))
            def _():
                for copy in loads[g]:
                    copy.wait()

        wt = w[c, t]
        col = lax.broadcasted_iota(jnp.int32, (1, PACK), 1)
        pre = nn(x_ref[...], wt) + b_ref[base + c, pl.ds(t, 1), :]
        low = (pre * jnp.where(col < HD, 1.0 / math.sqrt(HD), 1.0)).astype(BF)
        qkv_ref[0] = low
        q, k = low[:, :HD], low[:, HD : 2 * HD]
        vt_s[:HD, :] = low[:, 2 * HD :].T[:HD]
        square = pre[:, : 2 * HD] * pre[:, : 2 * HD]
        pick = lax.broadcasted_iota(jnp.int32, (2 * HD, LANES), 0) // HD == lax.broadcasted_iota(jnp.int32, (2 * HD, LANES), 1)
        norms = jnp.max(nn(square.astype(BF), pick.astype(BF)), axis=0, keepdims=True)
        bound = jnp.sqrt(norms[0, 0] * norms[0, 1]) * (1.1 / math.sqrt(HD))

        @pl.when(bound <= 40.0)
        def _():
            e_ref[0] = jnp.exp(nt(k, q)).astype(BF)

        @pl.when(jnp.logical_not(bound <= 40.0))
        def _():
            def some(j, _):
                at = pl.ds(pl.multiple_of(j * LANES, LANES), LANES)
                scores = nt(k, qkv_ref[0, at, :][:, :HD])
                e_ref[0, :, at] = jnp.exp(scores - jnp.max(scores, axis=0, keepdims=True)).astype(BF)
                return 0

            lax.fori_loop(0, length // LANES, some, 0)

        mixed = nn(vt_s[...], e_ref[0])
        inv = 1.0 / mixed[HD : HD + 1]
        inv_ref[0] = jnp.broadcast_to(inv, (8, length))
        ctxt_ref[0, pl.ds(t * HD, HD), :] = mixed[:HD] * inv
        ot_s[pl.ds(t * HD, HD), :] = wt[:, 2 * HD :].T[HD:].astype(F32)

        @pl.when(t == heads - 1)
        def _():
            ctx_ref[0] = ctxt_ref[0].T.astype(BF)
            ot_ref[0] = ot_s[...].astype(BF)

    by_head = lambda *s: pl.BlockSpec((1, *s), lambda c, t, *_: (c * heads + t, 0, 0))
    by_group = lambda *s: pl.BlockSpec((1, *s), lambda c, t, *_: (c, 0, 0))
    return call(
        body, (groups, heads), [devs],
        [(tokens, full(tokens.shape)), (bias, full(bias.shape))] + [(p, ANY) for p in pieces],
        [
            ((groups * heads, length, PACK), BF, by_head(length, PACK)),
            ((groups * heads, length, length), BF, by_head(length, length)),
            ((groups, length, inner), BF, by_group(length, inner)),
            ((groups, inner, length), F32, by_group(inner, length)),
            ((groups * heads, 8, length), F32, by_head(8, length)),
            ((groups, inner, width), BF, by_group(inner, width)),
        ],
        [pltpu.VMEM((groups, heads, width, PACK), BF), pltpu.VMEM((inner, width), F32), pltpu.VMEM((2 * HD, length), BF), pltpu.SemaphoreType.DMA((groups, blocks.n))],
        (groups * heads * (2 * length * width * PACK + 16 * length * length * HD), groups * heads * length * length * 2), "attention_forward",
    )


def attention_backward(tokens_t, err_t, forward, index, dctxt, total, weights, place, devs, blocks, more=None, into=None, lane=0, high=None, wide=PACK):
    width, length = tokens_t.shape
    pieces, piece_lane = weights
    chunk = min(256, length)
    qkv, e, ctx, ctxt, inv, _ = forward
    heads = blocks.tensor
    inner = heads * HD
    half = blocks.n // 2
    scale = 1.0 / math.sqrt(HD)
    rows, extra, given = blocks.rows, 0 if more is None else 1, 0 if into is None else 2
    high = high or blocks.rows + EXTRA
    tall = rows + EXTRA * (1 + extra)

    def body(place_ref, devs_ref, qkv_ref, e_ref, inv_ref, ctxt_ref, dctxt_ref, xt_hbm, et_hbm, ctx_hbm, total_hbm, *refs):
        piece_refs, refs = refs[: len(pieces)], refs[len(pieces) :]
        more_ref, (keep_ref, send_ref, out_hbm, stage, bias, xt, et, ctx, d_ref, sum_s, w, sems, in_sems, w_sems, out_sems) = refs[:extra], refs[extra + given :]
        keep_rows, send_rows = (r.at[:, pl.ds(0, tall), :] for r in (keep_ref, send_ref))
        t = pl.program_id(0)
        late = [pltpu.make_async_copy(a, b, in_sems.at[n]) for n, (a, b) in enumerate([(xt_hbm, xt), (et_hbm, et), (ctx_hbm.at[index], ctx), (total_hbm, sum_s)])]
        late += blocks.loads(devs_ref, piece_refs, w, w_sems, piece_lane)

        @pl.when(t == 0)
        def _():
            for copy in late:
                copy.start()

        q, k, v = qkv_ref[0, :, :HD], qkv_ref[0, :, HD : 2 * HD], qkv_ref[0, :, 2 * HD : 3 * HD]
        mine = pl.ds(t * HD, HD)
        dot = (dctxt_ref[mine, :].astype(F32) * inv_ref[0, :1, :]).astype(BF)
        delta = jnp.sum(dot.astype(F32) * ctxt_ref[0, mine, :], axis=0, keepdims=True)
        ee = e_ref[0]
        ds = (ee.astype(F32) * (nn(v, dot) - delta)).astype(BF)
        dv = nn(ee, dot.T)
        dk = nn(ds, q)
        dq = (nn(k.T, ds) * scale).T
        d = jnp.concatenate([dq, dk, dv, jnp.zeros_like(dv)], axis=1)
        bias[t] = jnp.broadcast_to(jnp.sum(d, axis=0, keepdims=True), (8, PACK))
        d_ref[:, pl.ds(pl.multiple_of(t * PACK, PACK), PACK)] = d.astype(BF)

        @pl.when(t == heads - 1)
        def _():
            for copy in late:
                copy.wait()
            outs = []
            for n, c in enumerate(range(0, length, chunk)):
                sum_s[c : c + chunk, :] += nt(d_ref[c : c + chunk, :], w[...])
                outs.append(pltpu.make_async_copy(sum_s.at[pl.ds(c, chunk), :], out_hbm.at[pl.ds(c, chunk), :], out_sems.at[n]))
                outs[-1].start()
            go = nn(et[...], ctx[...])
            for h in range(heads):
                if h % 2 == 0:
                    both = nn(xt[...], d_ref[:, h * PACK : (h + 2) * PACK])
                g = both[:, h % 2 * PACK : (h % 2 + 1) * PACK]
                low = jnp.concatenate([g[:, : 3 * HD], go[:, h * HD : (h + 1) * HD]], axis=1).astype(BF)
                row = jnp.concatenate([bias[h]] * (EXTRA // 8), axis=0).astype(BF)
                for i in range(width // rows):
                    stage[h, i, :rows, :] = low[i * rows : (i + 1) * rows]
                    stage[h, i, rows : rows + EXTRA, :] = row
                    if extra:
                        stage[h, i, rows + EXTRA :, :] = more_ref[0][place_ref[i * heads + h]]
                blocks.stores(place_ref, h, stage.at[h], keep_rows, send_rows, sems.at[h], "start", lane)
            for h in range(heads):
                blocks.stores(place_ref, h, stage.at[h], keep_rows, send_rows, sems.at[h], "wait", lane)
            for copy in outs:
                copy.wait()

    by_head = lambda *s: pl.BlockSpec((1, *s), lambda t, *_: (index * heads + t, 0, 0))
    out = (half, high, wide)
    return call(
        body, (heads,), [place, devs],
        [
            (qkv, by_head(length, PACK)), (e, by_head(length, length)), (inv, by_head(8, length)),
            (ctxt, pl.BlockSpec((1, *ctxt.shape[1:]), lambda t, *_: (index, 0, 0))), (dctxt, full(dctxt.shape)), (tokens_t, ANY), (err_t, ANY), (ctx, ANY), (total, ANY), *((p, ANY) for p in pieces),
            *([] if more is None else [(more, full(more.shape))]), *((a, ANY) for a in into or ()),
        ],
        [(out, BF, ANY), (out, BF, ANY), ((length, width), F32, ANY)],
        [
            pltpu.VMEM((heads, width // rows, tall, PACK), BF), pltpu.VMEM((heads, 8, PACK), F32), pltpu.VMEM((width, length), BF), pltpu.VMEM((width, length), BF), pltpu.VMEM((length, inner), BF),
            pltpu.VMEM((length, heads * PACK), BF), pltpu.VMEM((length, width), F32), pltpu.VMEM((width, heads * PACK), BF),
            pltpu.SemaphoreType.DMA((heads, blocks.n // heads)), pltpu.SemaphoreType.DMA((4,)), pltpu.SemaphoreType.DMA((blocks.n,)),
            pltpu.SemaphoreType.DMA((length // chunk,)),
        ],
        (heads * (2 * length * width * PACK + 32 * length * length * HD), heads * length * length * 2), "attention_backward",
        {11 + len(pieces) + extra: 0, 12 + len(pieces) + extra: 1} if given else {},
    )


def layer_norm(residual):
    centered = residual - jnp.mean(residual, axis=-1, keepdims=True)
    inverse = lax.rsqrt(jnp.mean(centered * centered, axis=-1, keepdims=True) + EPSILON)
    return centered * inverse, inverse


def norm_backward(scaled, normed, inverse):
    first = jnp.mean(scaled, axis=-1, keepdims=True)
    second = jnp.mean(scaled * normed, axis=-1, keepdims=True)
    return inverse * (scaled - first - normed * second)


def feed_loads(feed, target, sems, blocks, t, tops):
    copies = []
    for kind, top in enumerate(tops):
        for i in range(blocks.n // blocks.tensor):
            d = i * blocks.tensor + t
            copies.append(pltpu.make_async_copy(
                feed.at[d, pl.ds(top, blocks.rows), :], target.at[t, kind, pl.ds(i * blocks.rows, blocks.rows), :], sems.at[kind, d]
            ))
    return copies


def feed_forward(tokens, cotangent, contexts, outputs, vec, up_bias, feed, place, blocks):
    length, width = tokens.shape
    tensor = blocks.tensor
    feed, tops = feed
    part = feed.shape[-1]
    groups = len(contexts)
    chunk = min(256, length)

    def body(place_ref, x_ref, vec_ref, ub_ref, *refs):
        c_refs, o_refs, refs = refs[:groups], refs[groups : 2 * groups], refs[2 * groups :]
        cot_hbm, feed_hbm, norm_hbm, inv_ref, hidt_hbm, slope_ref, out_hbm, low_hbm, keep, send, sums_ref, *refs = refs
        w, act, hidden, norm, hidt, acc, out, norm_low, low, errt, cot, stage, feed_sems, sems, store_sems = refs
        s = pl.program_id(0)
        cot_copy = pltpu.make_async_copy(cot_hbm, cot, sems.at[0])
        early = [pltpu.make_async_copy(a, b, sems.at[1 + n]) for n, (a, b) in enumerate([(norm_low, norm_hbm), (hidt, hidt_hbm)])]
        late = [pltpu.make_async_copy(a, b, sems.at[3 + n]) for n, (a, b) in enumerate([(out, out_hbm), (low, low_hbm)])]

        @pl.when(s == 0)
        def _():
            acc[...] = jnp.zeros_like(acc)
            for t in range(tensor):
                for copy in feed_loads(feed_hbm, w, feed_sems, blocks, t, tops):
                    copy.start()
            cot_copy.start()
            for c in range(0, length, chunk):
                rows = slice(c, c + chunk)
                attended = sum(nn(a[0, rows, :], b[0]) for a, b in zip(c_refs, o_refs)) + vec_ref[0:1, :]
                normed, inverse = layer_norm(x_ref[rows, :].astype(F32) + attended)
                norm[rows, :] = normed
                norm_low[rows, :] = normed.astype(BF)
                inv_ref[rows, :] = inverse
                first_out = normed * vec_ref[1:2, :] + vec_ref[2:3, :]
                hidden[rows, :] = first_out.astype(BF)
                hidt[:, rows] = first_out.T.astype(BF)
            for copy in early:
                copy.start()

        @pl.when(s < tensor)
        def _():
            for copy in feed_loads(feed_hbm, w, feed_sems, blocks, s, tops):
                copy.wait()
            rows_of = [slice(r, r + chunk) for r in range(0, length, chunk)]
            pre = nn(hidden[rows_of[0], :], w[s, 0])
            for n, rows in enumerate(rows_of):
                following = nn(hidden[rows_of[n + 1], :], w[s, 0]) if n + 1 < len(rows_of) else None
                pre = pre + ub_ref[pl.ds(s, 1), :]
                phi = 0.5 * (1.0 + lax.erf(pre * (1.0 / math.sqrt(2.0))))
                some = (pre * phi).astype(BF)
                act[s, rows, :] = some
                density = jnp.exp(-0.5 * pre * pre) * (1.0 / math.sqrt(2.0 * math.pi))
                slope_ref[0, rows, :] = (phi + pre * density).astype(BF)
                branch = nt(some, w[s, 1])
                acc[rows, :] += branch
                pre = following

        @pl.when(s == tensor - 1)
        def _():
            cot_copy.wait()
            totals = jnp.zeros((8, width), F32)
            for c in range(0, length, chunk):
                rows = slice(c, c + chunk)
                first_out = norm[rows, :] * vec_ref[1:2, :] + vec_ref[2:3, :]
                normed, inverse = layer_norm(first_out + (acc[rows, :] + vec_ref[3:4, :]))
                out[rows, :] = (normed * vec_ref[4:5, :] + vec_ref[5:6, :]).astype(BF)
                upstream = cot[rows, :].astype(F32)
                error = norm_backward(upstream * vec_ref[4:5, :], normed, inverse)
                low[rows, :] = error.astype(BF)
                errt[:, rows] = error.T.astype(BF)
                sums = [jnp.sum(a, axis=0, keepdims=True) for a in (error, upstream * normed, upstream)]
                totals += jnp.concatenate(sums + [jnp.zeros((5, width), F32)], axis=0)
            sums_ref[...] = totals
            for copy in late:
                copy.start()

        @pl.when(s >= tensor)
        def _():
            t = s - tensor
            slot = lax.rem(t, 2)

            @pl.when(t >= 2)
            def _():
                blocks.stores(place_ref, t - 2, stage.at[slot], keep, send, store_sems.at[slot], "wait")

            stage[slot] = nn(errt[...], act[t]).astype(BF).reshape(-1, blocks.rows, part)
            blocks.stores(place_ref, t, stage.at[slot], keep, send, store_sems.at[slot], "start")

        @pl.when(s == 2 * tensor - 1)
        def _():
            for last in range(max(tensor - 2, 0), tensor):
                blocks.stores(place_ref, last, stage.at[last % 2], keep, send, store_sems.at[last % 2], "wait")
            for copy in early + late:
                copy.wait()

    block_out = (blocks.n // 2, blocks.rows, part)
    wide = (length, width)
    return call(
        body, (2 * tensor,), [place],
        [(a, once(a.shape)) for a in (tokens, vec, up_bias)] + [at_index(a, i) for a, i in (*contexts, *outputs)] + [(cotangent, ANY), (feed, ANY)],
        [
            (wide, BF, ANY), ((length, 1), F32, once((length, 1))), ((width, length), BF, ANY),
            ((tensor, length, part), BF, pl.BlockSpec((1, length, part), lambda s, *_: (jnp.minimum(s, tensor - 1), 0, 0))),
            (wide, BF, ANY), (wide, BF, ANY), (block_out, BF, ANY), (block_out, BF, ANY), ((8, width), F32, once((8, width))),
        ],
        [
            pltpu.VMEM((tensor, 2, width, part), BF), pltpu.VMEM((tensor, length, part), BF), pltpu.VMEM(wide, BF), pltpu.VMEM(wide, F32),
            pltpu.VMEM((width, length), BF), pltpu.VMEM(wide, F32), pltpu.VMEM(wide, BF), pltpu.VMEM(wide, BF), pltpu.VMEM(wide, BF),
            pltpu.VMEM((width, length), BF), pltpu.VMEM(wide, BF), pltpu.VMEM((2, width // blocks.rows, blocks.rows, part), BF),
            pltpu.SemaphoreType.DMA((2, blocks.n)), pltpu.SemaphoreType.DMA((6,)), pltpu.SemaphoreType.DMA((2, blocks.n // tensor)),
        ],
        (2 * length * width * (width + 3 * tensor * part), 30 * length * width + 4 * length * tensor * part), "feed_forward",
    )


def feed_backward(err_low, slope, hidden_t, normed_one, inverse_one, vec, outputs, feed, place, blocks):
    length, width = err_low.shape
    tensor = blocks.tensor
    feed, tops = feed
    part = feed.shape[-1]
    groups = len(outputs)
    chunk = min(256, length)
    inner = outputs[0][0].shape[1]

    def body(place_ref, e_ref, s_ref, h_ref, i1_ref, vec_ref, *refs):
        o_refs, refs = refs[:groups], refs[groups:]
        n1_hbm, feed_hbm, keep, send, up_sums, err_hbm, errt_hbm, sums_ref, *refs = refs
        dctx_hbm, refs = refs[:groups], refs[groups:]
        w, acc, n1, err, errt, dctx, stage, low, feed_sems, sems, out_sems, store_sems = refs
        t = pl.program_id(0)
        slot = lax.rem(t, 2)
        inputs = [pltpu.make_async_copy(n1_hbm, n1, sems.at[0])]

        @pl.when(t == 0)
        def _():
            acc[...] = jnp.zeros_like(acc)
            for k in range(tensor):
                for copy in feed_loads(feed_hbm, w, feed_sems, blocks, k, tops[::-1]):
                    copy.start()
            for copy in inputs:
                copy.start()

        for copy in feed_loads(feed_hbm, w, feed_sems, blocks, t, tops[::-1]):
            copy.wait()
        span = min(512, length)
        rows_of = [slice(r, r + span) for r in range(0, length, span)]
        product = nn(e_ref[rows_of[0], :], w[t, 0])
        total = jnp.zeros((1, part), F32)
        for n, rows in enumerate(rows_of):
            following = nn(e_ref[rows_of[n + 1], :], w[t, 0]) if n + 1 < len(rows_of) else None
            grad = product * s_ref[0, rows, :].astype(F32)
            total += jnp.sum(grad, axis=0, keepdims=True)
            some = grad.astype(BF)
            low[rows, :] = some
            acc[rows, :] += nt(some, w[t, 1])
            product = following
        up_sums[pl.ds(t, 1), :] = total

        @pl.when(t >= 2)
        def _():
            blocks.stores(place_ref, t - 2, stage.at[slot], keep, send, store_sems.at[slot], "wait")

        stage[slot] = nn(h_ref[...], low[...]).astype(BF).reshape(-1, blocks.rows, part)
        blocks.stores(place_ref, t, stage.at[slot], keep, send, store_sems.at[slot], "start")

        @pl.when(t == tensor - 1)
        def _():
            for copy in inputs:
                copy.wait()
            totals = jnp.zeros((8, width), F32)
            copies = []
            for n, c in enumerate(range(0, length, chunk)):
                rows = slice(c, c + chunk)
                err_in = e_ref[rows, :].astype(F32) + acc[rows, :]
                normed = n1[rows, :].astype(F32)
                error = norm_backward(err_in * vec_ref[1:2, :], normed, i1_ref[rows, :])
                err[rows, :] = error
                turned = error.T.astype(BF)
                errt[:, rows] = turned
                some = pl.ds(c, chunk)
                copies += [
                    pltpu.make_async_copy(err.at[some, :], err_hbm.at[some, :], out_sems.at[n, 0]),
                    pltpu.make_async_copy(errt.at[:, some], errt_hbm.at[:, some], out_sems.at[n, 1]),
                ]
                for g in range(groups):
                    dctx[g, :, rows] = nn(o_refs[g][0], turned).astype(BF)
                    copies.append(pltpu.make_async_copy(dctx.at[g, :, some], dctx_hbm[g].at[:, some], out_sems.at[n, 2 + g]))
                for copy in copies[-2 - groups :]:
                    copy.start()
                sums = [jnp.sum(a, axis=0, keepdims=True) for a in (error, err_in * normed, err_in)]
                totals += jnp.concatenate(sums + [jnp.zeros((5, width), F32)], axis=0)
            sums_ref[...] = totals
            for last in range(max(tensor - 2, 0), tensor):
                blocks.stores(place_ref, last, stage.at[last % 2], keep, send, store_sems.at[last % 2], "wait")
            for copy in copies:
                copy.wait()

    block_out = (blocks.n // 2, blocks.rows, part)
    wide = (length, width)
    return call(
        body, (tensor,), [place],
        [
            (err_low, once(wide)), (slope, pl.BlockSpec((1, length, part), lambda t, *_: (t, 0, 0))), (hidden_t, once((width, length))),
            (inverse_one, once((length, 1))), (vec, once(vec.shape)), *[at_index(o, i) for o, i in outputs],
            (normed_one, ANY), (feed, ANY),
        ],
        [
            (block_out, BF, ANY), (block_out, BF, ANY), ((8, part), F32, once((8, part))), (wide, F32, ANY), ((width, length), BF, ANY),
            ((8, width), F32, once((8, width))), *[((inner, length), BF, ANY) for _ in outputs],
        ],
        [
            pltpu.VMEM((tensor, 2, width, part), BF), pltpu.VMEM(wide, F32), pltpu.VMEM(wide, BF), pltpu.VMEM(wide, F32),
            pltpu.VMEM((width, length), BF), pltpu.VMEM((groups, inner, length), BF), pltpu.VMEM((2, width // blocks.rows, blocks.rows, part), BF), pltpu.VMEM((length, part), BF),
            pltpu.SemaphoreType.DMA((2, blocks.n)), pltpu.SemaphoreType.DMA((2,)), pltpu.SemaphoreType.DMA((length // chunk, 2 + groups)),
            pltpu.SemaphoreType.DMA((2, blocks.n // tensor)),
        ],
        (2 * length * width * (width + 3 * tensor * part), 30 * length * width + 2 * length * tensor * part), "feed_backward",
    )


def finish(first_terms, other_terms, rows, groups, column, cols):
    width = groups * HD
    n = len(first_terms)

    def body(i_ref, *refs):
        (q_ref, k_ref, v_ref, o_ref, qb_ref, vb_ref), terms = refs[2 * n :], refs[: 2 * n]
        sums = [sum(r[0].astype(F32) for r in part) for part in (terms[:n], terms[n:])]
        biases = []
        for c in range(groups):
            block = sums[0] if c == 0 else sums[1][:, (c - 1) * PACK : c * PACK]
            for j, out in enumerate((q_ref, k_ref, v_ref)):
                out[:, c * HD : (c + 1) * HD] = block[:rows, j * HD : (j + 1) * HD]
            o_ref[c * HD : (c + 1) * HD, :] = block[:rows, 2 * HD :].T[HD:]
            biases.append(block[rows : rows + 1])
        biases = jnp.concatenate(biases + [jnp.zeros((8 - groups, PACK), F32)], axis=0)
        for out, start in ((qb_ref, 0), (vb_ref, 2 * HD)):
            out[...] = pltpu.roll(biases, lax.rem(2 * PACK - start - i_ref[0], PACK), 1)[:groups, :cols]

    def block(array):
        return array, pl.BlockSpec((1, *array.shape[1:]), lambda *_: (0, 0, 0))

    shapes = [(rows, width)] * 3 + [(width, rows), (groups, cols), (groups, cols)]
    return call(
        body, (1,), [column.reshape(1)], [block(t) for t in (*first_terms, *other_terms)],
        [(shape, F32, full(shape)) for shape in shapes], [], (1e6, 2 * n * rows * PACK * 6), "finish",
    )


def local(
    tokens, query_weight, key_weight, value_weight, output_weight, query_bias, value_bias,
    output_bias, first_gain, first_shift, up_weight, up_bias, down_weight, down_bias,
    second_gain, second_shift, cotangent,
):
    dp, tensor = lax.axis_size("dp"), lax.axis_size("tensor")
    count = dp * tensor
    rows = query_weight.shape[0]
    width = rows * dp
    groups = query_weight.shape[1] // HD
    heads = groups * tensor
    slot = output_bias.shape[0]
    cols = query_bias.shape[1]
    me = lax.axis_index(AXES)
    place, devs, owners = position_table(me, count), device_table(me, count), owner_table(me, count)
    direct = rows % 16 == 0

    vectors = jnp.stack([output_bias, first_gain, first_shift, down_bias, second_gain, second_shift])
    extra = small_block(vectors, query_bias, value_bias, up_bias)
    output_turned = output_weight.T
    by_group = [
        jnp.concatenate([w[:, c * HD : (c + 1) * HD] for w in (query_weight, key_weight, value_weight, output_turned)], axis=1)
        for c in range(groups)
    ]
    first, second = (Gathering(jnp.concatenate(blocks, axis=axis), count) for blocks, axis in (([by_group[0], extra], 0), (by_group[1:], 1)))
    feed = lax.all_gather(jnp.concatenate([up_weight, down_weight.T], axis=0), AXES, axis=0, tiled=False)
    tokens_t, place, devs, owners, owner_column, dev_column = wave(
        [first], tokens.T, place, devs, owners, owners.reshape(count, 1), devs.reshape(count, 1)
    )
    wave([first, second])
    wave([first])
    direct = rows % 16 == 0
    small_set = (first.pieces, rows) if direct else ([jnp.concatenate([p[:, rows:] for p in first.pieces], axis=0)], 0)
    if direct:
        blocks = Blocks(count, rows, tensor)
        block_place, block_devs = place, devs
    else:
        blocks = Blocks(tensor, width, tensor)
        block_place = block_devs = jnp.arange(tensor, dtype=jnp.int32)

    def by_matrix(ordered):
        return [ordered.reshape(dp, tensor, rows, -1).transpose(1, 0, 2, 3).reshape(tensor, width, -1)]

    def ready(gathering):
        if direct:
            return gathering.pieces
        return by_matrix(jnp.take(jnp.concatenate(gathering.pieces, axis=0)[:, :rows], gathered_place(me, count), axis=0))

    def scattering(keep, send, more=None):
        if not direct:
            stacked = jnp.concatenate([keep, send], axis=0)
            parts = [stacked[:, :width].reshape(tensor, dp, rows, -1).transpose(1, 0, 2, 3).reshape(count, rows, -1)]
            if stacked.shape[1] > width:
                parts.append(jnp.tile(stacked[:, width:], (dp, 1, 1)))
            stacked = jnp.take(jnp.concatenate(parts, axis=1), owners, axis=0)
            if more is not None:
                stacked = jnp.concatenate([stacked, more], axis=1)
            keep, send = stacked[: count // 2], stacked[count // 2 :]
        return Scattering(keep, send, count)

    tokens_now = wave([second], tokens)
    vec, bias_pack, up_rows = unpack_small(*small_set, dev_column, slot, cols, width, tensor)
    first_set = ready(first)
    one = attention_forward(tokens_now, first_set, bias_pack, 0, block_devs, blocks)
    tokens_now = wave([second], tokens, one[4])[0]
    second_set = ready(second)
    others = attention_forward(tokens_now, second_set, bias_pack, 1, block_devs, blocks)
    weights = [(first_set, 0)] + [(second_set, c * PACK) for c in range(groups - 1)]
    forward = [(one, 0)] + [(others, c) for c in range(groups - 1)]
    if not direct:
        feed = jnp.concatenate([by_matrix(feed[:, :rows])[0], by_matrix(feed[:, rows:])[0]], axis=1)
    feed = (feed, (0, feed.shape[1] // 2))
    outputs = [(f[5], i) for f, i in forward]
    normed_one, inverse_one, hidden_t, slope, layer_out, err_two_low, down_keep, down_send, sums_two = feed_forward(
        tokens, cotangent, [(f[2], i) for f, i in forward], outputs, vec, up_rows, feed, block_place, blocks
    )
    grad_down = scattering(down_keep, down_send)
    err_two_low = wave([grad_down], err_two_low)
    up_keep, up_send, up_sums, err_one, err_one_t, sums_one, *context_grads = feed_backward(
        err_two_low, slope, hidden_t, normed_one, inverse_one, vec, outputs, feed, block_place, blocks
    )
    grad_up = scattering(up_keep, up_send)
    small = pack_small_grads(sums_one, sums_two, up_sums, owner_column, slot, cols, tensor)
    column = lax.axis_index("dp") * cols
    backward = [None] * groups
    token_sum = err_one
    last, packed, moving = (err_one_t,), None, [grad_down, grad_up]
    for c in reversed(range(groups)):
        carries = c == groups - 1
        options = {}
        if c and direct:
            options = dict(into=packed, lane=(c - 1) * PACK, high=rows + 2 * EXTRA, wide=(groups - 1) * PACK)
        backward[c] = attention_backward(
            tokens_t, err_one_t, *forward[c], wave(moving, context_grads[c], since=last), token_sum, weights[c], block_place, block_devs, blocks,
            small if direct and carries else None, **options,
        )
        token_sum = backward[c][2]
        last = (token_sum,)
        if c and direct:
            packed = backward[c][:2]
        if c == 1:
            if direct:
                others = scattering(*packed)
            else:
                packed = [jnp.concatenate([backward[g][i] for g in range(1, groups)], axis=2) for i in range(2)]
                others = scattering(*packed, jnp.pad(small, ((0, 0), (0, 0), ((groups - 2) * PACK, 0))))
            moving = [others, grad_down, grad_up]
    zero = scattering(*backward[0][:2])
    while grad_down.phases:
        wave([grad_down])
    grad_up.terms, grad_down.terms = wave([zero], grad_up.terms, grad_down.terms)
    wave([others], since=last)
    wave([zero, grad_up])
    while grad_up.phases:
        wave([grad_up])
    grad_up.terms, grad_down.terms = wave([zero, others], grad_up.terms, grad_down.terms)
    grad_up, grad_down = grad_up.result(), grad_down.result()
    while zero.phases:
        grad_up, grad_down = wave([zero, others], grad_up, grad_down)
    tail = sum(t[0, rows + EXTRA :, (groups - 2) * PACK :].astype(F32) for t in others.terms)
    if direct:
        out_query, out_key, out_value, out_output, *bias_out = finish(zero.terms, others.terms, rows, groups, column, cols)
    else:
        results = [zero.result()] + jnp.split(others.result()[: rows + EXTRA], groups - 1, axis=1)
        bias_rows = jnp.stack([r[rows] for r in results])
        bias_out = [lax.dynamic_slice(bias_rows, (0, start + column), (groups, cols)) for start in (0, 2 * HD)]
        out = jnp.stack([r[:rows] for r in results], axis=1).reshape(rows, groups, 4, HD)
        out_query, out_key, out_value, out_output = (out[:, :, i].reshape(rows, groups * HD) for i in range(4))
        out_output = out_output.T
    vecs = [tail[v // 2, (v % 2) * LANES : (v % 2) * LANES + slot] for v in range(6)]
    return (
        layer_out,
        token_sum,
        out_query,
        out_key,
        out_value,
        out_output,
        bias_out[0],
        bias_out[1],
        vecs[0],
        vecs[1],
        vecs[2],
        grad_up,
        tail[: up_bias.shape[0], 64 : 64 + cols],
        grad_down.T,
        vecs[3],
        vecs[4],
        vecs[5],
    )


def solution(mesh):
    both, cross, turned, vector = P(AXES, None), P("dp", "tensor"), P("tensor", "dp"), P(AXES)
    return jax.shard_map(
        local,
        mesh=mesh,
        in_specs=(
            both, cross, cross, cross, turned, turned, turned, vector, vector, vector,
            cross, turned, turned, vector, vector, vector, both,
        ),
        out_specs=(
            both, both, cross, cross, cross, turned, turned, turned, vector, vector, vector,
            cross, turned, turned, vector, vector, vector,
        ),
        check_vma=False,
    )
```

```python
import functools
import math

import jax
import jax.numpy as jnp
import numpy as np
from jax import lax
from jax.experimental import pallas as pl
from jax.experimental.pallas import tpu as pltpu
from jax.sharding import PartitionSpec as P

HD = 64
L = 1024
PACK = 4 * HD
EPSILON = 1e-12
AXES = ("dp", "tensor")
EXTRA = 16
LANES = 128
BF = jnp.bfloat16
F32 = jnp.float32
SDS = jax.ShapeDtypeStruct
ANY = pl.BlockSpec(memory_space=pl.ANY)


def nn(a, b):
    return lax.dot_general(a, b, (((1,), (0,)), ((), ())), preferred_element_type=F32)


def nt(a, b):
    return lax.dot_general(a, b, (((1,), (1,)), ((), ())), preferred_element_type=F32)


def full(shape):
    return pl.BlockSpec(shape, lambda *_: (0,) * len(shape))


def once(shape):
    return pl.BlockSpec(shape, lambda *_: (0,) * len(shape), pipeline_mode=pl.Buffered(1))


def at_index(array, i):
    shape = (1, *array.shape[1:])
    return array, pl.BlockSpec(shape, lambda *_: (i,) + (0,) * (len(shape) - 1), pipeline_mode=pl.Buffered(1))


def call(body, grid, tables, ins, outs, scratch, cost, name, aliases={}):
    flops, moved = cost
    return pl.pallas_call(
        body,
        grid_spec=pltpu.PrefetchScalarGridSpec(
            num_scalar_prefetch=len(tables),
            grid=grid,
            in_specs=[s for _, s in ins],
            out_specs=[s for _, _, s in outs],
            scratch_shapes=scratch,
        ),
        out_shape=[SDS(s, d) for s, d, _ in outs],
        compiler_params=pltpu.CompilerParams(
            dimension_semantics=("arbitrary",) * len(grid), vmem_limit_bytes=60 * 2**20
        ),
        cost_estimate=pl.CostEstimate(flops=int(flops * 0.01), bytes_accessed=int(moved * 0.01), transcendentals=0),
        name=name,
        input_output_aliases=aliases,
    )(*tables, *[a for a, _ in ins])


def exchange(array, differs, count):
    even, odd = differs if isinstance(differs, tuple) else (differs, differs)
    return lax.ppermute(array, AXES, [(d, d ^ (odd if d & 1 else even)) for d in range(count)])


def phases_of(count):
    bits = count.bit_length() - 1
    return [*((k, 1) for k in range(bits - 1, 4, -1)), (3, 2), (1, 2), (0, 1)]


def scatter_phases_of(count):
    bits = count.bit_length() - 1
    return [[1], [(2, 4)], [(4, 2)], [8, 16, 24], *([1 << k] for k in range(5, bits))]


class Gathering:
    def __init__(self, block, count):
        self.pieces, self.count, self.phases = [block[None]], count, phases_of(count)
        while self.phases[0][1] == 1:
            self.move(self.outgoing())

    def outgoing(self):
        if self.phases[0] != (0, 1) and len(self.pieces) > 1:
            self.pieces = [jnp.concatenate(self.pieces, axis=0)]
        return self.pieces

    def move(self, pieces):
        low, bits = self.phases.pop(0)
        self.pieces = self.pieces + [exchange(p, k << low, self.count) for k in range(1, 1 << bits) for p in pieces]


class Scattering:
    def __init__(self, keep, send, count):
        self.terms, self.sends, self.count, self.phases = [keep], [send], count, scatter_phases_of(count)
        self.size = keep.shape[0]

    def looked_at(self, *since):
        self.terms = lax.optimization_barrier((self.terms, since))[0]

    def outgoing(self):
        if self.sends is None:
            parts = 1 + len(self.phases[0])
            size = self.size // parts
            self.sends = [sum(t[k * size : (k + 1) * size].astype(F32) for t in self.terms).astype(BF) for k in range(1, parts)]
            self.size = size
        return self.sends

    def move(self, sends):
        self.terms = self.terms + [exchange(p, k, self.count) for k, p in zip(self.phases.pop(0), sends)]
        self.sends = None

    def result(self):
        return sum(t[0].astype(F32) for t in self.terms)


def wave(moves, *beside, since=()):
    moves = [m for m in moves if m.phases]
    for m in moves:
        if since and isinstance(m, Scattering):
            m.looked_at(*since)
    outgoing, beside = lax.optimization_barrier(([m.outgoing() for m in moves], beside))
    for m, array in zip(moves, outgoing):
        m.move(array)
    return beside[0] if len(beside) == 1 else beside


def fields_of(count):
    top, fields = count.bit_length() - 1, []
    for low, bits in phases_of(count)[::-1]:
        top -= bits
        fields.append((low, bits, top))
    return fields


def position_table(me, count):
    bits = count.bit_length() - 1
    device = jnp.arange(count, dtype=jnp.int32)
    differs = device ^ me
    one, two = (differs >> 1) & 1, (differs >> 2) & 1
    odd = (device & 1) == 1
    place = ((differs & 1) << (bits - 1)) | (jnp.where(odd, two, one) << (bits - 2)) | (jnp.where(odd, one, two) << (bits - 3))
    place = place | (((differs >> 3) & 3) << (bits - 5))
    for k in range(5, bits):
        place = place | (((differs >> k) & 1) << (bits - 1 - k))
    return place


def owner_table(me, count):
    bits = count.bit_length() - 1
    place = jnp.arange(count, dtype=jnp.int32)
    core, upper, lower = ((place >> (bits - k)) & 1 for k in (1, 2, 3))
    odd = ((me ^ core) & 1) == 1
    differs = core | (jnp.where(odd, lower, upper) << 1) | (jnp.where(odd, upper, lower) << 2) | (((place >> (bits - 5)) & 3) << 3)
    for k in range(5, bits):
        differs = differs | (((place >> (bits - 1 - k)) & 1) << k)
    return differs ^ me


def gathered_place(me, count):
    differs = jnp.arange(count, dtype=jnp.int32) ^ me
    return sum(((differs >> low) & ((1 << bits) - 1)) << at for low, bits, at in fields_of(count))


def device_table(me, count):
    place = jnp.arange(count, dtype=jnp.int32)
    return sum(((place >> at) & ((1 << bits) - 1)) << low for low, bits, at in fields_of(count)) ^ me


class Blocks:
    def __init__(self, n, rows, tensor):
        self.n, self.rows, self.tensor = n, rows, tensor

    def at(self, d):
        return lax.rem(d, self.tensor), pl.multiple_of(lax.div(d, self.tensor) * self.rows, self.rows)

    def loads(self, devs, pieces, target, sems, lane=0, top=0):
        out, p = [], 0
        flat = len(target.shape) == 2
        width = target.shape[-1] // (self.tensor if flat else 1)
        for piece in pieces:
            for j in range(piece.shape[0]):
                t, row = self.at(devs[p])
                rows = pl.ds(row, self.rows)
                into = target.at[rows, pl.ds(pl.multiple_of(t * width, width), width)] if flat else target.at[t, rows, :]
                out.append(pltpu.make_async_copy(
                    piece.at[j, pl.ds(top, self.rows), pl.ds(lane, width)], into, sems.at[p]
                ))
                p += 1
        return out

    def stores(self, place, t, stage, keep, send, sems, action, lane=0):
        half = self.n // 2
        lanes = pl.ds(lane, stage.shape[-1])
        for i in range(self.n // self.tensor):
            p = place[i * self.tensor + t]
            kept = pltpu.make_async_copy(stage.at[i], keep.at[lax.rem(p, half), :, lanes], sems.at[i])
            if action == "wait":
                kept.wait()
            else:
                sent = pltpu.make_async_copy(stage.at[i], send.at[lax.rem(p, half), :, lanes], sems.at[i])
                pl.when(p < half)(kept.start)
                pl.when(p >= half)(sent.start)


def spread_constants(slot, cols, width):
    lane = np.arange(width)
    a, c = np.zeros((LANES, width), np.float32), np.zeros((LANES, width), np.float32)
    for j in range(slot):
        a[j] = lane % slot == j
    for j in range(cols):
        a[32 + j] = lane % cols == j
        c[64 + j] = lane % cols == j
    return jnp.asarray(a, BF), jnp.asarray(c, BF)


def small_masks(device, slot, cols, width, tensor):
    n = device.shape[0]
    shift = tensor.bit_length() - 1
    row = lax.broadcasted_iota(jnp.int32, (n, EXTRA, width), 1)
    lane = lax.broadcasted_iota(jnp.int32, (n, EXTRA, width), 2)
    i, t = device >> shift, device & (tensor - 1)
    in_head = (lane & (HD - 1)) >> (cols.bit_length() - 1)
    groups = width // HD // tensor
    vector = (row < 9) & (lane >= device * slot) & (lane < (device + 1) * slot)
    bias = (row >= 9) & (row < 9 + groups) & ((lane >> 6) == t * groups + row - 9) & (in_head == i)
    hidden = (row < width // HD) & ((lane >> 6) == row) & (in_head == i)
    return vector | bias, hidden, t


def unpack_small(pieces, top, device, slot, cols, width, tensor):
    n = device.shape[0]
    groups = width // HD // tensor
    spread_a, spread_c = spread_constants(slot, cols, width)

    def body(d_ref, a_ref, c_ref, *refs):
        piece_refs, (vec_ref, bias_ref, up_ref, x_s, sems) = refs[: len(pieces)], refs[len(pieces) :]
        copies, at = [], 0
        for j, piece in enumerate(piece_refs):
            size = piece.shape[0]
            copies.append(pltpu.make_async_copy(piece.at[:, pl.ds(top, EXTRA), :], x_s.at[pl.ds(at, size)], sems.at[j]))
            at += size
        for copy in copies:
            copy.start()
        d = d_ref[...].reshape(n, 1, 1)
        main, hidden, t = small_masks(d, slot, cols, width, tensor)
        for copy in copies:
            copy.wait()
        x = x_s[...].reshape(n * EXTRA, 2 * LANES)
        bias_ref[...] = jnp.zeros_like(bias_ref)
        for half in range(2):
            y = nn(x[:, half * LANES : (half + 1) * LANES], a_ref[...]).reshape(n, EXTRA, width)
            total = jnp.sum(jnp.where(main, y, 0.0), axis=0)
            for v in range(half, 6, 2):
                r = v // 2
                vec_ref[v : v + 1, :] = total[r : r + 1] + total[3 + r : 4 + r] + total[6 + r : 7 + r]
            row = jnp.sum(total[9:EXTRA], axis=0, keepdims=True)
            for head in range(groups * tensor):
                at = half * 2 * HD
                bias_ref[head % groups, head // groups : head // groups + 1, at : at + HD] = row[:, head * HD : (head + 1) * HD]
        y = nn(x[:, :LANES], c_ref[...]).reshape(n, EXTRA, width)
        y = jnp.where(hidden, y, 0.0)
        for k in range(tensor):
            picked = jnp.sum(jnp.where(t == k, y, 0.0), axis=0)
            up_ref[k : k + 1, :] = jnp.sum(picked, axis=0, keepdims=True)

    row8, bias = (8, width), (groups, tensor, PACK)
    return call(
        body, (1,), [],
        [(a, full(a.shape)) for a in (device, spread_a, spread_c)] + [(p, ANY) for p in pieces],
        [(row8, F32, full(row8)), (bias, F32, full(bias)), (row8, F32, full(row8))],
        [pltpu.VMEM((n, EXTRA, PACK), BF), pltpu.SemaphoreType.DMA((len(pieces),))],
        (3 * 2 * n * EXTRA * LANES * width, n * EXTRA * PACK * 2), "unpack_small",
    )


def spread_small_grads(one_ref, two_ref, u_ref, d_ref, a_ref, c_ref, slot, cols, tensor):
    n, width = d_ref.shape[0], one_ref.shape[-1]
    d = d_ref[...].reshape(n, 1, 1)
    main, hidden, t = small_masks(d, slot, cols, width, tensor)
    row = lax.broadcasted_iota(jnp.int32, (EXTRA, width), 0)
    halves = []
    for half in range(2):
        z = jnp.zeros((EXTRA, width), F32)
        for v in range(half, 6, 2):
            z = jnp.where(row == v // 2, (one_ref, two_ref)[v // 3][v % 3 : v % 3 + 1, :], z)
        spread = jnp.where(main, z[None], 0.0).astype(BF).reshape(n * EXTRA, width)
        halves.append(nt(spread, a_ref[...]))
    z = jnp.zeros((n, EXTRA, width), F32)
    for k in range(tensor):
        z = jnp.where(t == k, u_ref[k : k + 1, :].reshape(1, 1, width), z)
    spread = jnp.where(hidden, z, 0.0).astype(BF).reshape(n * EXTRA, width)
    halves[0] = halves[0] + nt(spread, c_ref[...])
    return jnp.concatenate(halves, axis=1).astype(BF).reshape(n, EXTRA, 2 * LANES)


def pack_small_grads(one, two, up, device, slot, cols, tensor):
    n, width = device.shape[0], one.shape[-1]
    spread_a, spread_c = spread_constants(slot, cols, width)

    def body(one_ref, two_ref, u_ref, d_ref, a_ref, c_ref, out_ref):
        out_ref[...] = spread_small_grads(one_ref, two_ref, u_ref, d_ref, a_ref, c_ref, slot, cols, tensor)

    shape = (n, EXTRA, PACK)
    return call(
        body, (1,), [],
        [(a, full(a.shape)) for a in (one, two, up, device, spread_a, spread_c)],
        [(shape, BF, full(shape))], [], (3 * 2 * n * EXTRA * LANES * width, 2 * n * EXTRA * PACK), "pack_small",
    )[0]


def three_parts(vector):
    high = lax.reduce_precision(vector, 8, 7)
    middle = lax.reduce_precision(vector - high, 8, 7)
    lowest = lax.reduce_precision(vector - high - middle, 8, 7)
    return jnp.stack([high, middle, lowest]).astype(BF)


def small_block(vectors, query_bias, value_bias, up_bias):
    slot = vectors.shape[1]
    parts = three_parts(vectors).reshape(9, 2, slot)

    def placed(array, row, lane):
        return jnp.pad(array, ((row, EXTRA - row - array.shape[0]), (lane, PACK - lane - array.shape[1])))

    return (
        placed(parts[:, 0], 0, 0) + placed(parts[:, 1], 0, LANES) + placed(query_bias, 9, 32)
        + placed(value_bias, 9, LANES + 32) + placed(up_bias, 0, 64)
    )


def attention_forward(tokens, pieces, bias, base, devs, blocks):
    length, width = tokens.shape
    heads = blocks.tensor
    inner = heads * HD
    groups = pieces[0].shape[-1] // PACK

    def body(devs_ref, x_ref, b_ref, *refs):
        piece_refs, (qkv_ref, e_ref, ctx_ref, ctxt_ref, inv_ref, ot_ref, w, ot_s, vt_s, sems) = refs[: len(pieces)], refs[len(pieces) :]
        c, t = pl.program_id(0), pl.program_id(1)

        loads = [blocks.loads(devs_ref, piece_refs, w.at[g], sems.at[g], g * PACK) for g in range(groups)]

        @pl.when((c == 0) & (t == 0))
        def _():
            for copies in loads:
                for copy in copies:
                    copy.start()
            vt_s[HD:, :] = jnp.ones((HD, length), BF)

        for g in range(groups):
            @pl.when((c == g) & (t == 0))
            def _():
                for copy in loads[g]:
                    copy.wait()

        wt = w[c, t]
        col = lax.broadcasted_iota(jnp.int32, (1, PACK), 1)
        pre = nn(x_ref[...], wt) + b_ref[base + c, pl.ds(t, 1), :]
        low = (pre * jnp.where(col < HD, 1.0 / math.sqrt(HD), 1.0)).astype(BF)
        qkv_ref[0] = low
        q, k = low[:, :HD], low[:, HD : 2 * HD]
        vt_s[:HD, :] = low[:, 2 * HD :].T[:HD]
        square = pre[:, : 2 * HD] * pre[:, : 2 * HD]
        pick = lax.broadcasted_iota(jnp.int32, (2 * HD, LANES), 0) // HD == lax.broadcasted_iota(jnp.int32, (2 * HD, LANES), 1)
        norms = jnp.max(nn(square.astype(BF), pick.astype(BF)), axis=0, keepdims=True)
        bound = jnp.sqrt(norms[0, 0] * norms[0, 1]) * (1.1 / math.sqrt(HD))

        @pl.when(bound <= 40.0)
        def _():
            e_ref[0] = jnp.exp(nt(k, q)).astype(BF)

        @pl.when(jnp.logical_not(bound <= 40.0))
        def _():
            def some(j, _):
                at = pl.ds(pl.multiple_of(j * LANES, LANES), LANES)
                scores = nt(k, qkv_ref[0, at, :][:, :HD])
                e_ref[0, :, at] = jnp.exp(scores - jnp.max(scores, axis=0, keepdims=True)).astype(BF)
                return 0

            lax.fori_loop(0, length // LANES, some, 0)

        mixed = nn(vt_s[...], e_ref[0])
        inv = 1.0 / mixed[HD : HD + 1]
        inv_ref[0] = jnp.broadcast_to(inv, (8, length))
        ctxt_ref[0, pl.ds(t * HD, HD), :] = mixed[:HD] * inv
        ot_s[pl.ds(t * HD, HD), :] = wt[:, 2 * HD :].T[HD:].astype(F32)

        @pl.when(t == heads - 1)
        def _():
            ctx_ref[0] = ctxt_ref[0].T.astype(BF)
            ot_ref[0] = ot_s[...].astype(BF)

    by_head = lambda *s: pl.BlockSpec((1, *s), lambda c, t, *_: (c * heads + t, 0, 0))
    by_group = lambda *s: pl.BlockSpec((1, *s), lambda c, t, *_: (c, 0, 0))
    return call(
        body, (groups, heads), [devs],
        [(tokens, full(tokens.shape)), (bias, full(bias.shape))] + [(p, ANY) for p in pieces],
        [
            ((groups * heads, length, PACK), BF, by_head(length, PACK)),
            ((groups * heads, length, length), BF, by_head(length, length)),
            ((groups, length, inner), BF, by_group(length, inner)),
            ((groups, inner, length), F32, by_group(inner, length)),
            ((groups * heads, 8, length), F32, by_head(8, length)),
            ((groups, inner, width), BF, by_group(inner, width)),
        ],
        [pltpu.VMEM((groups, heads, width, PACK), BF), pltpu.VMEM((inner, width), F32), pltpu.VMEM((2 * HD, length), BF), pltpu.SemaphoreType.DMA((groups, blocks.n))],
        (groups * heads * (2 * length * width * PACK + 16 * length * length * HD), groups * heads * length * length * 2), "attention_forward",
    )


def attention_backward(tokens_t, err_t, forward, index, dctxt, total, weights, place, devs, blocks, more=None, into=None, lane=0, high=None, wide=PACK):
    width, length = tokens_t.shape
    pieces, piece_lane = weights
    chunk = min(256, length)
    qkv, e, ctx, ctxt, inv, _ = forward
    heads = blocks.tensor
    inner = heads * HD
    half = blocks.n // 2
    scale = 1.0 / math.sqrt(HD)
    rows, extra, given = blocks.rows, 0 if more is None else 6, 0 if into is None else 2
    high = high or blocks.rows + EXTRA
    tall = rows + EXTRA * (1 if more is None else 2)
    if more is not None:
        sums, slot, cols = more
        more = [*sums, *spread_constants(slot, cols, width)]

    def body(place_ref, devs_ref, qkv_ref, e_ref, inv_ref, ctxt_ref, dctxt_ref, xt_hbm, et_hbm, ctx_hbm, total_hbm, *refs):
        piece_refs, refs = refs[: len(pieces)], refs[len(pieces) :]
        more_ref, (keep_ref, send_ref, out_hbm, stage, bias, xt, et, ctx, d_ref, sum_s, w, sems, in_sems, w_sems, out_sems, *small) = refs[:extra], refs[extra + given :]
        keep_rows, send_rows = (r.at[:, pl.ds(0, tall), :] for r in (keep_ref, send_ref))
        t = pl.program_id(0)
        late = [pltpu.make_async_copy(a, b, in_sems.at[n]) for n, (a, b) in enumerate([(xt_hbm, xt), (et_hbm, et), (ctx_hbm.at[index], ctx), (total_hbm, sum_s)])]
        late += blocks.loads(devs_ref, piece_refs, w, w_sems, piece_lane)

        @pl.when(t == 0)
        def _():
            for copy in late:
                copy.start()
            if extra:
                small[0][...] = spread_small_grads(*more_ref, slot, cols, heads)

        q, k, v = qkv_ref[0, :, :HD], qkv_ref[0, :, HD : 2 * HD], qkv_ref[0, :, 2 * HD : 3 * HD]
        mine = pl.ds(t * HD, HD)
        dot = (dctxt_ref[mine, :].astype(F32) * inv_ref[0, :1, :]).astype(BF)
        delta = jnp.sum(dot.astype(F32) * ctxt_ref[0, mine, :], axis=0, keepdims=True)
        ee = e_ref[0]
        ds = (ee.astype(F32) * (nn(v, dot) - delta)).astype(BF)
        dv = nn(ee, dot.T)
        dk = nn(ds, q)
        dq = (nn(k.T, ds) * scale).T
        d = jnp.concatenate([dq, dk, dv, jnp.zeros_like(dv)], axis=1)
        bias[t] = jnp.broadcast_to(jnp.sum(d, axis=0, keepdims=True), (8, PACK))
        d_ref[:, pl.ds(pl.multiple_of(t * PACK, PACK), PACK)] = d.astype(BF)

        @pl.when(t == heads - 1)
        def _():
            for copy in late:
                copy.wait()
            outs = []
            for n, c in enumerate(range(0, length, chunk)):
                sum_s[c : c + chunk, :] += nt(d_ref[c : c + chunk, :], w[...])
                outs.append(pltpu.make_async_copy(sum_s.at[pl.ds(c, chunk), :], out_hbm.at[pl.ds(c, chunk), :], out_sems.at[n]))
                outs[-1].start()
            go = nn(et[...], ctx[...])
            for h in range(heads):
                if h % 2 == 0:
                    both = nn(xt[...], d_ref[:, h * PACK : (h + 2) * PACK])
                g = both[:, h % 2 * PACK : (h % 2 + 1) * PACK]
                low = jnp.concatenate([g[:, : 3 * HD], go[:, h * HD : (h + 1) * HD]], axis=1).astype(BF)
                row = jnp.concatenate([bias[h]] * (EXTRA // 8), axis=0).astype(BF)
                for i in range(width // rows):
                    stage[h, i, :rows, :] = low[i * rows : (i + 1) * rows]
                    stage[h, i, rows : rows + EXTRA, :] = row
                    if extra:
                        stage[h, i, rows + EXTRA :, :] = small[0][place_ref[i * heads + h]]
                blocks.stores(place_ref, h, stage.at[h], keep_rows, send_rows, sems.at[h], "start", lane)
            for h in range(heads):
                blocks.stores(place_ref, h, stage.at[h], keep_rows, send_rows, sems.at[h], "wait", lane)
            for copy in outs:
                copy.wait()

    by_head = lambda *s: pl.BlockSpec((1, *s), lambda t, *_: (index * heads + t, 0, 0))
    out = (half, high, wide)
    return call(
        body, (heads,), [place, devs],
        [
            (qkv, by_head(length, PACK)), (e, by_head(length, length)), (inv, by_head(8, length)),
            (ctxt, pl.BlockSpec((1, *ctxt.shape[1:]), lambda t, *_: (index, 0, 0))), (dctxt, full(dctxt.shape)), (tokens_t, ANY), (err_t, ANY), (ctx, ANY), (total, ANY), *((p, ANY) for p in pieces),
            *((m, full(m.shape)) for m in more or ()), *((a, ANY) for a in into or ()),
        ],
        [(out, BF, ANY), (out, BF, ANY), ((length, width), F32, ANY)],
        [
            pltpu.VMEM((heads, width // rows, tall, PACK), BF), pltpu.VMEM((heads, 8, PACK), F32), pltpu.VMEM((width, length), BF), pltpu.VMEM((width, length), BF), pltpu.VMEM((length, inner), BF),
            pltpu.VMEM((length, heads * PACK), BF), pltpu.VMEM((length, width), F32), pltpu.VMEM((width, heads * PACK), BF),
            pltpu.SemaphoreType.DMA((heads, blocks.n // heads)), pltpu.SemaphoreType.DMA((4,)), pltpu.SemaphoreType.DMA((blocks.n,)),
            pltpu.SemaphoreType.DMA((length // chunk,)), *([pltpu.VMEM((blocks.n, EXTRA, PACK), BF)] if extra else []),
        ],
        (heads * (2 * length * width * PACK + 32 * length * length * HD), heads * length * length * 2), "attention_backward",
        {11 + len(pieces) + extra: 0, 12 + len(pieces) + extra: 1} if given else {},
    )


def layer_norm(residual):
    centered = residual - jnp.mean(residual, axis=-1, keepdims=True)
    inverse = lax.rsqrt(jnp.mean(centered * centered, axis=-1, keepdims=True) + EPSILON)
    return centered * inverse, inverse


def norm_backward(scaled, normed, inverse):
    first = jnp.mean(scaled, axis=-1, keepdims=True)
    second = jnp.mean(scaled * normed, axis=-1, keepdims=True)
    return inverse * (scaled - first - normed * second)


def feed_loads(feed, target, sems, blocks, t, tops):
    copies = []
    for kind, top in enumerate(tops):
        for i in range(blocks.n // blocks.tensor):
            d = i * blocks.tensor + t
            copies.append(pltpu.make_async_copy(
                feed.at[d, pl.ds(top, blocks.rows), :], target.at[t, kind, pl.ds(i * blocks.rows, blocks.rows), :], sems.at[kind, d]
            ))
    return copies


def feed_forward(tokens, cotangent, contexts, outputs, vec, up_bias, feed, place, blocks):
    length, width = tokens.shape
    tensor = blocks.tensor
    feed, tops = feed
    part = feed.shape[-1]
    groups = len(contexts)
    chunk = min(256, length)

    def body(place_ref, x_ref, vec_ref, ub_ref, *refs):
        c_refs, o_refs, refs = refs[:groups], refs[groups : 2 * groups], refs[2 * groups :]
        cot_hbm, feed_hbm, norm_hbm, inv_ref, hidt_hbm, slope_ref, out_hbm, low_hbm, keep, send, sums_ref, *refs = refs
        w, act, hidden, norm, hidt, acc, out, norm_low, low, errt, cot, stage, feed_sems, sems, store_sems = refs
        s = pl.program_id(0)
        cot_copy = pltpu.make_async_copy(cot_hbm, cot, sems.at[0])
        early = [pltpu.make_async_copy(a, b, sems.at[1 + n]) for n, (a, b) in enumerate([(norm_low, norm_hbm), (hidt, hidt_hbm)])]
        late = [pltpu.make_async_copy(a, b, sems.at[3 + n]) for n, (a, b) in enumerate([(out, out_hbm), (low, low_hbm)])]

        @pl.when(s == 0)
        def _():
            acc[...] = jnp.zeros_like(acc)
            for t in range(tensor):
                for copy in feed_loads(feed_hbm, w, feed_sems, blocks, t, tops):
                    copy.start()
            cot_copy.start()
            for c in range(0, length, chunk):
                rows = slice(c, c + chunk)
                attended = sum(nn(a[0, rows, :], b[0]) for a, b in zip(c_refs, o_refs)) + vec_ref[0:1, :]
                normed, inverse = layer_norm(x_ref[rows, :].astype(F32) + attended)
                norm[rows, :] = normed
                norm_low[rows, :] = normed.astype(BF)
                inv_ref[rows, :] = inverse
                first_out = normed * vec_ref[1:2, :] + vec_ref[2:3, :]
                hidden[rows, :] = first_out.astype(BF)
                hidt[:, rows] = first_out.T.astype(BF)
            for copy in early:
                copy.start()

        @pl.when(s < tensor)
        def _():
            for copy in feed_loads(feed_hbm, w, feed_sems, blocks, s, tops):
                copy.wait()
            rows_of = [slice(r, r + chunk) for r in range(0, length, chunk)]
            pre = nn(hidden[rows_of[0], :], w[s, 0])
            for n, rows in enumerate(rows_of):
                following = nn(hidden[rows_of[n + 1], :], w[s, 0]) if n + 1 < len(rows_of) else None
                pre = pre + ub_ref[pl.ds(s, 1), :]
                phi = 0.5 * (1.0 + lax.erf(pre * (1.0 / math.sqrt(2.0))))
                some = (pre * phi).astype(BF)
                act[s, rows, :] = some
                density = jnp.exp(-0.5 * pre * pre) * (1.0 / math.sqrt(2.0 * math.pi))
                slope_ref[0, rows, :] = (phi + pre * density).astype(BF)
                branch = nt(some, w[s, 1])
                acc[rows, :] += branch
                pre = following

        @pl.when(s == tensor - 1)
        def _():
            cot_copy.wait()
            totals = jnp.zeros((8, width), F32)
            for c in range(0, length, chunk):
                rows = slice(c, c + chunk)
                first_out = norm[rows, :] * vec_ref[1:2, :] + vec_ref[2:3, :]
                normed, inverse = layer_norm(first_out + (acc[rows, :] + vec_ref[3:4, :]))
                out[rows, :] = (normed * vec_ref[4:5, :] + vec_ref[5:6, :]).astype(BF)
                upstream = cot[rows, :].astype(F32)
                error = norm_backward(upstream * vec_ref[4:5, :], normed, inverse)
                low[rows, :] = error.astype(BF)
                errt[:, rows] = error.T.astype(BF)
                sums = [jnp.sum(a, axis=0, keepdims=True) for a in (error, upstream * normed, upstream)]
                totals += jnp.concatenate(sums + [jnp.zeros((5, width), F32)], axis=0)
            sums_ref[...] = totals
            for copy in late:
                copy.start()

        @pl.when(s >= tensor)
        def _():
            t = s - tensor
            slot = lax.rem(t, 2)

            @pl.when(t >= 2)
            def _():
                blocks.stores(place_ref, t - 2, stage.at[slot], keep, send, store_sems.at[slot], "wait")

            stage[slot] = nn(errt[...], act[t]).astype(BF).reshape(-1, blocks.rows, part)
            blocks.stores(place_ref, t, stage.at[slot], keep, send, store_sems.at[slot], "start")

        @pl.when(s == 2 * tensor - 1)
        def _():
            for last in range(max(tensor - 2, 0), tensor):
                blocks.stores(place_ref, last, stage.at[last % 2], keep, send, store_sems.at[last % 2], "wait")
            for copy in early + late:
                copy.wait()

    block_out = (blocks.n // 2, blocks.rows, part)
    wide = (length, width)
    return call(
        body, (2 * tensor,), [place],
        [(a, once(a.shape)) for a in (tokens, vec, up_bias)] + [at_index(a, i) for a, i in (*contexts, *outputs)] + [(cotangent, ANY), (feed, ANY)],
        [
            (wide, BF, ANY), ((length, 1), F32, once((length, 1))), ((width, length), BF, ANY),
            ((tensor, length, part), BF, pl.BlockSpec((1, length, part), lambda s, *_: (jnp.minimum(s, tensor - 1), 0, 0))),
            (wide, BF, ANY), (wide, BF, ANY), (block_out, BF, ANY), (block_out, BF, ANY), ((8, width), F32, once((8, width))),
        ],
        [
            pltpu.VMEM((tensor, 2, width, part), BF), pltpu.VMEM((tensor, length, part), BF), pltpu.VMEM(wide, BF), pltpu.VMEM(wide, F32),
            pltpu.VMEM((width, length), BF), pltpu.VMEM(wide, F32), pltpu.VMEM(wide, BF), pltpu.VMEM(wide, BF), pltpu.VMEM(wide, BF),
            pltpu.VMEM((width, length), BF), pltpu.VMEM(wide, BF), pltpu.VMEM((2, width // blocks.rows, blocks.rows, part), BF),
            pltpu.SemaphoreType.DMA((2, blocks.n)), pltpu.SemaphoreType.DMA((6,)), pltpu.SemaphoreType.DMA((2, blocks.n // tensor)),
        ],
        (2 * length * width * (width + 3 * tensor * part), 30 * length * width + 4 * length * tensor * part), "feed_forward",
    )


def feed_backward(err_low, slope, hidden_t, normed_one, inverse_one, vec, outputs, feed, place, blocks):
    length, width = err_low.shape
    tensor = blocks.tensor
    feed, tops = feed
    part = feed.shape[-1]
    groups = len(outputs)
    chunk = min(256, length)
    inner = outputs[0][0].shape[1]

    def body(place_ref, e_ref, s_ref, h_ref, i1_ref, vec_ref, *refs):
        o_refs, refs = refs[:groups], refs[groups:]
        n1_hbm, feed_hbm, keep, send, up_sums, err_hbm, errt_hbm, sums_ref, *refs = refs
        dctx_hbm, refs = refs[:groups], refs[groups:]
        w, acc, n1, err, errt, dctx, stage, low, feed_sems, sems, out_sems, store_sems = refs
        t = pl.program_id(0)
        slot = lax.rem(t, 2)
        inputs = [pltpu.make_async_copy(n1_hbm, n1, sems.at[0])]

        @pl.when(t == 0)
        def _():
            acc[...] = jnp.zeros_like(acc)
            for k in range(tensor):
                for copy in feed_loads(feed_hbm, w, feed_sems, blocks, k, tops[::-1]):
                    copy.start()
            for copy in inputs:
                copy.start()

        for copy in feed_loads(feed_hbm, w, feed_sems, blocks, t, tops[::-1]):
            copy.wait()
        span = min(512, length)
        rows_of = [slice(r, r + span) for r in range(0, length, span)]
        product = nn(e_ref[rows_of[0], :], w[t, 0])
        total = jnp.zeros((1, part), F32)
        for n, rows in enumerate(rows_of):
            following = nn(e_ref[rows_of[n + 1], :], w[t, 0]) if n + 1 < len(rows_of) else None
            grad = product * s_ref[0, rows, :].astype(F32)
            total += jnp.sum(grad, axis=0, keepdims=True)
            some = grad.astype(BF)
            low[rows, :] = some
            acc[rows, :] += nt(some, w[t, 1])
            product = following
        up_sums[pl.ds(t, 1), :] = total

        @pl.when(t >= 2)
        def _():
            blocks.stores(place_ref, t - 2, stage.at[slot], keep, send, store_sems.at[slot], "wait")

        stage[slot] = nn(h_ref[...], low[...]).astype(BF).reshape(-1, blocks.rows, part)
        blocks.stores(place_ref, t, stage.at[slot], keep, send, store_sems.at[slot], "start")

        @pl.when(t == tensor - 1)
        def _():
            for copy in inputs:
                copy.wait()
            totals = jnp.zeros((8, width), F32)
            copies = []
            for n, c in enumerate(range(0, length, chunk)):
                rows = slice(c, c + chunk)
                err_in = e_ref[rows, :].astype(F32) + acc[rows, :]
                normed = n1[rows, :].astype(F32)
                error = norm_backward(err_in * vec_ref[1:2, :], normed, i1_ref[rows, :])
                err[rows, :] = error
                turned = error.T.astype(BF)
                errt[:, rows] = turned
                some = pl.ds(c, chunk)
                copies += [
                    pltpu.make_async_copy(err.at[some, :], err_hbm.at[some, :], out_sems.at[n, 0]),
                    pltpu.make_async_copy(errt.at[:, some], errt_hbm.at[:, some], out_sems.at[n, 1]),
                ]
                for g in range(groups):
                    dctx[g, :, rows] = nn(o_refs[g][0], turned).astype(BF)
                    copies.append(pltpu.make_async_copy(dctx.at[g, :, some], dctx_hbm[g].at[:, some], out_sems.at[n, 2 + g]))
                for copy in copies[-2 - groups :]:
                    copy.start()
                sums = [jnp.sum(a, axis=0, keepdims=True) for a in (error, err_in * normed, err_in)]
                totals += jnp.concatenate(sums + [jnp.zeros((5, width), F32)], axis=0)
            sums_ref[...] = totals
            for last in range(max(tensor - 2, 0), tensor):
                blocks.stores(place_ref, last, stage.at[last % 2], keep, send, store_sems.at[last % 2], "wait")
            for copy in copies:
                copy.wait()

    block_out = (blocks.n // 2, blocks.rows, part)
    wide = (length, width)
    return call(
        body, (tensor,), [place],
        [
            (err_low, once(wide)), (slope, pl.BlockSpec((1, length, part), lambda t, *_: (t, 0, 0))), (hidden_t, once((width, length))),
            (inverse_one, once((length, 1))), (vec, once(vec.shape)), *[at_index(o, i) for o, i in outputs],
            (normed_one, ANY), (feed, ANY),
        ],
        [
            (block_out, BF, ANY), (block_out, BF, ANY), ((8, part), F32, once((8, part))), (wide, F32, ANY), ((width, length), BF, ANY),
            ((8, width), F32, once((8, width))), *[((inner, length), BF, ANY) for _ in outputs],
        ],
        [
            pltpu.VMEM((tensor, 2, width, part), BF), pltpu.VMEM(wide, F32), pltpu.VMEM(wide, BF), pltpu.VMEM(wide, F32),
            pltpu.VMEM((width, length), BF), pltpu.VMEM((groups, inner, length), BF), pltpu.VMEM((2, width // blocks.rows, blocks.rows, part), BF), pltpu.VMEM((length, part), BF),
            pltpu.SemaphoreType.DMA((2, blocks.n)), pltpu.SemaphoreType.DMA((2,)), pltpu.SemaphoreType.DMA((length // chunk, 2 + groups)),
            pltpu.SemaphoreType.DMA((2, blocks.n // tensor)),
        ],
        (2 * length * width * (width + 3 * tensor * part), 30 * length * width + 2 * length * tensor * part), "feed_backward",
    )


def finish(first_terms, other_terms, rows, groups, column, cols):
    width = groups * HD
    n = len(first_terms)

    def body(i_ref, *refs):
        (q_ref, k_ref, v_ref, o_ref, qb_ref, vb_ref), terms = refs[2 * n :], refs[: 2 * n]
        sums = [sum(r[0].astype(F32) for r in part) for part in (terms[:n], terms[n:])]
        biases = []
        for c in range(groups):
            block = sums[0] if c == 0 else sums[1][:, (c - 1) * PACK : c * PACK]
            for j, out in enumerate((q_ref, k_ref, v_ref)):
                out[:, c * HD : (c + 1) * HD] = block[:rows, j * HD : (j + 1) * HD]
            o_ref[c * HD : (c + 1) * HD, :] = block[:rows, 2 * HD :].T[HD:]
            biases.append(block[rows : rows + 1])
        biases = jnp.concatenate(biases + [jnp.zeros((8 - groups, PACK), F32)], axis=0)
        for out, start in ((qb_ref, 0), (vb_ref, 2 * HD)):
            out[...] = pltpu.roll(biases, lax.rem(2 * PACK - start - i_ref[0], PACK), 1)[:groups, :cols]

    def block(array):
        return array, pl.BlockSpec((1, *array.shape[1:]), lambda *_: (0, 0, 0))

    shapes = [(rows, width)] * 3 + [(width, rows), (groups, cols), (groups, cols)]
    return call(
        body, (1,), [column.reshape(1)], [block(t) for t in (*first_terms, *other_terms)],
        [(shape, F32, full(shape)) for shape in shapes], [], (1e6, 2 * n * rows * PACK * 6), "finish",
    )


def local(
    tokens, query_weight, key_weight, value_weight, output_weight, query_bias, value_bias,
    output_bias, first_gain, first_shift, up_weight, up_bias, down_weight, down_bias,
    second_gain, second_shift, cotangent,
):
    dp, tensor = lax.axis_size("dp"), lax.axis_size("tensor")
    count = dp * tensor
    rows = query_weight.shape[0]
    width = rows * dp
    groups = query_weight.shape[1] // HD
    heads = groups * tensor
    slot = output_bias.shape[0]
    cols = query_bias.shape[1]
    me = lax.axis_index(AXES)
    place, devs, owners = position_table(me, count), device_table(me, count), owner_table(me, count)
    direct = rows % 16 == 0

    vectors = jnp.stack([output_bias, first_gain, first_shift, down_bias, second_gain, second_shift])
    extra = small_block(vectors, query_bias, value_bias, up_bias)
    output_turned = output_weight.T
    by_group = [
        jnp.concatenate([w[:, c * HD : (c + 1) * HD] for w in (query_weight, key_weight, value_weight, output_turned)], axis=1)
        for c in range(groups)
    ]
    first, second = (Gathering(jnp.concatenate(blocks, axis=axis), count) for blocks, axis in (([by_group[0], extra], 0), (by_group[1:], 1)))
    feed = lax.all_gather(jnp.concatenate([up_weight, down_weight.T], axis=0), AXES, axis=0, tiled=False)
    tokens_t, place, devs, owners, owner_column, dev_column = wave(
        [first], tokens.T, place, devs, owners, owners.reshape(count, 1), devs.reshape(count, 1)
    )
    wave([first, second])
    wave([first])
    direct = rows % 16 == 0
    small_set = (first.pieces, rows) if direct else ([jnp.concatenate([p[:, rows:] for p in first.pieces], axis=0)], 0)
    if direct:
        blocks = Blocks(count, rows, tensor)
        block_place, block_devs = place, devs
    else:
        blocks = Blocks(tensor, width, tensor)
        block_place = block_devs = jnp.arange(tensor, dtype=jnp.int32)

    def by_matrix(ordered):
        return [ordered.reshape(dp, tensor, rows, -1).transpose(1, 0, 2, 3).reshape(tensor, width, -1)]

    def ready(gathering):
        if direct:
            return gathering.pieces
        return by_matrix(jnp.take(jnp.concatenate(gathering.pieces, axis=0)[:, :rows], gathered_place(me, count), axis=0))

    def scattering(keep, send, more=None):
        if not direct:
            stacked = jnp.concatenate([keep, send], axis=0)
            parts = [stacked[:, :width].reshape(tensor, dp, rows, -1).transpose(1, 0, 2, 3).reshape(count, rows, -1)]
            if stacked.shape[1] > width:
                parts.append(jnp.tile(stacked[:, width:], (dp, 1, 1)))
            stacked = jnp.take(jnp.concatenate(parts, axis=1), owners, axis=0)
            if more is not None:
                stacked = jnp.concatenate([stacked, more], axis=1)
            keep, send = stacked[: count // 2], stacked[count // 2 :]
        return Scattering(keep, send, count)

    tokens_now = wave([second], tokens)
    vec, bias_pack, up_rows = unpack_small(*small_set, dev_column, slot, cols, width, tensor)
    first_set = ready(first)
    one = attention_forward(tokens_now, first_set, bias_pack, 0, block_devs, blocks)
    tokens_now = wave([second], tokens, one[4])[0]
    second_set = ready(second)
    others = attention_forward(tokens_now, second_set, bias_pack, 1, block_devs, blocks)
    weights = [(first_set, 0)] + [(second_set, c * PACK) for c in range(groups - 1)]
    forward = [(one, 0)] + [(others, c) for c in range(groups - 1)]
    if not direct:
        feed = jnp.concatenate([by_matrix(feed[:, :rows])[0], by_matrix(feed[:, rows:])[0]], axis=1)
    feed = (feed, (0, feed.shape[1] // 2))
    outputs = [(f[5], i) for f, i in forward]
    normed_one, inverse_one, hidden_t, slope, layer_out, err_two_low, down_keep, down_send, sums_two = feed_forward(
        tokens, cotangent, [(f[2], i) for f, i in forward], outputs, vec, up_rows, feed, block_place, blocks
    )
    grad_down = scattering(down_keep, down_send)
    err_two_low = wave([grad_down], err_two_low)
    up_keep, up_send, up_sums, err_one, err_one_t, sums_one, *context_grads = feed_backward(
        err_two_low, slope, hidden_t, normed_one, inverse_one, vec, outputs, feed, block_place, blocks
    )
    grad_up = scattering(up_keep, up_send)
    small = (sums_one, sums_two, up_sums, owner_column)
    if not direct:
        small = pack_small_grads(*small, slot, cols, tensor)
    column = lax.axis_index("dp") * cols
    backward = [None] * groups
    token_sum = err_one
    last, packed, moving = (err_one_t,), None, [grad_down, grad_up]
    for c in reversed(range(groups)):
        carries = c == groups - 1
        options = {}
        if c and direct:
            options = dict(into=packed, lane=(c - 1) * PACK, high=rows + 2 * EXTRA, wide=(groups - 1) * PACK)
        if c:
            context_grad = wave(moving, context_grads[c], since=last)
        backward[c] = attention_backward(
            tokens_t, err_one_t, *forward[c], context_grad, token_sum, weights[c], block_place, block_devs, blocks,
            (small, slot, cols) if direct and carries else None, **options,
        )
        token_sum = backward[c][2]
        last = (token_sum,)
        if c and direct:
            packed = backward[c][:2]
        if c == 1:
            if direct:
                others = scattering(*packed)
            else:
                packed = [jnp.concatenate([backward[g][i] for g in range(1, groups)], axis=2) for i in range(2)]
                others = scattering(*packed, jnp.pad(small, ((0, 0), (0, 0), ((groups - 2) * PACK, 0))))
            grad_down.terms, grad_up.terms = wave([others], grad_down.terms, grad_up.terms)
            ahead = [*grad_down.outgoing(), *grad_up.outgoing()]
            wave([grad_down, grad_up])
            others.looked_at(*ahead)
            context_grad = wave([others], context_grads[0])
    zero = scattering(*backward[0][:2])
    while grad_down.phases:
        wave([grad_down])
    grad_up.terms, grad_down.terms, others.terms = wave([zero], grad_up.terms, grad_down.terms, others.terms)
    wave([others])
    wave([zero, grad_up])
    while grad_up.phases:
        wave([grad_up])
    wave([zero])
    grad_up.terms, zero.terms = wave([others], grad_up.terms, zero.terms)
    grad_up, grad_down = grad_up.result(), grad_down.result()
    while zero.phases or others.phases:
        grad_up, grad_down = wave([zero, others], grad_up, grad_down)
    tail = sum(t[0, rows + EXTRA :, (groups - 2) * PACK :].astype(F32) for t in others.terms)
    if direct:
        out_query, out_key, out_value, out_output, *bias_out = finish(zero.terms, others.terms, rows, groups, column, cols)
    else:
        results = [zero.result()] + jnp.split(others.result()[: rows + EXTRA], groups - 1, axis=1)
        bias_rows = jnp.stack([r[rows] for r in results])
        bias_out = [lax.dynamic_slice(bias_rows, (0, start + column), (groups, cols)) for start in (0, 2 * HD)]
        out = jnp.stack([r[:rows] for r in results], axis=1).reshape(rows, groups, 4, HD)
        out_query, out_key, out_value, out_output = (out[:, :, i].reshape(rows, groups * HD) for i in range(4))
        out_output = out_output.T
    vecs = [tail[v // 2, (v % 2) * LANES : (v % 2) * LANES + slot] for v in range(6)]
    return (
        layer_out,
        token_sum,
        out_query,
        out_key,
        out_value,
        out_output,
        bias_out[0],
        bias_out[1],
        vecs[0],
        vecs[1],
        vecs[2],
        grad_up,
        tail[: up_bias.shape[0], 64 : 64 + cols],
        grad_down.T,
        vecs[3],
        vecs[4],
        vecs[5],
    )


def solution(mesh):
    both, cross, turned, vector = P(AXES, None), P("dp", "tensor"), P("tensor", "dp"), P(AXES)
    return jax.shard_map(
        local,
        mesh=mesh,
        in_specs=(
            both, cross, cross, cross, turned, turned, turned, vector, vector, vector,
            cross, turned, turned, vector, vector, vector, both,
        ),
        out_specs=(
            both, both, cross, cross, cross, turned, turned, turned, vector, vector, vector,
            cross, turned, turned, vector, vector, vector,
        ),
        check_vma=False,
    )
```

```python
import functools
import math

import jax
import jax.numpy as jnp
import numpy as np
from jax import lax
from jax.experimental import pallas as pl
from jax.experimental.pallas import tpu as pltpu
from jax.sharding import PartitionSpec as P

HD = 64
L = 1024
PACK = 4 * HD
EPSILON = 1e-12
AXES = ("dp", "tensor")
EXTRA = 16
LANES = 128
BF = jnp.bfloat16
F32 = jnp.float32
SDS = jax.ShapeDtypeStruct
ANY = pl.BlockSpec(memory_space=pl.ANY)


def nn(a, b):
    return lax.dot_general(a, b, (((1,), (0,)), ((), ())), preferred_element_type=F32)


def nt(a, b):
    return lax.dot_general(a, b, (((1,), (1,)), ((), ())), preferred_element_type=F32)


def full(shape):
    return pl.BlockSpec(shape, lambda *_: (0,) * len(shape))


def once(shape):
    return pl.BlockSpec(shape, lambda *_: (0,) * len(shape), pipeline_mode=pl.Buffered(1))


def at_index(array, i):
    shape = (1, *array.shape[1:])
    return array, pl.BlockSpec(shape, lambda *_: (i,) + (0,) * (len(shape) - 1), pipeline_mode=pl.Buffered(1))


def call(body, grid, tables, ins, outs, scratch, cost, name, aliases={}):
    flops, moved = cost
    return pl.pallas_call(
        body,
        grid_spec=pltpu.PrefetchScalarGridSpec(
            num_scalar_prefetch=len(tables),
            grid=grid,
            in_specs=[s for _, s in ins],
            out_specs=[s for _, _, s in outs],
            scratch_shapes=scratch,
        ),
        out_shape=[SDS(s, d) for s, d, _ in outs],
        compiler_params=pltpu.CompilerParams(
            dimension_semantics=("arbitrary",) * len(grid), vmem_limit_bytes=60 * 2**20
        ),
        cost_estimate=pl.CostEstimate(flops=int(flops * 0.01), bytes_accessed=int(moved * 0.01), transcendentals=0),
        name=name,
        input_output_aliases=aliases,
    )(*tables, *[a for a, _ in ins])


def exchange(array, differs, count):
    even, odd = differs if isinstance(differs, tuple) else (differs, differs)
    return lax.ppermute(array, AXES, [(d, d ^ (odd if d & 1 else even)) for d in range(count)])


def phases_of(count):
    bits = count.bit_length() - 1
    return [*((k, 1) for k in range(bits - 1, 4, -1)), (3, 2), (1, 2), (0, 1)]


def scatter_phases_of(count):
    bits = count.bit_length() - 1
    return [[1], [(2, 4)], [(4, 2)], [8, 16, 24], *([1 << k] for k in range(5, bits))]


class Gathering:
    def __init__(self, block, count):
        self.pieces, self.count, self.phases = [block[None]], count, phases_of(count)
        while self.phases[0][1] == 1:
            self.move(self.outgoing())

    def outgoing(self):
        if self.phases[0] != (0, 1) and len(self.pieces) > 1:
            self.pieces = [jnp.concatenate(self.pieces, axis=0)]
        return self.pieces

    def move(self, pieces):
        low, bits = self.phases.pop(0)
        self.pieces = self.pieces + [exchange(p, k << low, self.count) for k in range(1, 1 << bits) for p in pieces]


class Scattering:
    def __init__(self, keep, send, count):
        self.terms, self.sends, self.count, self.phases = [keep], [send], count, scatter_phases_of(count)
        self.size = keep.shape[0]

    def looked_at(self, *since):
        self.terms = lax.optimization_barrier((self.terms, since))[0]

    def outgoing(self):
        if self.sends is None:
            parts = 1 + len(self.phases[0])
            size = self.size // parts
            self.sends = [sum(t[k * size : (k + 1) * size].astype(F32) for t in self.terms).astype(BF) for k in range(1, parts)]
            self.size = size
        return self.sends

    def move(self, sends):
        self.terms = self.terms + [exchange(p, k, self.count) for k, p in zip(self.phases.pop(0), sends)]
        self.sends = None

    def result(self):
        return sum(t[0].astype(F32) for t in self.terms)


def wave(moves, *beside, since=()):
    moves = [m for m in moves if m.phases]
    for m in moves:
        if since and isinstance(m, Scattering):
            m.looked_at(*since)
    outgoing, beside = lax.optimization_barrier(([m.outgoing() for m in moves], beside))
    for m, array in zip(moves, outgoing):
        m.move(array)
    return beside[0] if len(beside) == 1 else beside


def fields_of(count):
    top, fields = count.bit_length() - 1, []
    for low, bits in phases_of(count)[::-1]:
        top -= bits
        fields.append((low, bits, top))
    return fields


def position_table(me, count):
    bits = count.bit_length() - 1
    device = jnp.arange(count, dtype=jnp.int32)
    differs = device ^ me
    one, two = (differs >> 1) & 1, (differs >> 2) & 1
    odd = (device & 1) == 1
    place = ((differs & 1) << (bits - 1)) | (jnp.where(odd, two, one) << (bits - 2)) | (jnp.where(odd, one, two) << (bits - 3))
    place = place | (((differs >> 3) & 3) << (bits - 5))
    for k in range(5, bits):
        place = place | (((differs >> k) & 1) << (bits - 1 - k))
    return place


def owner_table(me, count):
    bits = count.bit_length() - 1
    place = jnp.arange(count, dtype=jnp.int32)
    core, upper, lower = ((place >> (bits - k)) & 1 for k in (1, 2, 3))
    odd = ((me ^ core) & 1) == 1
    differs = core | (jnp.where(odd, lower, upper) << 1) | (jnp.where(odd, upper, lower) << 2) | (((place >> (bits - 5)) & 3) << 3)
    for k in range(5, bits):
        differs = differs | (((place >> (bits - 1 - k)) & 1) << k)
    return differs ^ me


def gathered_place(me, count):
    differs = jnp.arange(count, dtype=jnp.int32) ^ me
    return sum(((differs >> low) & ((1 << bits) - 1)) << at for low, bits, at in fields_of(count))


def device_table(me, count):
    place = jnp.arange(count, dtype=jnp.int32)
    return sum(((place >> at) & ((1 << bits) - 1)) << low for low, bits, at in fields_of(count)) ^ me


class Blocks:
    def __init__(self, n, rows, tensor):
        self.n, self.rows, self.tensor = n, rows, tensor

    def at(self, d):
        return lax.rem(d, self.tensor), pl.multiple_of(lax.div(d, self.tensor) * self.rows, self.rows)

    def loads(self, devs, pieces, target, sems, lane=0, top=0):
        out, p = [], 0
        flat = len(target.shape) == 2
        width = target.shape[-1] // (self.tensor if flat else 1)
        for piece in pieces:
            for j in range(piece.shape[0]):
                t, row = self.at(devs[p])
                rows = pl.ds(row, self.rows)
                into = target.at[rows, pl.ds(pl.multiple_of(t * width, width), width)] if flat else target.at[t, rows, :]
                out.append(pltpu.make_async_copy(
                    piece.at[j, pl.ds(top, self.rows), pl.ds(lane, width)], into, sems.at[p]
                ))
                p += 1
        return out

    def stores(self, place, t, stage, keep, send, sems, action, lane=0):
        half = self.n // 2
        lanes = pl.ds(lane, stage.shape[-1])
        for i in range(self.n // self.tensor):
            p = place[i * self.tensor + t]
            kept = pltpu.make_async_copy(stage.at[i], keep.at[lax.rem(p, half), :, lanes], sems.at[i])
            if action == "wait":
                kept.wait()
            else:
                sent = pltpu.make_async_copy(stage.at[i], send.at[lax.rem(p, half), :, lanes], sems.at[i])
                pl.when(p < half)(kept.start)
                pl.when(p >= half)(sent.start)


def spread_constants(slot, cols, width):
    lane = np.arange(width)
    a, c = np.zeros((LANES, width), np.float32), np.zeros((LANES, width), np.float32)
    for j in range(slot):
        a[j] = lane % slot == j
    for j in range(cols):
        a[32 + j] = lane % cols == j
        c[64 + j] = lane % cols == j
    return jnp.asarray(a, BF), jnp.asarray(c, BF)


def small_masks(device, slot, cols, width, tensor):
    n = device.shape[0]
    shift = tensor.bit_length() - 1
    row = lax.broadcasted_iota(jnp.int32, (n, EXTRA, width), 1)
    lane = lax.broadcasted_iota(jnp.int32, (n, EXTRA, width), 2)
    i, t = device >> shift, device & (tensor - 1)
    in_head = (lane & (HD - 1)) >> (cols.bit_length() - 1)
    groups = width // HD // tensor
    vector = (row < 9) & (lane >= device * slot) & (lane < (device + 1) * slot)
    bias = (row >= 9) & (row < 9 + groups) & ((lane >> 6) == t * groups + row - 9) & (in_head == i)
    hidden = (row < width // HD) & ((lane >> 6) == row) & (in_head == i)
    return vector | bias, hidden, t


def unpack_small(pieces, top, device, slot, cols, width, tensor):
    n = device.shape[0]
    groups = width // HD // tensor
    spread_a, spread_c = spread_constants(slot, cols, width)

    def body(d_ref, a_ref, c_ref, *refs):
        piece_refs, (vec_ref, bias_ref, up_ref, x_s, sems) = refs[: len(pieces)], refs[len(pieces) :]
        copies, at = [], 0
        for j, piece in enumerate(piece_refs):
            size = piece.shape[0]
            copies.append(pltpu.make_async_copy(piece.at[:, pl.ds(top, EXTRA), :], x_s.at[pl.ds(at, size)], sems.at[j]))
            at += size
        for copy in copies:
            copy.start()
        d = d_ref[...].reshape(n, 1, 1)
        main, hidden, t = small_masks(d, slot, cols, width, tensor)
        for copy in copies:
            copy.wait()
        x = x_s[...].reshape(n * EXTRA, 2 * LANES)
        bias_ref[...] = jnp.zeros_like(bias_ref)
        for half in range(2):
            y = nn(x[:, half * LANES : (half + 1) * LANES], a_ref[...]).reshape(n, EXTRA, width)
            total = jnp.sum(jnp.where(main, y, 0.0), axis=0)
            for v in range(half, 6, 2):
                r = v // 2
                vec_ref[v : v + 1, :] = total[r : r + 1] + total[3 + r : 4 + r] + total[6 + r : 7 + r]
            row = jnp.sum(total[9:EXTRA], axis=0, keepdims=True)
            for head in range(groups * tensor):
                at = half * 2 * HD
                bias_ref[head % groups, head // groups : head // groups + 1, at : at + HD] = row[:, head * HD : (head + 1) * HD]
        y = nn(x[:, :LANES], c_ref[...]).reshape(n, EXTRA, width)
        y = jnp.where(hidden, y, 0.0)
        for k in range(tensor):
            picked = jnp.sum(jnp.where(t == k, y, 0.0), axis=0)
            up_ref[k : k + 1, :] = jnp.sum(picked, axis=0, keepdims=True)

    row8, bias = (8, width), (groups, tensor, PACK)
    return call(
        body, (1,), [],
        [(a, full(a.shape)) for a in (device, spread_a, spread_c)] + [(p, ANY) for p in pieces],
        [(row8, F32, full(row8)), (bias, F32, full(bias)), (row8, F32, full(row8))],
        [pltpu.VMEM((n, EXTRA, PACK), BF), pltpu.SemaphoreType.DMA((len(pieces),))],
        (3 * 2 * n * EXTRA * LANES * width, n * EXTRA * PACK * 2), "unpack_small",
    )


def spread_small_grads(one_ref, two_ref, u_ref, d_ref, a_ref, c_ref, slot, cols, tensor):
    n, width = d_ref.shape[0], one_ref.shape[-1]
    d = d_ref[...].reshape(n, 1, 1)
    main, hidden, t = small_masks(d, slot, cols, width, tensor)
    row = lax.broadcasted_iota(jnp.int32, (EXTRA, width), 0)
    halves = []
    for half in range(2):
        z = jnp.zeros((EXTRA, width), F32)
        for v in range(half, 6, 2):
            z = jnp.where(row == v // 2, (one_ref, two_ref)[v // 3][v % 3 : v % 3 + 1, :], z)
        spread = jnp.where(main, z[None], 0.0).astype(BF).reshape(n * EXTRA, width)
        halves.append(nt(spread, a_ref[...]))
    z = jnp.zeros((n, EXTRA, width), F32)
    for k in range(tensor):
        z = jnp.where(t == k, u_ref[k : k + 1, :].reshape(1, 1, width), z)
    spread = jnp.where(hidden, z, 0.0).astype(BF).reshape(n * EXTRA, width)
    halves[0] = halves[0] + nt(spread, c_ref[...])
    return jnp.concatenate(halves, axis=1).astype(BF).reshape(n, EXTRA, 2 * LANES)


def pack_small_grads(one, two, up, device, slot, cols, tensor):
    n, width = device.shape[0], one.shape[-1]
    spread_a, spread_c = spread_constants(slot, cols, width)

    def body(one_ref, two_ref, u_ref, d_ref, a_ref, c_ref, out_ref):
        out_ref[...] = spread_small_grads(one_ref, two_ref, u_ref, d_ref, a_ref, c_ref, slot, cols, tensor)

    shape = (n, EXTRA, PACK)
    return call(
        body, (1,), [],
        [(a, full(a.shape)) for a in (one, two, up, device, spread_a, spread_c)],
        [(shape, BF, full(shape))], [], (3 * 2 * n * EXTRA * LANES * width, 2 * n * EXTRA * PACK), "pack_small",
    )[0]


def three_parts(vector):
    high = lax.reduce_precision(vector, 8, 7)
    middle = lax.reduce_precision(vector - high, 8, 7)
    lowest = lax.reduce_precision(vector - high - middle, 8, 7)
    return jnp.stack([high, middle, lowest]).astype(BF)


def small_block(vectors, query_bias, value_bias, up_bias):
    slot = vectors.shape[1]
    parts = three_parts(vectors).reshape(9, 2, slot)

    def placed(array, row, lane):
        return jnp.pad(array, ((row, EXTRA - row - array.shape[0]), (lane, PACK - lane - array.shape[1])))

    return (
        placed(parts[:, 0], 0, 0) + placed(parts[:, 1], 0, LANES) + placed(query_bias, 9, 32)
        + placed(value_bias, 9, LANES + 32) + placed(up_bias, 0, 64)
    )


def attention_forward(tokens, pieces, bias, base, devs, blocks):
    length, width = tokens.shape
    heads = blocks.tensor
    inner = heads * HD
    groups = pieces[0].shape[-1] // PACK

    def body(devs_ref, x_ref, b_ref, *refs):
        piece_refs, (qkv_ref, e_ref, ctx_ref, ctxt_ref, inv_ref, ot_ref, w, ot_s, vt_s, sems) = refs[: len(pieces)], refs[len(pieces) :]
        c, t = pl.program_id(0), pl.program_id(1)

        loads = [blocks.loads(devs_ref, piece_refs, w.at[g], sems.at[g], g * PACK) for g in range(groups)]

        @pl.when((c == 0) & (t == 0))
        def _():
            for copies in loads:
                for copy in copies:
                    copy.start()
            vt_s[HD:, :] = jnp.ones((HD, length), BF)

        for g in range(groups):
            @pl.when((c == g) & (t == 0))
            def _():
                for copy in loads[g]:
                    copy.wait()

        wt = w[c, t]
        col = lax.broadcasted_iota(jnp.int32, (1, PACK), 1)
        pre = nn(x_ref[...], wt) + b_ref[base + c, pl.ds(t, 1), :]
        low = (pre * jnp.where(col < HD, 1.0 / math.sqrt(HD), 1.0)).astype(BF)
        qkv_ref[0] = low
        q, k = low[:, :HD], low[:, HD : 2 * HD]
        vt_s[:HD, :] = low[:, 2 * HD :].T[:HD]
        square = pre[:, : 2 * HD] * pre[:, : 2 * HD]
        pick = lax.broadcasted_iota(jnp.int32, (2 * HD, LANES), 0) // HD == lax.broadcasted_iota(jnp.int32, (2 * HD, LANES), 1)
        norms = jnp.max(nn(square.astype(BF), pick.astype(BF)), axis=0, keepdims=True)
        bound = jnp.sqrt(norms[0, 0] * norms[0, 1]) * (1.1 / math.sqrt(HD))

        @pl.when(bound <= 40.0)
        def _():
            e_ref[0] = jnp.exp(nt(k, q)).astype(BF)

        @pl.when(jnp.logical_not(bound <= 40.0))
        def _():
            def some(j, _):
                at = pl.ds(pl.multiple_of(j * LANES, LANES), LANES)
                scores = nt(k, qkv_ref[0, at, :][:, :HD])
                e_ref[0, :, at] = jnp.exp(scores - jnp.max(scores, axis=0, keepdims=True)).astype(BF)
                return 0

            lax.fori_loop(0, length // LANES, some, 0)

        mixed = nn(vt_s[...], e_ref[0])
        inv = 1.0 / mixed[HD : HD + 1]
        inv_ref[0] = jnp.broadcast_to(inv, (8, length))
        ctxt_ref[0, pl.ds(t * HD, HD), :] = mixed[:HD] * inv
        ot_s[pl.ds(t * HD, HD), :] = wt[:, 2 * HD :].T[HD:].astype(F32)

        @pl.when(t == heads - 1)
        def _():
            ctx_ref[0] = ctxt_ref[0].T.astype(BF)
            ot_ref[0] = ot_s[...].astype(BF)

    by_head = lambda *s: pl.BlockSpec((1, *s), lambda c, t, *_: (c * heads + t, 0, 0))
    by_group = lambda *s: pl.BlockSpec((1, *s), lambda c, t, *_: (c, 0, 0))
    return call(
        body, (groups, heads), [devs],
        [(tokens, full(tokens.shape)), (bias, full(bias.shape))] + [(p, ANY) for p in pieces],
        [
            ((groups * heads, length, PACK), BF, by_head(length, PACK)),
            ((groups * heads, length, length), BF, by_head(length, length)),
            ((groups, length, inner), BF, by_group(length, inner)),
            ((groups, inner, length), F32, by_group(inner, length)),
            ((groups * heads, 8, length), F32, by_head(8, length)),
            ((groups, inner, width), BF, by_group(inner, width)),
        ],
        [pltpu.VMEM((groups, heads, width, PACK), BF), pltpu.VMEM((inner, width), F32), pltpu.VMEM((2 * HD, length), BF), pltpu.SemaphoreType.DMA((groups, blocks.n))],
        (groups * heads * (2 * length * width * PACK + 16 * length * length * HD), groups * heads * length * length * 2), "attention_forward",
    )


def attention_backward(tokens_t, err_t, forward, index, dctxt, total, weights, place, devs, blocks, more=None, into=None, lane=0, high=None, wide=PACK):
    width, length = tokens_t.shape
    pieces, piece_lane = weights
    chunk = min(256, length)
    qkv, e, ctx, ctxt, inv, _ = forward
    heads = blocks.tensor
    inner = heads * HD
    half = blocks.n // 2
    scale = 1.0 / math.sqrt(HD)
    rows, extra, given = blocks.rows, 0 if more is None else 6, 0 if into is None else 2
    high = high or blocks.rows + EXTRA
    tall = rows + EXTRA * (1 if more is None else 2)
    if more is not None:
        sums, slot, cols = more
        more = [*sums, *spread_constants(slot, cols, width)]

    def body(place_ref, devs_ref, qkv_ref, e_ref, inv_ref, ctxt_ref, dctxt_ref, xt_hbm, et_hbm, ctx_hbm, total_hbm, *refs):
        piece_refs, refs = refs[: len(pieces)], refs[len(pieces) :]
        more_ref, (keep_ref, send_ref, out_hbm, stage, bias, xt, et, ctx, d_ref, sum_s, w, sems, in_sems, w_sems, out_sems, *small) = refs[:extra], refs[extra + given :]
        keep_rows, send_rows = (r.at[:, pl.ds(0, tall), :] for r in (keep_ref, send_ref))
        t = pl.program_id(0)
        late = [pltpu.make_async_copy(a, b, in_sems.at[n]) for n, (a, b) in enumerate([(xt_hbm, xt), (et_hbm, et), (ctx_hbm.at[index], ctx), (total_hbm, sum_s)])]
        late += blocks.loads(devs_ref, piece_refs, w, w_sems, piece_lane)

        @pl.when(t == 0)
        def _():
            for copy in late:
                copy.start()
            if extra:
                small[0][...] = spread_small_grads(*more_ref, slot, cols, heads)

        q, k, v = qkv_ref[0, :, :HD], qkv_ref[0, :, HD : 2 * HD], qkv_ref[0, :, 2 * HD : 3 * HD]
        mine = pl.ds(t * HD, HD)
        dot = (dctxt_ref[mine, :].astype(F32) * inv_ref[0, :1, :]).astype(BF)
        delta = jnp.sum(dot.astype(F32) * ctxt_ref[0, mine, :], axis=0, keepdims=True)
        ee = e_ref[0]
        ds = (ee.astype(F32) * (nn(v, dot) - delta)).astype(BF)
        dv = nn(ee, dot.T)
        dk = nn(ds, q)
        dq = (nn(k.T, ds) * scale).T
        d = jnp.concatenate([dq, dk, dv, jnp.zeros_like(dv)], axis=1)
        bias[t] = jnp.broadcast_to(jnp.sum(d, axis=0, keepdims=True), (8, PACK))
        d_ref[:, pl.ds(pl.multiple_of(t * PACK, PACK), PACK)] = d.astype(BF)

        @pl.when(t == heads - 1)
        def _():
            for copy in late:
                copy.wait()
            outs = []
            for n, c in enumerate(range(0, length, chunk)):
                sum_s[c : c + chunk, :] += nt(d_ref[c : c + chunk, :], w[...])
                outs.append(pltpu.make_async_copy(sum_s.at[pl.ds(c, chunk), :], out_hbm.at[pl.ds(c, chunk), :], out_sems.at[n]))
                outs[-1].start()
            go = nn(et[...], ctx[...])
            for h in range(heads):
                if h % 2 == 0:
                    both = nn(xt[...], d_ref[:, h * PACK : (h + 2) * PACK])
                g = both[:, h % 2 * PACK : (h % 2 + 1) * PACK]
                low = jnp.concatenate([g[:, : 3 * HD], go[:, h * HD : (h + 1) * HD]], axis=1).astype(BF)
                row = jnp.concatenate([bias[h]] * (EXTRA // 8), axis=0).astype(BF)
                for i in range(width // rows):
                    stage[h, i, :rows, :] = low[i * rows : (i + 1) * rows]
                    stage[h, i, rows : rows + EXTRA, :] = row
                    if extra:
                        stage[h, i, rows + EXTRA :, :] = small[0][place_ref[i * heads + h]]
                blocks.stores(place_ref, h, stage.at[h], keep_rows, send_rows, sems.at[h], "start", lane)
            for h in range(heads):
                blocks.stores(place_ref, h, stage.at[h], keep_rows, send_rows, sems.at[h], "wait", lane)
            for copy in outs:
                copy.wait()

    by_head = lambda *s: pl.BlockSpec((1, *s), lambda t, *_: (index * heads + t, 0, 0))
    out = (half, high, wide)
    return call(
        body, (heads,), [place, devs],
        [
            (qkv, by_head(length, PACK)), (e, by_head(length, length)), (inv, by_head(8, length)),
            (ctxt, pl.BlockSpec((1, *ctxt.shape[1:]), lambda t, *_: (index, 0, 0))), (dctxt, full(dctxt.shape)), (tokens_t, ANY), (err_t, ANY), (ctx, ANY), (total, ANY), *((p, ANY) for p in pieces),
            *((m, full(m.shape)) for m in more or ()), *((a, ANY) for a in into or ()),
        ],
        [(out, BF, ANY), (out, BF, ANY), ((length, width), F32, ANY)],
        [
            pltpu.VMEM((heads, width // rows, tall, PACK), BF), pltpu.VMEM((heads, 8, PACK), F32), pltpu.VMEM((width, length), BF), pltpu.VMEM((width, length), BF), pltpu.VMEM((length, inner), BF),
            pltpu.VMEM((length, heads * PACK), BF), pltpu.VMEM((length, width), F32), pltpu.VMEM((width, heads * PACK), BF),
            pltpu.SemaphoreType.DMA((heads, blocks.n // heads)), pltpu.SemaphoreType.DMA((4,)), pltpu.SemaphoreType.DMA((blocks.n,)),
            pltpu.SemaphoreType.DMA((length // chunk,)), *([pltpu.VMEM((blocks.n, EXTRA, PACK), BF)] if extra else []),
        ],
        (heads * (2 * length * width * PACK + 32 * length * length * HD), heads * length * length * 2), "attention_backward",
        {11 + len(pieces) + extra: 0, 12 + len(pieces) + extra: 1} if given else {},
    )


def layer_norm(residual):
    centered = residual - jnp.mean(residual, axis=-1, keepdims=True)
    inverse = lax.rsqrt(jnp.mean(centered * centered, axis=-1, keepdims=True) + EPSILON)
    return centered * inverse, inverse


def norm_backward(scaled, normed, inverse):
    first = jnp.mean(scaled, axis=-1, keepdims=True)
    second = jnp.mean(scaled * normed, axis=-1, keepdims=True)
    return inverse * (scaled - first - normed * second)


def feed_loads(feed, target, sems, blocks, t, tops):
    copies = []
    for kind, top in enumerate(tops):
        for i in range(blocks.n // blocks.tensor):
            d = i * blocks.tensor + t
            copies.append(pltpu.make_async_copy(
                feed.at[d, pl.ds(top, blocks.rows), :], target.at[t, kind, pl.ds(i * blocks.rows, blocks.rows), :], sems.at[kind, d]
            ))
    return copies


def output_and_norm(tokens, contexts, outputs, vec):
    length, width = tokens.shape
    groups = len(contexts)
    chunk = min(256, length)

    def body(x_ref, vec_ref, *refs):
        c_refs, o_refs, (norm_ref, norm_low_ref, inv_ref, hid_ref, hidt_ref) = refs[:groups], refs[groups : 2 * groups], refs[2 * groups :]
        attended = sum(nn(a[0], b[0]) for a, b in zip(c_refs, o_refs)) + vec_ref[0:1, :]
        normed, inverse = layer_norm(x_ref[...].astype(F32) + attended)
        norm_ref[...] = normed
        norm_low_ref[...] = normed.astype(BF)
        inv_ref[...] = inverse
        first_out = normed * vec_ref[1:2, :] + vec_ref[2:3, :]
        hid_ref[...] = first_out.astype(BF)
        hidt_ref[...] = first_out.T.astype(BF)

    rows = lambda n: pl.BlockSpec((chunk, n), lambda c, *_: (c, 0))

    def some_rows(i, n):
        return pl.BlockSpec((1, chunk, n), lambda c, *_: (i, c, 0))

    wide = (length, width)
    return call(
        body, (length // chunk,), [],
        [(tokens, rows(width)), (vec, once(vec.shape))] + [(a, some_rows(i, a.shape[2])) for a, i in contexts] + [at_index(a, i) for a, i in outputs],
        [
            (wide, F32, rows(width)), (wide, BF, rows(width)), ((length, 1), F32, rows(1)), (wide, BF, rows(width)),
            ((width, length), BF, pl.BlockSpec((width, chunk), lambda c, *_: (0, c))),
        ],
        [], (2 * length * width * width, 12 * length * width), "output_and_norm",
    )


def feed_forward(hidden, normed_one, cotangent, vec, up_bias, feed, place, blocks):
    length, width = hidden.shape
    tensor = blocks.tensor
    feed, tops = feed
    part = feed.shape[-1]
    chunk = min(256, length)

    def body(place_ref, hidden, vec_ref, ub_ref, *refs):
        cot_hbm, norm_hbm, feed_hbm, slope_ref, out_hbm, low_hbm, keep, send, sums_ref, *refs = refs
        w, act, norm, acc, out, low, errt, cot, stage, feed_sems, sems, store_sems = refs
        s = pl.program_id(0)
        cot_copy = pltpu.make_async_copy(cot_hbm, cot, sems.at[0])
        norm_copy = pltpu.make_async_copy(norm_hbm, norm, sems.at[1])
        late = [pltpu.make_async_copy(a, b, sems.at[3 + n]) for n, (a, b) in enumerate([(out, out_hbm), (low, low_hbm)])]

        @pl.when(s == 0)
        def _():
            acc[...] = jnp.zeros_like(acc)
            for t in range(tensor):
                for copy in feed_loads(feed_hbm, w, feed_sems, blocks, t, tops):
                    copy.start()
            cot_copy.start()
            norm_copy.start()

        @pl.when(s < tensor)
        def _():
            for copy in feed_loads(feed_hbm, w, feed_sems, blocks, s, tops):
                copy.wait()
            rows_of = [slice(r, r + chunk) for r in range(0, length, chunk)]
            pre = nn(hidden[rows_of[0], :], w[s, 0])
            for n, rows in enumerate(rows_of):
                following = nn(hidden[rows_of[n + 1], :], w[s, 0]) if n + 1 < len(rows_of) else None
                pre = pre + ub_ref[pl.ds(s, 1), :]
                phi = 0.5 * (1.0 + lax.erf(pre * (1.0 / math.sqrt(2.0))))
                some = (pre * phi).astype(BF)
                act[s, rows, :] = some
                density = jnp.exp(-0.5 * pre * pre) * (1.0 / math.sqrt(2.0 * math.pi))
                slope_ref[0, rows, :] = (phi + pre * density).astype(BF)
                branch = nt(some, w[s, 1])
                acc[rows, :] += branch
                pre = following

        @pl.when(s == tensor - 1)
        def _():
            cot_copy.wait()
            norm_copy.wait()
            totals = jnp.zeros((8, width), F32)
            for c in range(0, length, chunk):
                rows = slice(c, c + chunk)
                first_out = norm[rows, :] * vec_ref[1:2, :] + vec_ref[2:3, :]
                normed, inverse = layer_norm(first_out + (acc[rows, :] + vec_ref[3:4, :]))
                out[rows, :] = (normed * vec_ref[4:5, :] + vec_ref[5:6, :]).astype(BF)
                upstream = cot[rows, :].astype(F32)
                error = norm_backward(upstream * vec_ref[4:5, :], normed, inverse)
                low[rows, :] = error.astype(BF)
                errt[:, rows] = error.T.astype(BF)
                sums = [jnp.sum(a, axis=0, keepdims=True) for a in (error, upstream * normed, upstream)]
                totals += jnp.concatenate(sums + [jnp.zeros((5, width), F32)], axis=0)
            sums_ref[...] = totals
            for copy in late:
                copy.start()

        @pl.when(s >= tensor)
        def _():
            t = s - tensor
            slot = lax.rem(t, 2)

            @pl.when(t >= 2)
            def _():
                blocks.stores(place_ref, t - 2, stage.at[slot], keep, send, store_sems.at[slot], "wait")

            stage[slot] = nn(errt[...], act[t]).astype(BF).reshape(-1, blocks.rows, part)
            blocks.stores(place_ref, t, stage.at[slot], keep, send, store_sems.at[slot], "start")

        @pl.when(s == 2 * tensor - 1)
        def _():
            for last in range(max(tensor - 2, 0), tensor):
                blocks.stores(place_ref, last, stage.at[last % 2], keep, send, store_sems.at[last % 2], "wait")
            for copy in late:
                copy.wait()

    block_out = (blocks.n // 2, blocks.rows, part)
    wide = (length, width)
    return call(
        body, (2 * tensor,), [place],
        [(a, once(a.shape)) for a in (hidden, vec, up_bias)] + [(cotangent, ANY), (normed_one, ANY), (feed, ANY)],
        [
            ((tensor, length, part), BF, pl.BlockSpec((1, length, part), lambda s, *_: (jnp.minimum(s, tensor - 1), 0, 0))),
            (wide, BF, ANY), (wide, BF, ANY), (block_out, BF, ANY), (block_out, BF, ANY), ((8, width), F32, once((8, width))),
        ],
        [
            pltpu.VMEM((tensor, 2, width, part), BF), pltpu.VMEM((tensor, length, part), BF), pltpu.VMEM(wide, F32), pltpu.VMEM(wide, F32),
            pltpu.VMEM(wide, BF), pltpu.VMEM(wide, BF), pltpu.VMEM((width, length), BF), pltpu.VMEM(wide, BF),
            pltpu.VMEM((2, width // blocks.rows, blocks.rows, part), BF),
            pltpu.SemaphoreType.DMA((2, blocks.n)), pltpu.SemaphoreType.DMA((6,)), pltpu.SemaphoreType.DMA((2, blocks.n // tensor)),
        ],
        (2 * length * width * (width + 3 * tensor * part), 30 * length * width + 4 * length * tensor * part), "feed_forward",
    )


def feed_backward(err_low, slope, hidden_t, normed_one, inverse_one, vec, outputs, feed, place, blocks):
    length, width = err_low.shape
    tensor = blocks.tensor
    feed, tops = feed
    part = feed.shape[-1]
    groups = len(outputs)
    chunk = min(256, length)
    inner = outputs[0][0].shape[1]

    def body(place_ref, e_ref, s_ref, h_ref, i1_ref, vec_ref, *refs):
        o_refs, refs = refs[:groups], refs[groups:]
        n1_hbm, feed_hbm, keep, send, up_sums, err_hbm, errt_hbm, sums_ref, *refs = refs
        dctx_hbm, refs = refs[:groups], refs[groups:]
        w, acc, n1, err, errt, dctx, stage, low, feed_sems, sems, out_sems, store_sems = refs
        t = pl.program_id(0)
        slot = lax.rem(t, 2)
        inputs = [pltpu.make_async_copy(n1_hbm, n1, sems.at[0])]

        @pl.when(t == 0)
        def _():
            acc[...] = jnp.zeros_like(acc)
            for k in range(tensor):
                for copy in feed_loads(feed_hbm, w, feed_sems, blocks, k, tops[::-1]):
                    copy.start()
            for copy in inputs:
                copy.start()

        for copy in feed_loads(feed_hbm, w, feed_sems, blocks, t, tops[::-1]):
            copy.wait()
        span = min(512, length)
        rows_of = [slice(r, r + span) for r in range(0, length, span)]
        product = nn(e_ref[rows_of[0], :], w[t, 0])
        total = jnp.zeros((1, part), F32)
        for n, rows in enumerate(rows_of):
            following = nn(e_ref[rows_of[n + 1], :], w[t, 0]) if n + 1 < len(rows_of) else None
            grad = product * s_ref[0, rows, :].astype(F32)
            total += jnp.sum(grad, axis=0, keepdims=True)
            some = grad.astype(BF)
            low[rows, :] = some
            acc[rows, :] += nt(some, w[t, 1])
            product = following
        up_sums[pl.ds(t, 1), :] = total

        @pl.when(t >= 2)
        def _():
            blocks.stores(place_ref, t - 2, stage.at[slot], keep, send, store_sems.at[slot], "wait")

        stage[slot] = nn(h_ref[...], low[...]).astype(BF).reshape(-1, blocks.rows, part)
        blocks.stores(place_ref, t, stage.at[slot], keep, send, store_sems.at[slot], "start")

        @pl.when(t == tensor - 1)
        def _():
            for copy in inputs:
                copy.wait()
            totals = jnp.zeros((8, width), F32)
            copies = []
            for n, c in enumerate(range(0, length, chunk)):
                rows = slice(c, c + chunk)
                err_in = e_ref[rows, :].astype(F32) + acc[rows, :]
                normed = n1[rows, :].astype(F32)
                error = norm_backward(err_in * vec_ref[1:2, :], normed, i1_ref[rows, :])
                err[rows, :] = error
                turned = error.T.astype(BF)
                errt[:, rows] = turned
                some = pl.ds(c, chunk)
                copies += [
                    pltpu.make_async_copy(err.at[some, :], err_hbm.at[some, :], out_sems.at[n, 0]),
                    pltpu.make_async_copy(errt.at[:, some], errt_hbm.at[:, some], out_sems.at[n, 1]),
                ]
                for g in range(groups):
                    dctx[g, :, rows] = nn(o_refs[g][0], turned).astype(BF)
                    copies.append(pltpu.make_async_copy(dctx.at[g, :, some], dctx_hbm[g].at[:, some], out_sems.at[n, 2 + g]))
                for copy in copies[-2 - groups :]:
                    copy.start()
                sums = [jnp.sum(a, axis=0, keepdims=True) for a in (error, err_in * normed, err_in)]
                totals += jnp.concatenate(sums + [jnp.zeros((5, width), F32)], axis=0)
            sums_ref[...] = totals
            for last in range(max(tensor - 2, 0), tensor):
                blocks.stores(place_ref, last, stage.at[last % 2], keep, send, store_sems.at[last % 2], "wait")
            for copy in copies:
                copy.wait()

    block_out = (blocks.n // 2, blocks.rows, part)
    wide = (length, width)
    return call(
        body, (tensor,), [place],
        [
            (err_low, once(wide)), (slope, pl.BlockSpec((1, length, part), lambda t, *_: (t, 0, 0))), (hidden_t, once((width, length))),
            (inverse_one, once((length, 1))), (vec, once(vec.shape)), *[at_index(o, i) for o, i in outputs],
            (normed_one, ANY), (feed, ANY),
        ],
        [
            (block_out, BF, ANY), (block_out, BF, ANY), ((8, part), F32, once((8, part))), (wide, F32, ANY), ((width, length), BF, ANY),
            ((8, width), F32, once((8, width))), *[((inner, length), BF, ANY) for _ in outputs],
        ],
        [
            pltpu.VMEM((tensor, 2, width, part), BF), pltpu.VMEM(wide, F32), pltpu.VMEM(wide, BF), pltpu.VMEM(wide, F32),
            pltpu.VMEM((width, length), BF), pltpu.VMEM((groups, inner, length), BF), pltpu.VMEM((2, width // blocks.rows, blocks.rows, part), BF), pltpu.VMEM((length, part), BF),
            pltpu.SemaphoreType.DMA((2, blocks.n)), pltpu.SemaphoreType.DMA((2,)), pltpu.SemaphoreType.DMA((length // chunk, 2 + groups)),
            pltpu.SemaphoreType.DMA((2, blocks.n // tensor)),
        ],
        (2 * length * width * (width + 3 * tensor * part), 30 * length * width + 2 * length * tensor * part), "feed_backward",
    )


def finish(first_terms, other_terms, rows, groups, column, cols):
    width = groups * HD
    n = len(first_terms)

    def body(i_ref, *refs):
        (q_ref, k_ref, v_ref, o_ref, qb_ref, vb_ref), terms = refs[2 * n :], refs[: 2 * n]
        sums = [sum(r[0].astype(F32) for r in part) for part in (terms[:n], terms[n:])]
        biases = []
        for c in range(groups):
            block = sums[0] if c == 0 else sums[1][:, (c - 1) * PACK : c * PACK]
            for j, out in enumerate((q_ref, k_ref, v_ref)):
                out[:, c * HD : (c + 1) * HD] = block[:rows, j * HD : (j + 1) * HD]
            o_ref[c * HD : (c + 1) * HD, :] = block[:rows, 2 * HD :].T[HD:]
            biases.append(block[rows : rows + 1])
        biases = jnp.concatenate(biases + [jnp.zeros((8 - groups, PACK), F32)], axis=0)
        for out, start in ((qb_ref, 0), (vb_ref, 2 * HD)):
            out[...] = pltpu.roll(biases, lax.rem(2 * PACK - start - i_ref[0], PACK), 1)[:groups, :cols]

    def block(array):
        return array, pl.BlockSpec((1, *array.shape[1:]), lambda *_: (0, 0, 0))

    shapes = [(rows, width)] * 3 + [(width, rows), (groups, cols), (groups, cols)]
    return call(
        body, (1,), [column.reshape(1)], [block(t) for t in (*first_terms, *other_terms)],
        [(shape, F32, full(shape)) for shape in shapes], [], (1e6, 2 * n * rows * PACK * 6), "finish",
    )


def local(
    tokens, query_weight, key_weight, value_weight, output_weight, query_bias, value_bias,
    output_bias, first_gain, first_shift, up_weight, up_bias, down_weight, down_bias,
    second_gain, second_shift, cotangent,
):
    dp, tensor = lax.axis_size("dp"), lax.axis_size("tensor")
    count = dp * tensor
    rows = query_weight.shape[0]
    width = rows * dp
    groups = query_weight.shape[1] // HD
    heads = groups * tensor
    slot = output_bias.shape[0]
    cols = query_bias.shape[1]
    me = lax.axis_index(AXES)
    place, devs, owners = position_table(me, count), device_table(me, count), owner_table(me, count)
    direct = rows % 16 == 0

    vectors = jnp.stack([output_bias, first_gain, first_shift, down_bias, second_gain, second_shift])
    extra = small_block(vectors, query_bias, value_bias, up_bias)
    output_turned = output_weight.T
    by_group = [
        jnp.concatenate([w[:, c * HD : (c + 1) * HD] for w in (query_weight, key_weight, value_weight, output_turned)], axis=1)
        for c in range(groups)
    ]
    first, second = (Gathering(jnp.concatenate(blocks, axis=axis), count) for blocks, axis in (([by_group[0], extra], 0), (by_group[1:], 1)))
    feed = lax.all_gather(jnp.concatenate([up_weight, down_weight.T], axis=0), AXES, axis=0, tiled=False)
    tokens_t, place, devs, owners, owner_column, dev_column = wave(
        [first], tokens.T, place, devs, owners, owners.reshape(count, 1), devs.reshape(count, 1)
    )
    wave([first, second])
    wave([first])
    direct = rows % 16 == 0
    small_set = (first.pieces, rows) if direct else ([jnp.concatenate([p[:, rows:] for p in first.pieces], axis=0)], 0)
    if direct:
        blocks = Blocks(count, rows, tensor)
        block_place, block_devs = place, devs
    else:
        blocks = Blocks(tensor, width, tensor)
        block_place = block_devs = jnp.arange(tensor, dtype=jnp.int32)

    def by_matrix(ordered):
        return [ordered.reshape(dp, tensor, rows, -1).transpose(1, 0, 2, 3).reshape(tensor, width, -1)]

    def ready(gathering):
        if direct:
            return gathering.pieces
        return by_matrix(jnp.take(jnp.concatenate(gathering.pieces, axis=0)[:, :rows], gathered_place(me, count), axis=0))

    def scattering(keep, send, more=None):
        if not direct:
            stacked = jnp.concatenate([keep, send], axis=0)
            parts = [stacked[:, :width].reshape(tensor, dp, rows, -1).transpose(1, 0, 2, 3).reshape(count, rows, -1)]
            if stacked.shape[1] > width:
                parts.append(jnp.tile(stacked[:, width:], (dp, 1, 1)))
            stacked = jnp.take(jnp.concatenate(parts, axis=1), owners, axis=0)
            if more is not None:
                stacked = jnp.concatenate([stacked, more], axis=1)
            keep, send = stacked[: count // 2], stacked[count // 2 :]
        return Scattering(keep, send, count)

    tokens_now = wave([second], tokens)
    vec, bias_pack, up_rows = unpack_small(*small_set, dev_column, slot, cols, width, tensor)
    first_set = ready(first)
    one = attention_forward(tokens_now, first_set, bias_pack, 0, block_devs, blocks)
    tokens_now = wave([second], tokens, one[4])[0]
    second_set = ready(second)
    others = attention_forward(tokens_now, second_set, bias_pack, 1, block_devs, blocks)
    weights = [(first_set, 0)] + [(second_set, c * PACK) for c in range(groups - 1)]
    forward = [(one, 0)] + [(others, c) for c in range(groups - 1)]
    outputs = [(f[5], i) for f, i in forward]
    normed_wide, normed_one, inverse_one, hidden, hidden_t = output_and_norm(tokens, [(f[2], i) for f, i in forward], outputs, vec)
    feed, hidden = lax.optimization_barrier((feed, hidden))
    if not direct:
        feed = jnp.concatenate([by_matrix(feed[:, :rows])[0], by_matrix(feed[:, rows:])[0]], axis=1)
    feed = (feed, (0, feed.shape[1] // 2))
    slope, layer_out, err_two_low, down_keep, down_send, sums_two = feed_forward(
        hidden, normed_wide, cotangent, vec, up_rows, feed, block_place, blocks
    )
    grad_down = scattering(down_keep, down_send)
    err_two_low = wave([grad_down], err_two_low)
    up_keep, up_send, up_sums, err_one, err_one_t, sums_one, *context_grads = feed_backward(
        err_two_low, slope, hidden_t, normed_one, inverse_one, vec, outputs, feed, block_place, blocks
    )
    grad_up = scattering(up_keep, up_send)
    small = (sums_one, sums_two, up_sums, owner_column)
    if not direct:
        small = pack_small_grads(*small, slot, cols, tensor)
    column = lax.axis_index("dp") * cols
    backward = [None] * groups
    token_sum = err_one
    last, packed, moving = (err_one_t,), None, [grad_down, grad_up]
    for c in reversed(range(groups)):
        carries = c == groups - 1
        options = {}
        if c and direct:
            options = dict(into=packed, lane=(c - 1) * PACK, high=rows + 2 * EXTRA, wide=(groups - 1) * PACK)
        if c:
            context_grad = wave(moving, context_grads[c], since=last)
        backward[c] = attention_backward(
            tokens_t, err_one_t, *forward[c], context_grad, token_sum, weights[c], block_place, block_devs, blocks,
            (small, slot, cols) if direct and carries else None, **options,
        )
        token_sum = backward[c][2]
        last = (token_sum,)
        if c and direct:
            packed = backward[c][:2]
        if c == 1:
            if direct:
                others = scattering(*packed)
            else:
                packed = [jnp.concatenate([backward[g][i] for g in range(1, groups)], axis=2) for i in range(2)]
                others = scattering(*packed, jnp.pad(small, ((0, 0), (0, 0), ((groups - 2) * PACK, 0))))
            grad_down.terms, grad_up.terms = wave([others], grad_down.terms, grad_up.terms)
            ahead = [*grad_down.outgoing(), *grad_up.outgoing()]
            wave([grad_down, grad_up])
            others.looked_at(*ahead)
            context_grad = wave([others], context_grads[0])
    zero = scattering(*backward[0][:2])
    while grad_down.phases:
        wave([grad_down])
    grad_up.terms, grad_down.terms, others.terms = wave([zero], grad_up.terms, grad_down.terms, others.terms)
    wave([others])
    wave([zero, grad_up])
    while grad_up.phases:
        wave([grad_up])
    wave([zero])
    grad_up.terms, zero.terms = wave([others], grad_up.terms, zero.terms)
    grad_up, grad_down = grad_up.result(), grad_down.result()
    while zero.phases or others.phases:
        grad_up, grad_down = wave([zero, others], grad_up, grad_down)
    tail = sum(t[0, rows + EXTRA :, (groups - 2) * PACK :].astype(F32) for t in others.terms)
    if direct:
        out_query, out_key, out_value, out_output, *bias_out = finish(zero.terms, others.terms, rows, groups, column, cols)
    else:
        results = [zero.result()] + jnp.split(others.result()[: rows + EXTRA], groups - 1, axis=1)
        bias_rows = jnp.stack([r[rows] for r in results])
        bias_out = [lax.dynamic_slice(bias_rows, (0, start + column), (groups, cols)) for start in (0, 2 * HD)]
        out = jnp.stack([r[:rows] for r in results], axis=1).reshape(rows, groups, 4, HD)
        out_query, out_key, out_value, out_output = (out[:, :, i].reshape(rows, groups * HD) for i in range(4))
        out_output = out_output.T
    vecs = [tail[v // 2, (v % 2) * LANES : (v % 2) * LANES + slot] for v in range(6)]
    return (
        layer_out,
        token_sum,
        out_query,
        out_key,
        out_value,
        out_output,
        bias_out[0],
        bias_out[1],
        vecs[0],
        vecs[1],
        vecs[2],
        grad_up,
        tail[: up_bias.shape[0], 64 : 64 + cols],
        grad_down.T,
        vecs[3],
        vecs[4],
        vecs[5],
    )


def solution(mesh):
    both, cross, turned, vector = P(AXES, None), P("dp", "tensor"), P("tensor", "dp"), P(AXES)
    return jax.shard_map(
        local,
        mesh=mesh,
        in_specs=(
            both, cross, cross, cross, turned, turned, turned, vector, vector, vector,
            cross, turned, turned, vector, vector, vector, both,
        ),
        out_specs=(
            both, both, cross, cross, cross, turned, turned, turned, vector, vector, vector,
            cross, turned, turned, vector, vector, vector,
        ),
        check_vma=False,
    )
```

```python
import functools
import math

import jax
import jax.numpy as jnp
import numpy as np
from jax import lax
from jax.experimental import pallas as pl
from jax.experimental.pallas import tpu as pltpu
from jax.sharding import PartitionSpec as P

HD = 64
L = 1024
PACK = 4 * HD
EPSILON = 1e-12
AXES = ("dp", "tensor")
EXTRA = 16
LANES = 128
BF = jnp.bfloat16
F32 = jnp.float32
SDS = jax.ShapeDtypeStruct
ANY = pl.BlockSpec(memory_space=pl.ANY)


def nn(a, b):
    return lax.dot_general(a, b, (((1,), (0,)), ((), ())), preferred_element_type=F32)


def nt(a, b):
    return lax.dot_general(a, b, (((1,), (1,)), ((), ())), preferred_element_type=F32)


def full(shape):
    return pl.BlockSpec(shape, lambda *_: (0,) * len(shape))


def once(shape):
    return pl.BlockSpec(shape, lambda *_: (0,) * len(shape), pipeline_mode=pl.Buffered(1))


def at_index(array, i):
    shape = (1, *array.shape[1:])
    return array, pl.BlockSpec(shape, lambda *_: (i,) + (0,) * (len(shape) - 1), pipeline_mode=pl.Buffered(1))


def call(body, grid, tables, ins, outs, scratch, cost, name, aliases={}):
    flops, moved = cost
    return pl.pallas_call(
        body,
        grid_spec=pltpu.PrefetchScalarGridSpec(
            num_scalar_prefetch=len(tables),
            grid=grid,
            in_specs=[s for _, s in ins],
            out_specs=[s for _, _, s in outs],
            scratch_shapes=scratch,
        ),
        out_shape=[SDS(s, d) for s, d, _ in outs],
        compiler_params=pltpu.CompilerParams(
            dimension_semantics=("arbitrary",) * len(grid), vmem_limit_bytes=60 * 2**20
        ),
        cost_estimate=pl.CostEstimate(flops=int(flops * 0.01), bytes_accessed=int(moved * 0.01), transcendentals=0),
        name=name,
        input_output_aliases=aliases,
    )(*tables, *[a for a, _ in ins])


def exchange(array, differs, count):
    even, odd = differs if isinstance(differs, tuple) else (differs, differs)
    return lax.ppermute(array, AXES, [(d, d ^ (odd if d & 1 else even)) for d in range(count)])


def phases_of(count):
    bits = count.bit_length() - 1
    return [*((k, 1) for k in range(bits - 1, 4, -1)), (3, 2), (1, 2), (0, 1)]


def scatter_phases_of(count):
    bits = count.bit_length() - 1
    return [[1], [(2, 4)], [(4, 2)], [8, 16, 24], *([1 << k] for k in range(5, bits))]


class Gathering:
    def __init__(self, block, count):
        self.pieces, self.count, self.phases = [block[None]], count, phases_of(count)
        while self.phases[0][1] == 1:
            self.move(self.outgoing())

    def outgoing(self):
        if self.phases[0] != (0, 1) and len(self.pieces) > 1:
            self.pieces = [jnp.concatenate(self.pieces, axis=0)]
        return self.pieces

    def move(self, pieces):
        low, bits = self.phases.pop(0)
        self.pieces = self.pieces + [exchange(p, k << low, self.count) for k in range(1, 1 << bits) for p in pieces]


class Scattering:
    def __init__(self, keep, send, count):
        self.terms, self.sends, self.count, self.phases = [keep], [send], count, scatter_phases_of(count)
        self.size = keep.shape[0]

    def looked_at(self, *since):
        self.terms = lax.optimization_barrier((self.terms, since))[0]

    def outgoing(self):
        if self.sends is None:
            parts = 1 + len(self.phases[0])
            size = self.size // parts
            self.sends = [sum(t[k * size : (k + 1) * size].astype(F32) for t in self.terms).astype(BF) for k in range(1, parts)]
            self.size = size
        return self.sends

    def move(self, sends):
        self.terms = self.terms + [exchange(p, k, self.count) for k, p in zip(self.phases.pop(0), sends)]
        self.sends = None

    def result(self):
        return sum(t[0].astype(F32) for t in self.terms)


def wave(moves, *beside, since=()):
    moves = [m for m in moves if m.phases]
    for m in moves:
        if since and isinstance(m, Scattering):
            m.looked_at(*since)
    outgoing, beside = lax.optimization_barrier(([m.outgoing() for m in moves], beside))
    for m, array in zip(moves, outgoing):
        m.move(array)
    return beside[0] if len(beside) == 1 else beside


def fields_of(count):
    top, fields = count.bit_length() - 1, []
    for low, bits in phases_of(count)[::-1]:
        top -= bits
        fields.append((low, bits, top))
    return fields


def position_table(me, count):
    bits = count.bit_length() - 1
    device = jnp.arange(count, dtype=jnp.int32)
    differs = device ^ me
    one, two = (differs >> 1) & 1, (differs >> 2) & 1
    odd = (device & 1) == 1
    place = ((differs & 1) << (bits - 1)) | (jnp.where(odd, two, one) << (bits - 2)) | (jnp.where(odd, one, two) << (bits - 3))
    place = place | (((differs >> 3) & 3) << (bits - 5))
    for k in range(5, bits):
        place = place | (((differs >> k) & 1) << (bits - 1 - k))
    return place


def owner_table(me, count):
    bits = count.bit_length() - 1
    place = jnp.arange(count, dtype=jnp.int32)
    core, upper, lower = ((place >> (bits - k)) & 1 for k in (1, 2, 3))
    odd = ((me ^ core) & 1) == 1
    differs = core | (jnp.where(odd, lower, upper) << 1) | (jnp.where(odd, upper, lower) << 2) | (((place >> (bits - 5)) & 3) << 3)
    for k in range(5, bits):
        differs = differs | (((place >> (bits - 1 - k)) & 1) << k)
    return differs ^ me


def gathered_place(me, count):
    differs = jnp.arange(count, dtype=jnp.int32) ^ me
    return sum(((differs >> low) & ((1 << bits) - 1)) << at for low, bits, at in fields_of(count))


def device_table(me, count):
    place = jnp.arange(count, dtype=jnp.int32)
    return sum(((place >> at) & ((1 << bits) - 1)) << low for low, bits, at in fields_of(count)) ^ me


class Blocks:
    def __init__(self, n, rows, tensor):
        self.n, self.rows, self.tensor = n, rows, tensor

    def at(self, d):
        return lax.rem(d, self.tensor), pl.multiple_of(lax.div(d, self.tensor) * self.rows, self.rows)

    def loads(self, devs, pieces, target, sems, lane=0, top=0):
        out, p = [], 0
        flat = len(target.shape) == 2
        width = target.shape[-1] // (self.tensor if flat else 1)
        for piece in pieces:
            for j in range(piece.shape[0]):
                t, row = self.at(devs[p])
                rows = pl.ds(row, self.rows)
                into = target.at[rows, pl.ds(pl.multiple_of(t * width, width), width)] if flat else target.at[t, rows, :]
                out.append(pltpu.make_async_copy(
                    piece.at[j, pl.ds(top, self.rows), pl.ds(lane, width)], into, sems.at[p]
                ))
                p += 1
        return out

    def stores(self, place, t, stage, keep, send, sems, action, lane=0):
        half = self.n // 2
        lanes = pl.ds(lane, stage.shape[-1])
        for i in range(self.n // self.tensor):
            p = place[i * self.tensor + t]
            kept = pltpu.make_async_copy(stage.at[i], keep.at[lax.rem(p, half), :, lanes], sems.at[i])
            if action == "wait":
                kept.wait()
            else:
                sent = pltpu.make_async_copy(stage.at[i], send.at[lax.rem(p, half), :, lanes], sems.at[i])
                pl.when(p < half)(kept.start)
                pl.when(p >= half)(sent.start)


def spread_constants(slot, cols, width):
    lane = np.arange(width)
    a, c = np.zeros((LANES, width), np.float32), np.zeros((LANES, width), np.float32)
    for j in range(slot):
        a[j] = lane % slot == j
    for j in range(cols):
        a[32 + j] = lane % cols == j
        c[64 + j] = lane % cols == j
    return jnp.asarray(a, BF), jnp.asarray(c, BF)


def small_masks(device, slot, cols, width, tensor):
    n = device.shape[0]
    shift = tensor.bit_length() - 1
    row = lax.broadcasted_iota(jnp.int32, (n, EXTRA, width), 1)
    lane = lax.broadcasted_iota(jnp.int32, (n, EXTRA, width), 2)
    i, t = device >> shift, device & (tensor - 1)
    in_head = (lane & (HD - 1)) >> (cols.bit_length() - 1)
    groups = width // HD // tensor
    vector = (row < 9) & (lane >= device * slot) & (lane < (device + 1) * slot)
    bias = (row >= 9) & (row < 9 + groups) & ((lane >> 6) == t * groups + row - 9) & (in_head == i)
    hidden = (row < width // HD) & ((lane >> 6) == row) & (in_head == i)
    return vector | bias, hidden, t


def unpack_small(pieces, top, device, slot, cols, width, tensor):
    n = device.shape[0]
    groups = width // HD // tensor
    spread_a, spread_c = spread_constants(slot, cols, width)

    def body(d_ref, a_ref, c_ref, *refs):
        piece_refs, (vec_ref, bias_ref, up_ref, x_s, sems) = refs[: len(pieces)], refs[len(pieces) :]
        copies, at = [], 0
        for j, piece in enumerate(piece_refs):
            size = piece.shape[0]
            copies.append(pltpu.make_async_copy(piece.at[:, pl.ds(top, EXTRA), :], x_s.at[pl.ds(at, size)], sems.at[j]))
            at += size
        for copy in copies:
            copy.start()
        d = d_ref[...].reshape(n, 1, 1)
        main, hidden, t = small_masks(d, slot, cols, width, tensor)
        for copy in copies:
            copy.wait()
        x = x_s[...].reshape(n * EXTRA, 2 * LANES)
        bias_ref[...] = jnp.zeros_like(bias_ref)
        for half in range(2):
            y = nn(x[:, half * LANES : (half + 1) * LANES], a_ref[...]).reshape(n, EXTRA, width)
            total = jnp.sum(jnp.where(main, y, 0.0), axis=0)
            for v in range(half, 6, 2):
                r = v // 2
                vec_ref[v : v + 1, :] = total[r : r + 1] + total[3 + r : 4 + r] + total[6 + r : 7 + r]
            row = jnp.sum(total[9:EXTRA], axis=0, keepdims=True)
            for head in range(groups * tensor):
                at = half * 2 * HD
                bias_ref[head % groups, head // groups : head // groups + 1, at : at + HD] = row[:, head * HD : (head + 1) * HD]
        y = nn(x[:, :LANES], c_ref[...]).reshape(n, EXTRA, width)
        y = jnp.where(hidden, y, 0.0)
        for k in range(tensor):
            picked = jnp.sum(jnp.where(t == k, y, 0.0), axis=0)
            up_ref[k : k + 1, :] = jnp.sum(picked, axis=0, keepdims=True)

    row8, bias = (8, width), (groups, tensor, PACK)
    return call(
        body, (1,), [],
        [(a, full(a.shape)) for a in (device, spread_a, spread_c)] + [(p, ANY) for p in pieces],
        [(row8, F32, full(row8)), (bias, F32, full(bias)), (row8, F32, full(row8))],
        [pltpu.VMEM((n, EXTRA, PACK), BF), pltpu.SemaphoreType.DMA((len(pieces),))],
        (3 * 2 * n * EXTRA * LANES * width, n * EXTRA * PACK * 2), "unpack_small",
    )


def spread_small_grads(one_ref, two_ref, u_ref, d_ref, a_ref, c_ref, slot, cols, tensor):
    n, width = d_ref.shape[0], one_ref.shape[-1]
    d = d_ref[...].reshape(n, 1, 1)
    main, hidden, t = small_masks(d, slot, cols, width, tensor)
    row = lax.broadcasted_iota(jnp.int32, (EXTRA, width), 0)
    halves = []
    for half in range(2):
        z = jnp.zeros((EXTRA, width), F32)
        for v in range(half, 6, 2):
            z = jnp.where(row == v // 2, (one_ref, two_ref)[v // 3][v % 3 : v % 3 + 1, :], z)
        spread = jnp.where(main, z[None], 0.0).astype(BF).reshape(n * EXTRA, width)
        halves.append(nt(spread, a_ref[...]))
    z = jnp.zeros((n, EXTRA, width), F32)
    for k in range(tensor):
        z = jnp.where(t == k, u_ref[k : k + 1, :].reshape(1, 1, width), z)
    spread = jnp.where(hidden, z, 0.0).astype(BF).reshape(n * EXTRA, width)
    halves[0] = halves[0] + nt(spread, c_ref[...])
    return jnp.concatenate(halves, axis=1).astype(BF).reshape(n, EXTRA, 2 * LANES)


def pack_small_grads(one, two, up, device, slot, cols, tensor):
    n, width = device.shape[0], one.shape[-1]
    spread_a, spread_c = spread_constants(slot, cols, width)

    def body(one_ref, two_ref, u_ref, d_ref, a_ref, c_ref, out_ref):
        out_ref[...] = spread_small_grads(one_ref, two_ref, u_ref, d_ref, a_ref, c_ref, slot, cols, tensor)

    shape = (n, EXTRA, PACK)
    return call(
        body, (1,), [],
        [(a, full(a.shape)) for a in (one, two, up, device, spread_a, spread_c)],
        [(shape, BF, full(shape))], [], (3 * 2 * n * EXTRA * LANES * width, 2 * n * EXTRA * PACK), "pack_small",
    )[0]


def three_parts(vector):
    high = lax.reduce_precision(vector, 8, 7)
    middle = lax.reduce_precision(vector - high, 8, 7)
    lowest = lax.reduce_precision(vector - high - middle, 8, 7)
    return jnp.stack([high, middle, lowest]).astype(BF)


def small_block(vectors, query_bias, value_bias, up_bias):
    slot = vectors.shape[1]
    parts = three_parts(vectors).reshape(9, 2, slot)

    def placed(array, row, lane):
        return jnp.pad(array, ((row, EXTRA - row - array.shape[0]), (lane, PACK - lane - array.shape[1])))

    return (
        placed(parts[:, 0], 0, 0) + placed(parts[:, 1], 0, LANES) + placed(query_bias, 9, 32)
        + placed(value_bias, 9, LANES + 32) + placed(up_bias, 0, 64)
    )


def attention_forward(tokens, pieces, bias, base, devs, blocks):
    length, width = tokens.shape
    heads = blocks.tensor
    inner = heads * HD
    groups = pieces[0].shape[-1] // PACK

    def body(devs_ref, x_ref, b_ref, *refs):
        piece_refs, (qkv_ref, e_ref, ctx_ref, ctxt_ref, inv_ref, ot_ref, w, ot_s, vt_s, sems) = refs[: len(pieces)], refs[len(pieces) :]
        c, t = pl.program_id(0), pl.program_id(1)

        loads = [blocks.loads(devs_ref, piece_refs, w.at[g], sems.at[g], g * PACK) for g in range(groups)]

        @pl.when((c == 0) & (t == 0))
        def _():
            for copies in loads:
                for copy in copies:
                    copy.start()
            vt_s[HD:, :] = jnp.ones((HD, length), BF)

        for g in range(groups):
            @pl.when((c == g) & (t == 0))
            def _():
                for copy in loads[g]:
                    copy.wait()

        wt = w[c, t]
        col = lax.broadcasted_iota(jnp.int32, (1, PACK), 1)
        pre = nn(x_ref[...], wt) + b_ref[base + c, pl.ds(t, 1), :]
        low = (pre * jnp.where(col < HD, 1.0 / math.sqrt(HD), 1.0)).astype(BF)
        qkv_ref[0] = low
        q, k = low[:, :HD], low[:, HD : 2 * HD]
        vt_s[:HD, :] = low[:, 2 * HD :].T[:HD]
        square = pre[:, : 2 * HD] * pre[:, : 2 * HD]
        pick = lax.broadcasted_iota(jnp.int32, (2 * HD, LANES), 0) // HD == lax.broadcasted_iota(jnp.int32, (2 * HD, LANES), 1)
        norms = jnp.max(nn(square.astype(BF), pick.astype(BF)), axis=0, keepdims=True)
        bound = jnp.sqrt(norms[0, 0] * norms[0, 1]) * (1.1 / math.sqrt(HD))

        @pl.when(bound <= 40.0)
        def _():
            e_ref[0] = jnp.exp(nt(k, q)).astype(BF)

        @pl.when(jnp.logical_not(bound <= 40.0))
        def _():
            def some(j, _):
                at = pl.ds(pl.multiple_of(j * LANES, LANES), LANES)
                scores = nt(k, qkv_ref[0, at, :][:, :HD])
                e_ref[0, :, at] = jnp.exp(scores - jnp.max(scores, axis=0, keepdims=True)).astype(BF)
                return 0

            lax.fori_loop(0, length // LANES, some, 0)

        mixed = nn(vt_s[...], e_ref[0])
        inv = 1.0 / mixed[HD : HD + 1]
        inv_ref[0] = jnp.broadcast_to(inv, (8, length))
        ctxt_ref[0, pl.ds(t * HD, HD), :] = mixed[:HD] * inv
        ot_s[pl.ds(t * HD, HD), :] = wt[:, 2 * HD :].T[HD:].astype(F32)

        @pl.when(t == heads - 1)
        def _():
            ctx_ref[0] = ctxt_ref[0].T.astype(BF)
            ot_ref[0] = ot_s[...].astype(BF)

    by_head = lambda *s: pl.BlockSpec((1, *s), lambda c, t, *_: (c * heads + t, 0, 0))
    by_group = lambda *s: pl.BlockSpec((1, *s), lambda c, t, *_: (c, 0, 0))
    return call(
        body, (groups, heads), [devs],
        [(tokens, full(tokens.shape)), (bias, full(bias.shape))] + [(p, ANY) for p in pieces],
        [
            ((groups * heads, length, PACK), BF, by_head(length, PACK)),
            ((groups * heads, length, length), BF, by_head(length, length)),
            ((groups, length, inner), BF, by_group(length, inner)),
            ((groups, inner, length), F32, by_group(inner, length)),
            ((groups * heads, 8, length), F32, by_head(8, length)),
            ((groups, inner, width), BF, by_group(inner, width)),
        ],
        [pltpu.VMEM((groups, heads, width, PACK), BF), pltpu.VMEM((inner, width), F32), pltpu.VMEM((2 * HD, length), BF), pltpu.SemaphoreType.DMA((groups, blocks.n))],
        (groups * heads * (2 * length * width * PACK + 16 * length * length * HD), groups * heads * length * length * 2), "attention_forward",
    )


def attention_backward(tokens_t, err_t, forward, index, dctxt, total, weights, place, devs, blocks, more=None, into=None, lane=0, high=None, wide=PACK):
    width, length = tokens_t.shape
    pieces, piece_lane = weights
    chunk = min(256, length)
    qkv, e, ctx, ctxt, inv, _ = forward
    heads = blocks.tensor
    inner = heads * HD
    half = blocks.n // 2
    scale = 1.0 / math.sqrt(HD)
    rows, extra, given = blocks.rows, 0 if more is None else 6, 0 if into is None else 2
    high = high or blocks.rows + EXTRA
    tall = rows + EXTRA * (1 if more is None else 2)
    if more is not None:
        sums, slot, cols = more
        more = [*sums, *spread_constants(slot, cols, width)]

    def body(place_ref, devs_ref, qkv_ref, e_ref, inv_ref, ctxt_ref, dctxt_ref, xt_hbm, et_hbm, ctx_hbm, total_hbm, *refs):
        piece_refs, refs = refs[: len(pieces)], refs[len(pieces) :]
        more_ref, (keep_ref, send_ref, out_hbm, stage, bias, xt, et, ctx, d_ref, sum_s, w, sems, in_sems, w_sems, out_sems, *small) = refs[:extra], refs[extra + given :]
        keep_rows, send_rows = (r.at[:, pl.ds(0, tall), :] for r in (keep_ref, send_ref))
        t = pl.program_id(0)
        late = [pltpu.make_async_copy(a, b, in_sems.at[n]) for n, (a, b) in enumerate([(xt_hbm, xt), (et_hbm, et), (ctx_hbm.at[index], ctx), (total_hbm, sum_s)])]
        late += blocks.loads(devs_ref, piece_refs, w, w_sems, piece_lane)

        @pl.when(t == 0)
        def _():
            for copy in late:
                copy.start()
            if extra:
                small[0][...] = spread_small_grads(*more_ref, slot, cols, heads)

        q, k, v = qkv_ref[0, :, :HD], qkv_ref[0, :, HD : 2 * HD], qkv_ref[0, :, 2 * HD : 3 * HD]
        mine = pl.ds(t * HD, HD)
        dot = (dctxt_ref[mine, :].astype(F32) * inv_ref[0, :1, :]).astype(BF)
        delta = jnp.sum(dot.astype(F32) * ctxt_ref[0, mine, :], axis=0, keepdims=True)
        ee = e_ref[0]
        ds = (ee.astype(F32) * (nn(v, dot) - delta)).astype(BF)
        dv = nn(ee, dot.T)
        dk = nn(ds, q)
        dq = (nn(k.T, ds) * scale).T
        d = jnp.concatenate([dq, dk, dv, jnp.zeros_like(dv)], axis=1)
        bias[t] = jnp.broadcast_to(jnp.sum(d, axis=0, keepdims=True), (8, PACK))
        d_ref[:, pl.ds(pl.multiple_of(t * PACK, PACK), PACK)] = d.astype(BF)

        @pl.when(t == heads - 1)
        def _():
            for copy in late:
                copy.wait()
            outs = []
            for n, c in enumerate(range(0, length, chunk)):
                sum_s[c : c + chunk, :] += nt(d_ref[c : c + chunk, :], w[...])
                outs.append(pltpu.make_async_copy(sum_s.at[pl.ds(c, chunk), :], out_hbm.at[pl.ds(c, chunk), :], out_sems.at[n]))
                outs[-1].start()
            go = nn(et[...], ctx[...])
            for h in range(heads):
                if h % 2 == 0:
                    both = nn(xt[...], d_ref[:, h * PACK : (h + 2) * PACK])
                g = both[:, h % 2 * PACK : (h % 2 + 1) * PACK]
                low = jnp.concatenate([g[:, : 3 * HD], go[:, h * HD : (h + 1) * HD]], axis=1).astype(BF)
                row = jnp.concatenate([bias[h]] * (EXTRA // 8), axis=0).astype(BF)
                for i in range(width // rows):
                    stage[h, i, :rows, :] = low[i * rows : (i + 1) * rows]
                    stage[h, i, rows : rows + EXTRA, :] = row
                    if extra:
                        stage[h, i, rows + EXTRA :, :] = small[0][place_ref[i * heads + h]]
                blocks.stores(place_ref, h, stage.at[h], keep_rows, send_rows, sems.at[h], "start", lane)
            for h in range(heads):
                blocks.stores(place_ref, h, stage.at[h], keep_rows, send_rows, sems.at[h], "wait", lane)
            for copy in outs:
                copy.wait()

    by_head = lambda *s: pl.BlockSpec((1, *s), lambda t, *_: (index * heads + t, 0, 0))
    out = (half, high, wide)
    return call(
        body, (heads,), [place, devs],
        [
            (qkv, by_head(length, PACK)), (e, by_head(length, length)), (inv, by_head(8, length)),
            (ctxt, pl.BlockSpec((1, *ctxt.shape[1:]), lambda t, *_: (index, 0, 0))), (dctxt, full(dctxt.shape)), (tokens_t, ANY), (err_t, ANY), (ctx, ANY), (total, ANY), *((p, ANY) for p in pieces),
            *((m, full(m.shape)) for m in more or ()), *((a, ANY) for a in into or ()),
        ],
        [(out, BF, ANY), (out, BF, ANY), ((length, width), F32, ANY)],
        [
            pltpu.VMEM((heads, width // rows, tall, PACK), BF), pltpu.VMEM((heads, 8, PACK), F32), pltpu.VMEM((width, length), BF), pltpu.VMEM((width, length), BF), pltpu.VMEM((length, inner), BF),
            pltpu.VMEM((length, heads * PACK), BF), pltpu.VMEM((length, width), F32), pltpu.VMEM((width, heads * PACK), BF),
            pltpu.SemaphoreType.DMA((heads, blocks.n // heads)), pltpu.SemaphoreType.DMA((4,)), pltpu.SemaphoreType.DMA((blocks.n,)),
            pltpu.SemaphoreType.DMA((length // chunk,)), *([pltpu.VMEM((blocks.n, EXTRA, PACK), BF)] if extra else []),
        ],
        (heads * (2 * length * width * PACK + 32 * length * length * HD), heads * length * length * 2), "attention_backward",
        {11 + len(pieces) + extra: 0, 12 + len(pieces) + extra: 1} if given else {},
    )


def layer_norm(residual):
    centered = residual - jnp.mean(residual, axis=-1, keepdims=True)
    inverse = lax.rsqrt(jnp.mean(centered * centered, axis=-1, keepdims=True) + EPSILON)
    return centered * inverse, inverse


def norm_backward(scaled, normed, inverse):
    first = jnp.mean(scaled, axis=-1, keepdims=True)
    second = jnp.mean(scaled * normed, axis=-1, keepdims=True)
    return inverse * (scaled - first - normed * second)


def feed_loads(feed, target, sems, blocks, t, tops):
    copies = []
    for kind, top in enumerate(tops):
        for i in range(blocks.n // blocks.tensor):
            d = i * blocks.tensor + t
            copies.append(pltpu.make_async_copy(
                feed.at[d, pl.ds(top, blocks.rows), :], target.at[t, kind, pl.ds(i * blocks.rows, blocks.rows), :], sems.at[kind, d]
            ))
    return copies


def output_and_norm(tokens, contexts, outputs, vec):
    length, width = tokens.shape
    groups = len(contexts)
    chunk = min(256, length)

    def body(x_ref, vec_ref, *refs):
        c_refs, o_refs, (norm_ref, norm_low_ref, inv_ref, hid_ref, hidt_ref) = refs[:groups], refs[groups : 2 * groups], refs[2 * groups :]
        attended = sum(nn(a[0], b[0]) for a, b in zip(c_refs, o_refs)) + vec_ref[0:1, :]
        normed, inverse = layer_norm(x_ref[...].astype(F32) + attended)
        norm_ref[...] = normed
        norm_low_ref[...] = normed.astype(BF)
        inv_ref[...] = inverse
        first_out = normed * vec_ref[1:2, :] + vec_ref[2:3, :]
        hid_ref[...] = first_out.astype(BF)
        hidt_ref[...] = first_out.T.astype(BF)

    rows = lambda n: pl.BlockSpec((chunk, n), lambda c, *_: (c, 0))

    def some_rows(i, n):
        return pl.BlockSpec((1, chunk, n), lambda c, *_: (i, c, 0))

    wide = (length, width)
    return call(
        body, (length // chunk,), [],
        [(tokens, rows(width)), (vec, once(vec.shape))] + [(a, some_rows(i, a.shape[2])) for a, i in contexts] + [at_index(a, i) for a, i in outputs],
        [
            (wide, F32, rows(width)), (wide, BF, rows(width)), ((length, 1), F32, rows(1)), (wide, BF, rows(width)),
            ((width, length), BF, pl.BlockSpec((width, chunk), lambda c, *_: (0, c))),
        ],
        [], (2 * length * width * width, 12 * length * width), "output_and_norm",
    )


def feed_forward(hidden, normed_one, cotangent, vec, up_bias, feed, place, blocks):
    length, width = hidden.shape
    tensor = blocks.tensor
    feed, tops = feed
    part = feed.shape[-1]
    chunk = min(256, length)

    def body(place_ref, hidden, vec_ref, ub_ref, *refs):
        cot_hbm, norm_hbm, feed_hbm, slope_ref, out_hbm, low_hbm, keep, send, sums_ref, *refs = refs
        w, act, norm, acc, out, low, errt, cot, stage, feed_sems, sems, store_sems = refs
        s = pl.program_id(0)
        cot_copy = pltpu.make_async_copy(cot_hbm, cot, sems.at[0])
        norm_copy = pltpu.make_async_copy(norm_hbm, norm, sems.at[1])
        late = [pltpu.make_async_copy(a, b, sems.at[3 + n]) for n, (a, b) in enumerate([(out, out_hbm), (low, low_hbm)])]

        @pl.when(s == 0)
        def _():
            acc[...] = jnp.zeros_like(acc)
            for t in range(tensor):
                for copy in feed_loads(feed_hbm, w, feed_sems, blocks, t, tops):
                    copy.start()
            cot_copy.start()
            norm_copy.start()

        @pl.when(s < tensor)
        def _():
            for copy in feed_loads(feed_hbm, w, feed_sems, blocks, s, tops):
                copy.wait()
            rows_of = [slice(r, r + chunk) for r in range(0, length, chunk)]
            pre = nn(hidden[rows_of[0], :], w[s, 0])
            for n, rows in enumerate(rows_of):
                following = nn(hidden[rows_of[n + 1], :], w[s, 0]) if n + 1 < len(rows_of) else None
                pre = pre + ub_ref[pl.ds(s, 1), :]
                phi = 0.5 * (1.0 + lax.erf(pre * (1.0 / math.sqrt(2.0))))
                some = (pre * phi).astype(BF)
                act[s, rows, :] = some
                density = jnp.exp(-0.5 * pre * pre) * (1.0 / math.sqrt(2.0 * math.pi))
                slope_ref[0, rows, :] = (phi + pre * density).astype(BF)
                branch = nt(some, w[s, 1])
                acc[rows, :] += branch
                pre = following

        @pl.when(s == tensor - 1)
        def _():
            cot_copy.wait()
            norm_copy.wait()
            totals = jnp.zeros((8, width), F32)
            for c in range(0, length, chunk):
                rows = slice(c, c + chunk)
                first_out = norm[rows, :] * vec_ref[1:2, :] + vec_ref[2:3, :]
                normed, inverse = layer_norm(first_out + (acc[rows, :] + vec_ref[3:4, :]))
                out[rows, :] = (normed * vec_ref[4:5, :] + vec_ref[5:6, :]).astype(BF)
                upstream = cot[rows, :].astype(F32)
                error = norm_backward(upstream * vec_ref[4:5, :], normed, inverse)
                low[rows, :] = error.astype(BF)
                errt[:, rows] = error.T.astype(BF)
                sums = [jnp.sum(a, axis=0, keepdims=True) for a in (error, upstream * normed, upstream)]
                totals += jnp.concatenate(sums + [jnp.zeros((5, width), F32)], axis=0)
            sums_ref[...] = totals
            for copy in late:
                copy.start()

        @pl.when(s >= tensor)
        def _():
            t = s - tensor
            slot = lax.rem(t, 2)

            @pl.when(t >= 2)
            def _():
                blocks.stores(place_ref, t - 2, stage.at[slot], keep, send, store_sems.at[slot], "wait")

            stage[slot] = nn(errt[...], act[t]).astype(BF).reshape(-1, blocks.rows, part)
            blocks.stores(place_ref, t, stage.at[slot], keep, send, store_sems.at[slot], "start")

        @pl.when(s == 2 * tensor - 1)
        def _():
            for last in range(max(tensor - 2, 0), tensor):
                blocks.stores(place_ref, last, stage.at[last % 2], keep, send, store_sems.at[last % 2], "wait")
            for copy in late:
                copy.wait()

    block_out = (blocks.n // 2, blocks.rows, part)
    wide = (length, width)
    return call(
        body, (2 * tensor,), [place],
        [(a, once(a.shape)) for a in (hidden, vec, up_bias)] + [(cotangent, ANY), (normed_one, ANY), (feed, ANY)],
        [
            ((tensor, length, part), BF, pl.BlockSpec((1, length, part), lambda s, *_: (jnp.minimum(s, tensor - 1), 0, 0))),
            (wide, BF, ANY), (wide, BF, ANY), (block_out, BF, ANY), (block_out, BF, ANY), ((8, width), F32, once((8, width))),
        ],
        [
            pltpu.VMEM((tensor, 2, width, part), BF), pltpu.VMEM((tensor, length, part), BF), pltpu.VMEM(wide, F32), pltpu.VMEM(wide, F32),
            pltpu.VMEM(wide, BF), pltpu.VMEM(wide, BF), pltpu.VMEM((width, length), BF), pltpu.VMEM(wide, BF),
            pltpu.VMEM((2, width // blocks.rows, blocks.rows, part), BF),
            pltpu.SemaphoreType.DMA((2, blocks.n)), pltpu.SemaphoreType.DMA((6,)), pltpu.SemaphoreType.DMA((2, blocks.n // tensor)),
        ],
        (2 * length * width * (width + 3 * tensor * part), 30 * length * width + 4 * length * tensor * part), "feed_forward",
    )


def feed_backward(err_low, slope, hidden_t, normed_one, inverse_one, vec, outputs, feed, place, blocks):
    length, width = err_low.shape
    tensor = blocks.tensor
    feed, tops = feed
    part = feed.shape[-1]
    groups = len(outputs)
    chunk = min(256, length)
    inner = outputs[0][0].shape[1]

    def body(place_ref, e_ref, s_ref, h_ref, i1_ref, vec_ref, *refs):
        o_refs, refs = refs[:groups], refs[groups:]
        n1_hbm, feed_hbm, keep, send, up_sums, err_hbm, errt_hbm, sums_ref, *refs = refs
        dctx_hbm, refs = refs[:groups], refs[groups:]
        w, acc, n1, err, errt, dctx, stage, low, feed_sems, sems, out_sems, store_sems = refs
        t = pl.program_id(0)
        slot = lax.rem(t, 2)
        inputs = [pltpu.make_async_copy(n1_hbm, n1, sems.at[0])]

        @pl.when(t == 0)
        def _():
            acc[...] = jnp.zeros_like(acc)
            for k in range(tensor):
                for copy in feed_loads(feed_hbm, w, feed_sems, blocks, k, tops[::-1]):
                    copy.start()
            for copy in inputs:
                copy.start()

        for copy in feed_loads(feed_hbm, w, feed_sems, blocks, t, tops[::-1]):
            copy.wait()
        span = min(512, length)
        rows_of = [slice(r, r + span) for r in range(0, length, span)]
        product = nn(e_ref[rows_of[0], :], w[t, 0])
        total = jnp.zeros((1, part), F32)
        for n, rows in enumerate(rows_of):
            following = nn(e_ref[rows_of[n + 1], :], w[t, 0]) if n + 1 < len(rows_of) else None
            grad = product * s_ref[0, rows, :].astype(F32)
            total += jnp.sum(grad, axis=0, keepdims=True)
            some = grad.astype(BF)
            low[rows, :] = some
            acc[rows, :] += nt(some, w[t, 1])
            product = following
        up_sums[pl.ds(t, 1), :] = total

        @pl.when(t >= 2)
        def _():
            blocks.stores(place_ref, t - 2, stage.at[slot], keep, send, store_sems.at[slot], "wait")

        stage[slot] = nn(h_ref[...], low[...]).astype(BF).reshape(-1, blocks.rows, part)
        blocks.stores(place_ref, t, stage.at[slot], keep, send, store_sems.at[slot], "start")

        @pl.when(t == tensor - 1)
        def _():
            for copy in inputs:
                copy.wait()
            totals = jnp.zeros((8, width), F32)
            copies = []
            for n, c in enumerate(range(0, length, chunk)):
                rows = slice(c, c + chunk)
                err_in = e_ref[rows, :].astype(F32) + acc[rows, :]
                normed = n1[rows, :].astype(F32)
                error = norm_backward(err_in * vec_ref[1:2, :], normed, i1_ref[rows, :])
                err[rows, :] = error
                turned = error.T.astype(BF)
                errt[:, rows] = turned
                some = pl.ds(c, chunk)
                copies += [
                    pltpu.make_async_copy(err.at[some, :], err_hbm.at[some, :], out_sems.at[n, 0]),
                    pltpu.make_async_copy(errt.at[:, some], errt_hbm.at[:, some], out_sems.at[n, 1]),
                ]
                for g in range(groups):
                    dctx[g, :, rows] = nn(o_refs[g][0], turned).astype(BF)
                    copies.append(pltpu.make_async_copy(dctx.at[g, :, some], dctx_hbm[g].at[:, some], out_sems.at[n, 2 + g]))
                for copy in copies[-2 - groups :]:
                    copy.start()
                sums = [jnp.sum(a, axis=0, keepdims=True) for a in (error, err_in * normed, err_in)]
                totals += jnp.concatenate(sums + [jnp.zeros((5, width), F32)], axis=0)
            sums_ref[...] = totals
            for last in range(max(tensor - 2, 0), tensor):
                blocks.stores(place_ref, last, stage.at[last % 2], keep, send, store_sems.at[last % 2], "wait")
            for copy in copies:
                copy.wait()

    block_out = (blocks.n // 2, blocks.rows, part)
    wide = (length, width)
    return call(
        body, (tensor,), [place],
        [
            (err_low, once(wide)), (slope, pl.BlockSpec((1, length, part), lambda t, *_: (t, 0, 0))), (hidden_t, once((width, length))),
            (inverse_one, once((length, 1))), (vec, once(vec.shape)), *[at_index(o, i) for o, i in outputs],
            (normed_one, ANY), (feed, ANY),
        ],
        [
            (block_out, BF, ANY), (block_out, BF, ANY), ((8, part), F32, once((8, part))), (wide, F32, ANY), ((width, length), BF, ANY),
            ((8, width), F32, once((8, width))), *[((inner, length), BF, ANY) for _ in outputs],
        ],
        [
            pltpu.VMEM((tensor, 2, width, part), BF), pltpu.VMEM(wide, F32), pltpu.VMEM(wide, BF), pltpu.VMEM(wide, F32),
            pltpu.VMEM((width, length), BF), pltpu.VMEM((groups, inner, length), BF), pltpu.VMEM((2, width // blocks.rows, blocks.rows, part), BF), pltpu.VMEM((length, part), BF),
            pltpu.SemaphoreType.DMA((2, blocks.n)), pltpu.SemaphoreType.DMA((2,)), pltpu.SemaphoreType.DMA((length // chunk, 2 + groups)),
            pltpu.SemaphoreType.DMA((2, blocks.n // tensor)),
        ],
        (2 * length * width * (width + 3 * tensor * part), 30 * length * width + 2 * length * tensor * part), "feed_backward",
    )


def finish(first_terms, other_terms, rows, groups, column, cols):
    width = groups * HD
    n = len(first_terms)

    def body(i_ref, *refs):
        (q_ref, k_ref, v_ref, o_ref, qb_ref, vb_ref), terms = refs[2 * n :], refs[: 2 * n]
        sums = [sum(r[0].astype(F32) for r in part) for part in (terms[:n], terms[n:])]
        biases = []
        for c in range(groups):
            block = sums[0] if c == 0 else sums[1][:, (c - 1) * PACK : c * PACK]
            for j, out in enumerate((q_ref, k_ref, v_ref)):
                out[:, c * HD : (c + 1) * HD] = block[:rows, j * HD : (j + 1) * HD]
            o_ref[c * HD : (c + 1) * HD, :] = block[:rows, 2 * HD :].T[HD:]
            biases.append(block[rows : rows + 1])
        biases = jnp.concatenate(biases + [jnp.zeros((8 - groups, PACK), F32)], axis=0)
        for out, start in ((qb_ref, 0), (vb_ref, 2 * HD)):
            out[...] = pltpu.roll(biases, lax.rem(2 * PACK - start - i_ref[0], PACK), 1)[:groups, :cols]

    def block(array):
        return array, pl.BlockSpec((1, *array.shape[1:]), lambda *_: (0, 0, 0))

    shapes = [(rows, width)] * 3 + [(width, rows), (groups, cols), (groups, cols)]
    return call(
        body, (1,), [column.reshape(1)], [block(t) for t in (*first_terms, *other_terms)],
        [(shape, F32, full(shape)) for shape in shapes], [], (1e6, 2 * n * rows * PACK * 6), "finish",
    )


def local(
    tokens, query_weight, key_weight, value_weight, output_weight, query_bias, value_bias,
    output_bias, first_gain, first_shift, up_weight, up_bias, down_weight, down_bias,
    second_gain, second_shift, cotangent,
):
    dp, tensor = lax.axis_size("dp"), lax.axis_size("tensor")
    count = dp * tensor
    rows = query_weight.shape[0]
    width = rows * dp
    groups = query_weight.shape[1] // HD
    heads = groups * tensor
    slot = output_bias.shape[0]
    cols = query_bias.shape[1]
    me = lax.axis_index(AXES)
    place, devs, owners = position_table(me, count), device_table(me, count), owner_table(me, count)
    direct = rows % 16 == 0

    vectors = jnp.stack([output_bias, first_gain, first_shift, down_bias, second_gain, second_shift])
    extra = small_block(vectors, query_bias, value_bias, up_bias)
    output_turned = output_weight.T
    by_group = [
        jnp.concatenate([w[:, c * HD : (c + 1) * HD] for w in (query_weight, key_weight, value_weight, output_turned)], axis=1)
        for c in range(groups)
    ]
    first, second = (Gathering(jnp.concatenate(blocks, axis=axis), count) for blocks, axis in (([by_group[0], extra], 0), (by_group[1:], 1)))
    feed = lax.all_gather(jnp.concatenate([up_weight, down_weight.T], axis=0), AXES, axis=0, tiled=False)
    tokens_t, place, devs, owners, owner_column, dev_column = wave(
        [first], tokens.T, place, devs, owners, owners.reshape(count, 1), devs.reshape(count, 1)
    )
    wave([first, second])
    wave([first])
    direct = rows % 16 == 0
    small_set = (first.pieces, rows) if direct else ([jnp.concatenate([p[:, rows:] for p in first.pieces], axis=0)], 0)
    if direct:
        blocks = Blocks(count, rows, tensor)
        block_place, block_devs = place, devs
    else:
        blocks = Blocks(tensor, width, tensor)
        block_place = block_devs = jnp.arange(tensor, dtype=jnp.int32)

    def by_matrix(ordered):
        return [ordered.reshape(dp, tensor, rows, -1).transpose(1, 0, 2, 3).reshape(tensor, width, -1)]

    def ready(gathering):
        if direct:
            return gathering.pieces
        return by_matrix(jnp.take(jnp.concatenate(gathering.pieces, axis=0)[:, :rows], gathered_place(me, count), axis=0))

    def scattering(keep, send, more=None):
        if not direct:
            stacked = jnp.concatenate([keep, send], axis=0)
            parts = [stacked[:, :width].reshape(tensor, dp, rows, -1).transpose(1, 0, 2, 3).reshape(count, rows, -1)]
            if stacked.shape[1] > width:
                parts.append(jnp.tile(stacked[:, width:], (dp, 1, 1)))
            stacked = jnp.take(jnp.concatenate(parts, axis=1), owners, axis=0)
            if more is not None:
                stacked = jnp.concatenate([stacked, more], axis=1)
            keep, send = stacked[: count // 2], stacked[count // 2 :]
        return Scattering(keep, send, count)

    tokens_now = wave([second], tokens)
    vec, bias_pack, up_rows = unpack_small(*small_set, dev_column, slot, cols, width, tensor)
    first_set = ready(first)
    one = attention_forward(tokens_now, first_set, bias_pack, 0, block_devs, blocks)
    tokens_now = wave([second], tokens, one[4])[0]
    second_set = ready(second)
    others = attention_forward(tokens_now, second_set, bias_pack, 1, block_devs, blocks)
    weights = [(first_set, 0)] + [(second_set, c * PACK) for c in range(groups - 1)]
    forward = [(one, 0)] + [(others, c) for c in range(groups - 1)]
    outputs = [(f[5], i) for f, i in forward]
    normed_wide, normed_one, inverse_one, hidden, hidden_t = output_and_norm(tokens, [(f[2], i) for f, i in forward], outputs, vec)
    feed, hidden = lax.optimization_barrier((feed, hidden))
    if not direct:
        feed = jnp.concatenate([by_matrix(feed[:, :rows])[0], by_matrix(feed[:, rows:])[0]], axis=1)
    feed = (feed, (0, feed.shape[1] // 2))
    slope, layer_out, err_two_low, down_keep, down_send, sums_two = feed_forward(
        hidden, normed_wide, cotangent, vec, up_rows, feed, block_place, blocks
    )
    grad_down = scattering(down_keep, down_send)
    err_two_low = wave([grad_down], err_two_low)
    up_keep, up_send, up_sums, err_one, err_one_t, sums_one, *context_grads = feed_backward(
        err_two_low, slope, hidden_t, normed_one, inverse_one, vec, outputs, feed, block_place, blocks
    )
    grad_up = scattering(up_keep, up_send)
    small = (sums_one, sums_two, up_sums, owner_column)
    if not direct:
        small = pack_small_grads(*small, slot, cols, tensor)
    column = lax.axis_index("dp") * cols
    backward = [None] * groups
    token_sum = err_one
    last, packed, moving = (err_one_t,), None, [grad_down, grad_up]
    for c in reversed(range(groups)):
        carries = c == groups - 1
        options = {}
        if c and direct:
            options = dict(into=packed, lane=(c - 1) * PACK, high=rows + 2 * EXTRA, wide=(groups - 1) * PACK)
        if c:
            context_grad = wave(moving, context_grads[c], since=last)
        backward[c] = attention_backward(
            tokens_t, err_one_t, *forward[c], context_grad, token_sum, weights[c], block_place, block_devs, blocks,
            (small, slot, cols) if direct and carries else None, **options,
        )
        token_sum = backward[c][2]
        last = (token_sum,)
        if c and direct:
            packed = backward[c][:2]
        if c == 1:
            if direct:
                others = scattering(*packed)
            else:
                packed = [jnp.concatenate([backward[g][i] for g in range(1, groups)], axis=2) for i in range(2)]
                others = scattering(*packed, jnp.pad(small, ((0, 0), (0, 0), ((groups - 2) * PACK, 0))))
            grad_down.terms, grad_up.terms = wave([others], grad_down.terms, grad_up.terms)
            ahead = [*grad_down.outgoing(), *grad_up.outgoing()]
            wave([grad_down, grad_up])
            others.looked_at(*ahead)
            context_grad = wave([others], context_grads[0])
    zero = scattering(*backward[0][:2])
    while grad_down.phases:
        wave([grad_down])
    grad_up.terms, grad_down.terms, others.terms = wave([zero], grad_up.terms, grad_down.terms, others.terms)
    wave([zero])
    wave([others, grad_up])
    while grad_up.phases:
        wave([grad_up])
    wave([zero])
    grad_up.terms, zero.terms = wave([others], grad_up.terms, zero.terms)
    grad_up, grad_down = grad_up.result(), grad_down.result()
    while zero.phases or others.phases:
        grad_up, grad_down = wave([zero, others], grad_up, grad_down)
    tail = sum(t[0, rows + EXTRA :, (groups - 2) * PACK :].astype(F32) for t in others.terms)
    if direct:
        out_query, out_key, out_value, out_output, *bias_out = finish(zero.terms, others.terms, rows, groups, column, cols)
    else:
        results = [zero.result()] + jnp.split(others.result()[: rows + EXTRA], groups - 1, axis=1)
        bias_rows = jnp.stack([r[rows] for r in results])
        bias_out = [lax.dynamic_slice(bias_rows, (0, start + column), (groups, cols)) for start in (0, 2 * HD)]
        out = jnp.stack([r[:rows] for r in results], axis=1).reshape(rows, groups, 4, HD)
        out_query, out_key, out_value, out_output = (out[:, :, i].reshape(rows, groups * HD) for i in range(4))
        out_output = out_output.T
    vecs = [tail[v // 2, (v % 2) * LANES : (v % 2) * LANES + slot] for v in range(6)]
    return (
        layer_out,
        token_sum,
        out_query,
        out_key,
        out_value,
        out_output,
        bias_out[0],
        bias_out[1],
        vecs[0],
        vecs[1],
        vecs[2],
        grad_up,
        tail[: up_bias.shape[0], 64 : 64 + cols],
        grad_down.T,
        vecs[3],
        vecs[4],
        vecs[5],
    )


def solution(mesh):
    both, cross, turned, vector = P(AXES, None), P("dp", "tensor"), P("tensor", "dp"), P(AXES)
    return jax.shard_map(
        local,
        mesh=mesh,
        in_specs=(
            both, cross, cross, cross, turned, turned, turned, vector, vector, vector,
            cross, turned, turned, vector, vector, vector, both,
        ),
        out_specs=(
            both, both, cross, cross, cross, turned, turned, turned, vector, vector, vector,
            cross, turned, turned, vector, vector, vector,
        ),
        check_vma=False,
    )
```
